128 devices in a mesh: ctx: 64 (over z_lo, x, y, core), fsdp: 2 (over z_hi).
Axes of the slice: x: 4, y: 4, z: 4 (z_hi: 2, z_lo: 2; z = z_hi * 2 + z_lo), core: 2. Of those that a mesh axis runs over, the one named last changes fastest.
Arguments:
- block_in: bfloat16 [2, 8192, 768], P('fsdp', 'ctx'), may hold values from -70 to 70
- out_grad: bfloat16 [2, 8192, 768], P('fsdp', 'ctx'), may hold values from -6 to 6
- ln1_gain: bfloat16 [768], P('fsdp'), may hold values from 0.5 to 1.5
- ln1_bias: bfloat16 [768], P('fsdp'), may hold values from -3 to 3
- w_qkv: bfloat16 [768, 2304], P('fsdp'), may hold values from -2 to 2
- q_bias: bfloat16 [768], P('fsdp'), may hold values from -3 to 3
- v_bias: bfloat16 [768], P('fsdp'), may hold values from -3 to 3
- w_proj: bfloat16 [768, 768], P('fsdp'), may hold values from -2 to 2
- b_proj: bfloat16 [768], P('fsdp'), may hold values from -3 to 3
- ln2_gain: bfloat16 [768], P('fsdp'), may hold values from 0.5 to 1.5
- ln2_bias: bfloat16 [768], P('fsdp'), may hold values from -3 to 3
- w_fc: bfloat16 [768, 3072], P('fsdp'), may hold values from -0.21875 to 0.21875
- b_fc: bfloat16 [3072], P('fsdp'), may hold values from -3 to 3
- w_out: bfloat16 [3072, 768], P('fsdp'), may hold values from -0.109375 to 0.109375
- b_out: bfloat16 [768], P('fsdp'), may hold values from -3 to 3
Outputs:
- block_out: bfloat16 [2, 8192, 768], P('fsdp', 'ctx')
- input_grad: float32 [2, 8192, 768], P('fsdp', 'ctx')
- grad_ln1_gain: float32 [768], P('fsdp')
- grad_ln1_bias: float32 [768], P('fsdp')
- grad_w_qkv: float32 [768, 2304], P('fsdp')
- grad_q_bias: float32 [768], P('fsdp')
- grad_v_bias: float32 [768], P('fsdp')
- grad_w_proj: float32 [768, 768], P('fsdp')
- grad_b_proj: float32 [768], P('fsdp')
- grad_ln2_gain: float32 [768], P('fsdp')
- grad_ln2_bias: float32 [768], P('fsdp')
- grad_w_fc: float32 [768, 3072], P('fsdp')
- grad_b_fc: float32 [3072], P('fsdp')
- grad_w_out: float32 [3072, 768], P('fsdp')
- grad_b_out: float32 [768], P('fsdp')
The draws below stay inside these ranges and needn't reach their ends.
All inputs are finite; a program needn't handle non-finite values.
Results may differ from the reference program's by a relative error of at most 0.025.
The reference program's roundings to bfloat16 on the way count: a program that leaves them out, or rounds other values in their place, can miss the bound.
Values may be sent and summed in bfloat16 or wider, within the bound.
No kernel may reach another device: no remote copies, remote signals or barrier semaphores. Data moves between devices by JAX's collectives and lax.ppermute only.
A program may use at most 256 MiB of HBM per device.

```python
import math
import jax
import jax.numpy as jnp
from jax import lax

D = 768
HEADS = 12
HD = 64
FF = 3072
SEQ = 8192
SEQS = 2


def draw_block_in(key, part):
    normal_key = jax.random.fold_in(jax.random.fold_in(key, 11), 0)
    drawn = jnp.clip(jax.random.normal(normal_key, (SEQS, SEQ, D), jnp.float32), -6.0, 6.0)
    return drawn.astype(jnp.bfloat16)


def draw_w_qkv(key, part):
    first_key = jax.random.fold_in(jax.random.fold_in(key, 23), 0)
    drawn = jnp.clip(jax.random.normal(first_key, (D, 3 * D), jnp.float32), -6.0, 6.0) * D ** (-0.5)
    return drawn.astype(jnp.bfloat16)


def level_of(stream_key, dims, cuts, smallest, largest):
    level = 1.0
    for dim, blocks in cuts:
        draws = jax.random.uniform(jax.random.fold_in(jax.random.fold_in(stream_key, 6), dim), (blocks,), jnp.float32, smallest / len(cuts), largest / len(cuts))
        level = level * jnp.repeat(jnp.exp(draws), dims[dim] // blocks).reshape((-1,) + (1,) * (len(dims) - 1 - dim))
    return level


def bell_draw(stream_key, extent, deviation, limit, shards=(), kind=jnp.bfloat16):
    level = level_of(stream_key, extent, shards, -0.22, 0.18) if shards else 1.0
    entries = jax.random.normal(stream_key, extent, jnp.float32) * deviation * level
    return jnp.minimum(jnp.maximum(entries, -limit), limit).astype(kind)


def setup_inputs(seed: int = 0) -> dict:
    keys = jax.random.split(jax.random.key(seed), 16)
    return {
        "block_in": draw_block_in(jax.random.fold_in(keys[15], 71), 0),
        "out_grad": bell_draw(keys[1], (SEQS, SEQ, D), 1.0, 6.0, ((0, 2), (1, 64))),
        "ln1_gain": jnp.clip(1.0 + 0.1 * jax.random.normal(keys[2], (D,), jnp.float32), 0.5, 1.5).astype(jnp.bfloat16),
        "ln1_bias": bell_draw(keys[3], (D,), 0.5, 3.0, ((0, 2),)),
        "w_qkv": draw_w_qkv(jax.random.fold_in(keys[15], 71), 0),
        "q_bias": bell_draw(keys[5], (D,), 0.5, 3.0, ((0, 2),)),
        "v_bias": bell_draw(keys[6], (D,), 0.5, 3.0, ((0, 2),)),
        "w_proj": bell_draw(keys[7], (D, D), 8 ** -0.5, 2.0, ((0, 2),)),
        "b_proj": bell_draw(keys[8], (D,), 0.5, 3.0, ((0, 2),)),
        "ln2_gain": jnp.clip(1.0 + 0.1 * jax.random.normal(keys[9], (D,), jnp.float32), 0.5, 1.5).astype(jnp.bfloat16),
        "ln2_bias": bell_draw(keys[10], (D,), 0.5, 3.0, ((0, 2),)),
        "w_fc": bell_draw(keys[11], (D, FF), D ** -0.5, 0.21875, ((0, 2),)),
        "b_fc": bell_draw(keys[12], (FF,), 0.5, 3.0, ((0, 2),)),
        "w_out": bell_draw(keys[13], (FF, D), FF ** -0.5, 0.109375, ((0, 2),)),
        "b_out": bell_draw(keys[14], (D,), 0.5, 3.0, ((0, 2),)),
    }


norm_epsilon = 1e-05
gelu_factor = 0.7978845608028654
gelu_cubic = 0.044715
masked_score = -1e+30

def layer_norm(values, gain, offset):
    center = lax.optimization_barrier(jnp.mean(values, axis=-1, keepdims=True))
    centered = values - center
    spread = lax.optimization_barrier(jnp.mean(centered * centered, axis=-1, keepdims=True))
    return centered * lax.rsqrt(spread + norm_epsilon) * gain + offset

def gelu_tanh(values):
    return 0.5 * values * (1.0 + jnp.tanh(gelu_factor * (values + gelu_cubic * values * values * values)))

def attend_forward(queries, keys_all, values_all, score_scale):
    row_total = queries.shape[0]
    span_rows = math.gcd(row_total, 512)
    key_pos = jnp.arange(row_total, dtype=jnp.int32)
    keys_wide = keys_all.astype(jnp.float32)
    values_wide = values_all.astype(jnp.float32)

    def one_span(span_index):
        first_row = span_index * span_rows
        query_span = lax.dynamic_slice_in_dim(queries, first_row, span_rows, 0).astype(jnp.float32)
        query_pos = first_row + jnp.arange(span_rows, dtype=jnp.int32)
        allowed = key_pos[None, :] <= query_pos[:, None]
        scores = jnp.einsum('thd,shd->hts', query_span, keys_wide) * score_scale
        scores = jnp.where(allowed[None], scores, masked_score)
        maximum = lax.optimization_barrier(jnp.max(scores, axis=2))
        weights = jnp.where(allowed[None], jnp.exp(scores - maximum[:, :, None]), 0.0)
        denominator = lax.optimization_barrier(jnp.sum(weights, axis=2))
        rounded = lax.optimization_barrier(weights.astype(jnp.bfloat16)).astype(jnp.float32)
        attended = jnp.einsum('hts,shd->thd', rounded, values_wide) / jnp.transpose(denominator)[:, :, None]
        return (attended, maximum + jnp.log(denominator))
    attended, log_sums = lax.map(one_span, jnp.arange(row_total // span_rows, dtype=jnp.int32))
    attended = attended.reshape(row_total, queries.shape[1], queries.shape[2])
    log_sums = jnp.transpose(log_sums, (1, 0, 2)).reshape(queries.shape[1], row_total)
    return (attended, log_sums)

def attend_backward(queries, keys_all, values_all, grad_heads, log_sums, delta_sums, score_scale):
    row_total = queries.shape[0]
    span_rows = math.gcd(row_total, 512)
    key_pos = jnp.arange(row_total, dtype=jnp.int32)
    keys_wide = keys_all.astype(jnp.float32)
    values_wide = values_all.astype(jnp.float32)

    def one_span(running, span_index):
        grad_keys, grad_values = running
        first_row = span_index * span_rows
        query_span = lax.dynamic_slice_in_dim(queries, first_row, span_rows, 0).astype(jnp.float32)
        grad_span = lax.dynamic_slice_in_dim(grad_heads, first_row, span_rows, 0).astype(jnp.float32)
        lse_span = lax.dynamic_slice_in_dim(log_sums, first_row, span_rows, 1)
        delta_span = lax.dynamic_slice_in_dim(delta_sums, first_row, span_rows, 1)
        query_pos = first_row + jnp.arange(span_rows, dtype=jnp.int32)
        allowed = key_pos[None, :] <= query_pos[:, None]
        scores = jnp.einsum('thd,shd->hts', query_span, keys_wide) * score_scale
        scores = jnp.where(allowed[None], scores, masked_score)
        probabilities = jnp.where(allowed[None], jnp.exp(scores - lse_span[:, :, None]), 0.0)
        grad_probs = jnp.einsum('thd,shd->hts', grad_span, values_wide)
        grad_scores = probabilities * (grad_probs - delta_span[:, :, None]) * score_scale
        grad_scores = lax.optimization_barrier(grad_scores.astype(jnp.bfloat16)).astype(jnp.float32)
        rounded = lax.optimization_barrier(probabilities.astype(jnp.bfloat16)).astype(jnp.float32)
        grad_query = jnp.einsum('hts,shd->thd', grad_scores, keys_wide)
        grad_keys = grad_keys + jnp.einsum('hts,thd->shd', grad_scores, query_span)
        grad_values = grad_values + jnp.einsum('hts,thd->shd', rounded, grad_span)
        return ((grad_keys, grad_values), grad_query)
    zeros_init = jnp.zeros(queries.shape, jnp.float32)
    (grad_keys, grad_values), grad_query = lax.scan(one_span, (zeros_init, zeros_init), jnp.arange(row_total // span_rows, dtype=jnp.int32))
    return (grad_query.reshape(queries.shape), grad_keys, grad_values)

def one_sequence(inputs, cotangent, params):
    gain_one, shift_one, qkv_weight, query_bias, value_bias, proj_weight, proj_bias, gain_two, shift_two, fc_weight, fc_bias, out_weight, out_bias = params
    width = D
    row_total = inputs.shape[0]
    score_scale = 1.0 / math.sqrt(HD)

    def split_heads(values):
        return values.reshape(row_total, HEADS, HD)
    inputs_wide = inputs.astype(jnp.float32)
    normed_one = layer_norm(inputs_wide, gain_one, shift_one).astype(jnp.bfloat16)
    projected = jnp.dot(normed_one, qkv_weight, preferred_element_type=jnp.float32)
    queries = (projected[:, :width] + query_bias).astype(jnp.bfloat16)
    keys_all = projected[:, width:2 * width].astype(jnp.bfloat16)
    values_all = (projected[:, 2 * width:] + value_bias).astype(jnp.bfloat16)
    attended, log_sums = attend_forward(split_heads(queries), split_heads(keys_all), split_heads(values_all), score_scale)
    attn_rows = lax.optimization_barrier(attended.reshape(row_total, width).astype(jnp.bfloat16))
    residual_one = jnp.dot(attn_rows, proj_weight, preferred_element_type=jnp.float32) + proj_bias + inputs_wide
    normed_two = layer_norm(residual_one, gain_two, shift_two).astype(jnp.bfloat16)
    hidden_pre = jnp.dot(normed_two, fc_weight, preferred_element_type=jnp.float32) + fc_bias
    activated = gelu_tanh(hidden_pre).astype(jnp.bfloat16)
    output = (jnp.dot(activated, out_weight, preferred_element_type=jnp.float32) + out_bias + residual_one).astype(jnp.bfloat16)
    grad_wide = cotangent.astype(jnp.float32)
    grad_out_weight = jnp.dot(activated.T, cotangent, preferred_element_type=jnp.float32)
    grad_out_bias = lax.optimization_barrier(jnp.sum(grad_wide, axis=0))
    grad_activated = jnp.dot(cotangent, out_weight.T, preferred_element_type=jnp.float32)
    unused, gelu_back = jax.vjp(gelu_tanh, hidden_pre)
    grad_hidden = gelu_back(grad_activated)[0]
    grad_hidden_low = grad_hidden.astype(jnp.bfloat16)
    grad_fc_weight = jnp.dot(normed_two.T, grad_hidden_low, preferred_element_type=jnp.float32)
    grad_fc_bias = lax.optimization_barrier(jnp.sum(grad_hidden, axis=0))
    grad_normed_two = jnp.dot(grad_hidden_low, fc_weight.T, preferred_element_type=jnp.float32)
    unused, norm_back_two = jax.vjp(layer_norm, residual_one, gain_two, shift_two)
    grad_residual, grad_gain_two, grad_shift_two = norm_back_two(grad_normed_two)
    grad_residual = grad_residual + grad_wide
    grad_residual_low = grad_residual.astype(jnp.bfloat16)
    grad_proj_weight = jnp.dot(attn_rows.T, grad_residual_low, preferred_element_type=jnp.float32)
    grad_proj_bias = lax.optimization_barrier(jnp.sum(grad_residual, axis=0))
    grad_attn = lax.optimization_barrier(jnp.dot(grad_residual_low, proj_weight.T, preferred_element_type=jnp.float32).astype(jnp.bfloat16))
    delta_sums = jnp.transpose(lax.optimization_barrier(jnp.sum(split_heads(grad_attn).astype(jnp.float32) * split_heads(attn_rows).astype(jnp.float32), axis=2)))
    grad_query, grad_keys, grad_values = attend_backward(split_heads(queries), split_heads(keys_all), split_heads(values_all), split_heads(grad_attn), log_sums, delta_sums, score_scale)
    grad_query = grad_query.reshape(row_total, width)
    grad_keys = grad_keys.reshape(row_total, width)
    grad_values = grad_values.reshape(row_total, width)
    grad_query_bias = lax.optimization_barrier(jnp.sum(grad_query, axis=0))
    grad_value_bias = lax.optimization_barrier(jnp.sum(grad_values, axis=0))
    grad_projected = jnp.concatenate([grad_query, grad_keys, grad_values], axis=1).astype(jnp.bfloat16)
    grad_qkv_weight = jnp.dot(normed_one.T, grad_projected, preferred_element_type=jnp.float32)
    grad_normed_one = jnp.dot(grad_projected, qkv_weight.T, preferred_element_type=jnp.float32)
    unused, norm_back_one = jax.vjp(layer_norm, inputs_wide, gain_one, shift_one)
    grad_inputs, grad_gain_one, grad_shift_one = norm_back_one(grad_normed_one)
    grad_inputs = grad_inputs + grad_residual
    return (output, grad_inputs, (grad_gain_one, grad_shift_one, grad_qkv_weight, grad_query_bias, grad_value_bias, grad_proj_weight, grad_proj_bias, grad_gain_two, grad_shift_two, grad_fc_weight, grad_fc_bias, grad_out_weight, grad_out_bias))

def reference(block_in, out_grad, ln1_gain, ln1_bias, w_qkv, q_bias, v_bias, w_proj, b_proj, ln2_gain, ln2_bias, w_fc, b_fc, w_out, b_out):
    params = (ln1_gain.astype(jnp.float32), ln1_bias.astype(jnp.float32), w_qkv, q_bias.astype(jnp.float32), v_bias.astype(jnp.float32), w_proj, b_proj.astype(jnp.float32), ln2_gain.astype(jnp.float32), ln2_bias.astype(jnp.float32), w_fc, b_fc.astype(jnp.float32), w_out, b_out.astype(jnp.float32))
    outputs = []
    input_grads = []
    totals = None
    for sequence_index in range(block_in.shape[0]):
        output, grad_inputs, grads = one_sequence(block_in[sequence_index], out_grad[sequence_index], params)
        outputs.append(output)
        input_grads.append(grad_inputs)
        if totals is None:
            totals = grads
        else:
            totals = jax.tree.map(lambda first, second: first + second, totals, grads)
    return (jnp.stack(outputs), jnp.stack(input_grads), totals[0], totals[1], totals[2], totals[3], totals[4], totals[5], totals[6], totals[7], totals[8], totals[9], totals[10], totals[11], totals[12])
```

```python
import jax
import jax.numpy as jnp
from jax import lax
from jax.experimental import pallas as pl
from jax.experimental.pallas import tpu as pltpu
from jax.sharding import Mesh, PartitionSpec as P

TP = ("zl", "xh")
SEQ_AXES = ("xl", "yh", "yl", "core")
CTX = TP + SEQ_AXES
EPS = 1e-05
GELU_F = 0.7978845608028654
GELU_C = 0.044715
NEG = -1e30
F32 = jnp.float32
BF16 = jnp.bfloat16
NT = (((1,), (1,)), ((), ()))
VMEM_LIMIT = 56 * 1024 * 1024


def lane_half(shape):
    return lax.broadcasted_iota(jnp.int32, shape, len(shape) - 1) >= 64


def slot_only(values, slot):
    lane = lax.broadcasted_iota(jnp.int32, values.shape, 1)
    keep = jnp.logical_and(lane >= 64 * slot, lane < 64 * slot + 64)
    return jnp.where(keep, values, jnp.zeros_like(values))


def wide(values):
    return jnp.concatenate([values] * 4, axis=1)


def pieces(values):
    high = values.astype(BF16)
    rest = values - high.astype(F32)
    middle = rest.astype(BF16)
    low = (rest - middle.astype(F32)).astype(BF16)
    return (high, middle, low)


def chunk_rows(ref, rank, chunk):
    rows = ref[pl.ds(4 * lax.rem(chunk, 4), 4), rank ^ (chunk // 4)]
    return rows.reshape(512, rows.shape[-1])


def causal(scores, first_query, first_key, keys_in_rows):
    rows = lax.broadcasted_iota(jnp.int32, (128, 512), 0)
    cols = lax.broadcasted_iota(jnp.int32, (128, 512), 1)
    if keys_in_rows:
        allowed = first_key + rows <= first_query + cols
    else:
        allowed = first_key + cols <= first_query + rows
    return jnp.concatenate(
        [jnp.where(allowed, scores[128 * h : 128 * h + 128], NEG) for h in range(3)], axis=0
    )


def value_halves(product):
    return jnp.concatenate([product[:256, 128:], product[256:, :128]], axis=0)


def row_halves(product):
    return jnp.concatenate([product[:256, :128], product[256:, 128:]], axis=0)


def forward_kernel(pos_ref, q_ref, kv_ref, attn_ref, qaug_ref, lse_ref, m_ref, l_ref, acc_ref):
    seq = pos_ref[0]
    rank = pos_ref[1]

    def tile(k, carry):
        slot = rank ^ k
        block = k * 16 + seq
        q_rows = q_ref[slot]
        queries = jnp.concatenate([slot_only(q_rows, h) for h in range(3)], axis=0)
        m_ref[...] = jnp.full(m_ref.shape, NEG, F32)
        l_ref[...] = jnp.zeros(l_ref.shape, F32)
        acc_ref[...] = jnp.zeros(acc_ref.shape, F32)

        def step(chunk, masked):
            kv = chunk_rows(kv_ref, rank, chunk)
            scores = lax.dot_general(queries, kv[:, :256], NT, preferred_element_type=F32)
            if masked:
                scores = causal(scores, block * 128, chunk * 512, False)
            before = m_ref[...]
            after = jnp.maximum(before, jnp.max(scores, axis=1, keepdims=True))
            weights = jnp.exp(scores - wide(after))
            factor = jnp.exp(before - after)
            m_ref[...] = after
            partial = (weights[:, :128] + weights[:, 128:256]) + (
                weights[:, 256:384] + weights[:, 384:]
            )
            l_ref[...] = l_ref[...] * factor + partial
            acc_ref[...] = acc_ref[...] * factor + value_halves(
                jnp.dot(weights.astype(BF16), kv[:, 128:], preferred_element_type=F32)
            )

        last = block // 4

        def full(chunk, inner):
            step(chunk, False)
            return inner

        lax.fori_loop(0, last, full, 0)
        step(last, True)
        lane = lax.broadcasted_iota(jnp.int32, (128, 128), 1)
        extra = jnp.zeros((128, 128), BF16)
        total = jnp.sum(l_ref[...], axis=1, keepdims=True)
        log_sum = m_ref[...] + jnp.log(total)
        lse_ref[slot] = log_sum
        outs = acc_ref[...] / total
        for p, part in enumerate(pieces(-log_sum)):
            for h in range(3):
                extra = jnp.where(
                    lane == 64 + 3 * h + p, part[128 * h : 128 * h + 128], extra
                )
        attn_ref[slot, :, :128] = jnp.where(lane < 64, outs[:128], outs[128:256]).astype(BF16)
        attn_ref[slot, :, 128:] = jnp.where(lane < 64, 0.0, outs[256:]).astype(BF16)
        qaug_ref[slot, :, :128] = q_rows[:, :128]
        qaug_ref[slot, :, 128:] = jnp.where(lane < 64, q_rows[:, 128:], extra)
        return carry

    lax.fori_loop(0, 4, tile, 0)


def vmem_spec():
    return pl.BlockSpec(memory_space=pltpu.VMEM)


def forward_attention(pos, q, kv):
    return pl.pallas_call(
        forward_kernel,
        out_shape=(
            jax.ShapeDtypeStruct((4, 128, 256), BF16),
            jax.ShapeDtypeStruct((4, 128, 256), BF16),
            jax.ShapeDtypeStruct((4, 384, 128), F32),
        ),
        in_specs=[pl.BlockSpec(memory_space=pltpu.SMEM), vmem_spec(), vmem_spec()],
        out_specs=(vmem_spec(), vmem_spec(), vmem_spec()),
        scratch_shapes=[pltpu.VMEM((384, 128), F32)] * 3,
        compiler_params=pltpu.CompilerParams(vmem_limit_bytes=VMEM_LIMIT),
        cost_estimate=pl.CostEstimate(
            flops=3 * 512 * 4096 * 512, transcendentals=3 * 512 * 4096, bytes_accessed=8 * 2**20
        ),
        name="attention_forward",
    )(pos, q, kv)


def grad_rows_kernel(dr_ref, w_ref, attn_ref, do_ref, delta_ref):
    lane = lax.broadcasted_iota(jnp.int32, (512, 128), 1)
    grads = lax.dot_general(dr_ref[...], w_ref[...], NT, preferred_element_type=F32).astype(BF16)
    attn = attn_ref[...].reshape(512, 256).astype(F32)
    product = grads.astype(F32) * attn
    extra = jnp.zeros((512, 128), BF16)
    for h, run in enumerate((0, 1, 3)):
        delta = jnp.sum(slot_only(product, run), axis=1, keepdims=True)
        delta = jnp.broadcast_to(delta, (512, 128))
        for k in range(4):
            delta_ref[k, 128 * h : 128 * h + 128] = delta[128 * k : 128 * k + 128]
        for p, piece in enumerate(pieces(-delta)):
            extra = jnp.where(lane == 3 * h + p, piece, extra)
    do_ref[:, :, :128] = grads[:, :128].reshape(4, 128, 128)
    do_ref[:, :, 128:] = jnp.where(lane < 64, extra, grads[:, 128:]).reshape(4, 128, 128)


def grad_rows(dr_low, w_rows, attn):
    return pl.pallas_call(
        grad_rows_kernel,
        out_shape=(
            jax.ShapeDtypeStruct((4, 128, 256), BF16),
            jax.ShapeDtypeStruct((4, 384, 128), F32),
        ),
        in_specs=[vmem_spec(), vmem_spec(), vmem_spec()],
        out_specs=(vmem_spec(), vmem_spec()),
        compiler_params=pltpu.CompilerParams(vmem_limit_bytes=VMEM_LIMIT),
        name="attention_grad_rows",
    )(dr_low, w_rows, attn)


def query_grad_kernel(pos_ref, q_ref, do_ref, lse_ref, delta_ref, kv_ref, dq_ref, acc_ref):
    seq = pos_ref[0]
    rank = pos_ref[1]

    def tile(k, carry):
        slot = rank ^ k
        block = k * 16 + seq
        q_rows = q_ref[slot]
        do_rows = do_ref[slot]
        queries = jnp.concatenate([slot_only(q_rows, h) for h in range(3)], axis=0)
        turned = jnp.concatenate([do_rows[:, 128:], do_rows[:, :128]], axis=1)
        grads = jnp.concatenate([slot_only(turned, run) for run in (2, 3, 1)], axis=0)
        acc_ref[...] = jnp.zeros(acc_ref.shape, F32)

        def step(chunk, masked):
            kv = chunk_rows(kv_ref, rank, chunk)
            scores = lax.dot_general(queries, kv[:, :256], NT, preferred_element_type=F32)
            scores = scores - wide(lse_ref[slot])
            if masked:
                scores = causal(scores, block * 128, chunk * 512, False)
            weights = jnp.exp(scores)
            grad_weights = lax.dot_general(grads, kv[:, 128:], NT, preferred_element_type=F32)
            grad_scores = (weights * (grad_weights - wide(delta_ref[slot]))).astype(BF16)
            acc_ref[...] += row_halves(
                jnp.dot(grad_scores, kv[:, :256], preferred_element_type=F32)
            )

        last = block // 4

        def full(chunk, inner):
            step(chunk, False)
            return inner

        lax.fori_loop(0, last, full, 0)
        step(last, True)
        lane = lax.broadcasted_iota(jnp.int32, (128, 128), 1)
        acc = acc_ref[...] * 0.125
        dq_ref[slot, :, :128] = jnp.where(lane < 64, acc[:128], acc[128:256])
        dq_ref[slot, :, 128:] = jnp.where(lane < 64, acc[256:], 0.0)
        return carry

    lax.fori_loop(0, 4, tile, 0)


def query_grad(pos, q, do, lse, delta, kv):
    return pl.pallas_call(
        query_grad_kernel,
        out_shape=jax.ShapeDtypeStruct((4, 128, 256), F32),
        in_specs=[pl.BlockSpec(memory_space=pltpu.SMEM)] + [vmem_spec()] * 5,
        out_specs=vmem_spec(),
        scratch_shapes=[pltpu.VMEM((384, 128), F32)],
        compiler_params=pltpu.CompilerParams(vmem_limit_bytes=VMEM_LIMIT),
        cost_estimate=pl.CostEstimate(
            flops=3 * 512 * 4096 * 768, transcendentals=3 * 512 * 4096, bytes_accessed=8 * 2**20
        ),
        name="attention_query_grad",
    )(pos, q, do, lse, delta, kv)


def key_grad_kernel(pos_ref, kv_ref, qg_ref, dog_ref, dkv_ref, dk_ref, dv_ref):
    seq = pos_ref[0]
    rank = pos_ref[1]

    def tile(k, carry):
        slot = rank ^ k
        block = k * 16 + seq
        rows = kv_ref[slot]
        lane = lax.broadcasted_iota(jnp.int32, (128, 256), 1)
        key_rows = rows[:, :256]
        value_rows = jnp.concatenate([rows[:, 256:], rows[:, 128:256]], axis=1)
        keys = []
        values = []
        for h, run in enumerate((0, 1, 3)):
            key_ones = jnp.logical_and(lane >= 192 + 3 * h, lane < 195 + 3 * h)
            value_ones = jnp.logical_and(lane >= 128 + 3 * h, lane < 131 + 3 * h)
            keys.append(jnp.where(key_ones, 1.0, slot_only(key_rows, h)).astype(BF16))
            values.append(jnp.where(value_ones, 1.0, slot_only(value_rows, run)).astype(BF16))
        keys = jnp.concatenate(keys, axis=0)
        values = jnp.concatenate(values, axis=0)
        dk_ref[...] = jnp.zeros(dk_ref.shape, F32)
        dv_ref[...] = jnp.zeros(dv_ref.shape, F32)

        def step(chunk, masked):
            q_rows = chunk_rows(qg_ref, rank, chunk)
            do_rows = chunk_rows(dog_ref, rank, chunk)
            scores = lax.dot_general(keys, q_rows, NT, preferred_element_type=F32)
            if masked:
                scores = causal(scores, chunk * 512, block * 128, True)
            weights = jnp.exp(scores)
            grad_weights = lax.dot_general(values, do_rows, NT, preferred_element_type=F32)
            grad_scores = (weights * grad_weights).astype(BF16)
            dv_ref[...] += row_halves(
                jnp.dot(weights.astype(BF16), do_rows, preferred_element_type=F32)
            )
            dk_ref[...] += row_halves(jnp.dot(grad_scores, q_rows, preferred_element_type=F32))

        first = block // 4

        def full(chunk, inner):
            step(chunk, False)
            return inner

        step(first, True)
        lax.fori_loop(first + 1, 16, full, 0)
        half = lax.broadcasted_iota(jnp.int32, (128, 128), 1) < 64
        dkv_ref[slot, :, :128] = jnp.where(half, dk_ref[:128], dk_ref[128:256])
        dkv_ref[slot, :, 128:256] = jnp.where(half, dk_ref[256:], dv_ref[256:])
        dkv_ref[slot, :, 256:] = jnp.where(half, dv_ref[:128], dv_ref[128:256])
        return carry

    lax.fori_loop(0, 4, tile, 0)


def key_grad(pos, kv_own, q_all, do_all):
    return pl.pallas_call(
        key_grad_kernel,
        out_shape=jax.ShapeDtypeStruct((4, 128, 384), F32),
        in_specs=[pl.BlockSpec(memory_space=pltpu.SMEM)] + [vmem_spec()] * 3,
        out_specs=vmem_spec(),
        scratch_shapes=[pltpu.VMEM((384, 128), F32), pltpu.VMEM((384, 128), F32)],
        compiler_params=pltpu.CompilerParams(vmem_limit_bytes=VMEM_LIMIT),
        cost_estimate=pl.CostEstimate(
            flops=3 * 512 * 4096 * 1024, transcendentals=3 * 512 * 4096, bytes_accessed=10 * 2**20
        ),
        name="attention_key_grad",
    )(pos, kv_own, q_all, do_all)


def unpack_mlp_kernel(in_ref, out_w_ref, fc_w_ref):
    step = pl.program_id(0)

    @pl.when(step < 8)
    def _():
        for g in range(4):
            out_w_ref[g, 0] = in_ref[0, g, :48].astype(F32)

    @pl.when(step >= 8)
    def _():
        for g in range(4):
            rows = in_ref[0, g, :48].astype(F32)
            fc_w_ref[0, :, 384 * g : 384 * g + 384] = rows[:, :384]
            fc_w_ref[0, :, 1536 + 384 * g : 1920 + 384 * g] = rows[:, 384:]


def unpack_mlp(early):
    out_w, fc_w = pl.pallas_call(
        unpack_mlp_kernel,
        grid=(16,),
        out_shape=(
            jax.ShapeDtypeStruct((4, 8, 48, 768), F32),
            jax.ShapeDtypeStruct((8, 48, 3072), F32),
        ),
        in_specs=[pl.BlockSpec((1, 4, 64, 768), lambda s: (s, 0, 0, 0))],
        out_specs=(
            pl.BlockSpec((4, 1, 48, 768), lambda s: (0, jnp.minimum(s, 7), 0, 0)),
            pl.BlockSpec((1, 48, 3072), lambda s: (jnp.maximum(s - 8, 0), 0, 0)),
        ),
        name="unpack_mlp",
    )(early)
    return out_w.reshape(1536, 768), fc_w.reshape(384, 3072)


def unpack_qkv_kernel(in_ref, out_ref):
    rows = [in_ref[0, g, :24].astype(F32) for g in range(4)]
    out_ref[0, :, :768] = jnp.concatenate([r[:, :192] for r in rows], axis=1)
    out_ref[0, :, 768:1536] = jnp.concatenate([r[:, 256:448] for r in rows], axis=1)
    out_ref[0, :, 1536:] = jnp.concatenate(
        [part for r in rows for part in (r[:, 512:], r[:, 448:512])], axis=1
    )


def unpack_qkv(late):
    rows = late.shape[2]
    return pl.pallas_call(
        unpack_qkv_kernel,
        grid=(16,),
        out_shape=jax.ShapeDtypeStruct((16, 24, 2304), F32),
        in_specs=[pl.BlockSpec((1, 4, rows, 640), lambda s: (s, 0, 0, 0))],
        out_specs=pl.BlockSpec((1, 24, 2304), lambda s: (s, 0, 0)),
        name="unpack_qkv",
    )(late).reshape(384, 2304)


def swap(values, axis):
    return lax.ppermute(values, axis, [(0, 1), (1, 0)])


def to_rank(values, offset):
    return lax.ppermute(values, TP, [(a, a ^ offset) for a in range(4)])


def gather_ranks(values):
    return [values] + [to_rank(values, r) for r in (1, 2, 3)]


def sum_ranks(partial):
    total = partial[0]
    for r in (1, 2, 3):
        total = total + to_rank(partial[r], r)
    return total


def pick(values, index, axis=0):
    return lax.dynamic_index_in_dim(values, index, axis, keepdims=False)


def normalize(values):
    center = jnp.mean(values, axis=-1, keepdims=True)
    centered = values - center
    scale = lax.rsqrt(jnp.mean(centered * centered, axis=-1, keepdims=True) + EPS)
    return (centered * scale, scale)


def norm_back(grad, normed, scale, gain):
    grad_normed = grad * gain
    first = jnp.mean(grad_normed, axis=-1, keepdims=True)
    second = jnp.mean(grad_normed * normed, axis=-1, keepdims=True)
    return scale * (grad_normed - first - normed * second)


def dot(a, b):
    return jnp.dot(a, b, preferred_element_type=F32)


def dot_nt(a, b):
    return jnp.einsum("ab,cb->ac", a, b, preferred_element_type=F32)


def dot_tn(a, b):
    return jnp.einsum("ta,tb->ab", a, b, preferred_element_type=F32)


def both_shards(own, fs):
    peer = swap(own, "fsdp")
    first = jnp.where(fs == 0, own, peer)
    second = jnp.where(fs == 0, peer, own)
    return jnp.stack([first, second])


def both_shards_by_core(own, fs):
    core = lax.axis_index("core")
    half = own.shape[0] // 2
    part = swap(lax.dynamic_slice_in_dim(own, half * core, half, 0), "fsdp")
    other = swap(part, "core")
    peer = jnp.concatenate(
        [jnp.where(core == 0, part, other), jnp.where(core == 0, other, part)], axis=0
    )
    first = jnp.where(fs == 0, own, peer)
    second = jnp.where(fs == 0, peer, own)
    return jnp.stack([first, second])


def after(values, *earlier):
    return lax.optimization_barrier((values, *earlier))[0]


def reduce_pieces(blocks, shared, fs, by_permute):
    half = blocks.shape[1] // 2
    local = jnp.concatenate([blocks, shared], axis=1)
    rows, width = local.shape[1:]
    if by_permute:
        part = local.reshape(2, 2, 2, 2, rows, width)
        for axis, dim in (("core", 3), ("yl", 2), ("yh", 1), ("xl", 0)):
            bit = lax.axis_index(axis)
            part = pick(part, bit, dim) + swap(pick(part, 1 - bit, dim), axis)
    else:
        part = lax.psum_scatter(local, SEQ_AXES, scatter_dimension=0, tiled=False)
    part = part.reshape(rows, width)
    rest = part[2 * half :]
    own = lax.dynamic_slice_in_dim(part, fs * half, half, 0)
    other = lax.dynamic_slice_in_dim(part, (1 - fs) * half, half, 0)
    total = jnp.concatenate([own, rest], axis=0) + swap(
        jnp.concatenate([other, rest], axis=0), "fsdp"
    )
    total = total.astype(BF16)
    rank = lax.axis_index(TP)
    ranks = jnp.stack(gather_ranks(total))
    ranks = jnp.stack([pick(ranks, rank ^ k) for k in range(4)])
    if by_permute:
        out = ranks[None]
        for axis in ("xl", "yh", "yl", "core"):
            peer = swap(out, axis)
            bit = lax.axis_index(axis)
            pair = jnp.stack([jnp.where(bit == 0, out, peer), jnp.where(bit == 0, peer, out)])
            out = jnp.moveaxis(pair, 0, 1).reshape((-1,) + ranks.shape)
        return out
    return lax.all_gather(ranks, SEQ_AXES, axis=0, tiled=False)


def body(
    block_in,
    out_grad,
    ln1_gain,
    ln1_bias,
    w_qkv,
    q_bias,
    v_bias,
    w_proj,
    b_proj,
    ln2_gain,
    ln2_bias,
    w_fc,
    b_fc,
    w_out,
    b_out,
):
    rank = lax.axis_index(TP)
    seq = lax.axis_index(SEQ_AXES)
    fs = lax.axis_index("fsdp")
    pos = jnp.stack([seq, rank]).astype(jnp.int32)

    x_low = jnp.concatenate(gather_ranks(block_in[0]), axis=0)
    w_q = lax.dynamic_slice_in_dim(w_qkv, 192 * rank, 192, 1)
    w_k = lax.dynamic_slice_in_dim(w_qkv, 768 + 192 * rank, 192, 1)
    w_v = lax.dynamic_slice_in_dim(w_qkv, 1536 + 192 * rank, 192, 1)
    qkv_shard = jnp.concatenate(
        [w_q, jnp.zeros((384, 64), BF16), w_k, w_v[:, 128:], w_v[:, :128]], axis=1
    )
    w_cols = both_shards(qkv_shard, fs).reshape(768, 640)
    small = jnp.concatenate(
        [ln1_gain, ln1_bias, q_bias, v_bias, b_proj, ln2_gain, ln2_bias, b_out, b_fc]
    )
    small = both_shards(small.reshape(36, 128), fs).reshape(2, 4608).astype(F32)
    wide = small[:, :3072].reshape(2, 8, 384).transpose(1, 0, 2).reshape(8, 768)
    gain_one, shift_one, query_bias, value_bias, proj_bias, gain_two, shift_two, out_bias = wide
    fc_bias = lax.dynamic_slice_in_dim(small[:, 3072:], 384 * rank, 384, 1).reshape(768)
    q_own = lax.dynamic_slice_in_dim(query_bias, 192 * rank, 192, 0)
    v_own = lax.dynamic_slice_in_dim(value_bias, 192 * rank, 192, 0)
    qkv_bias = jnp.concatenate(
        [q_own, jnp.zeros((64 + 192,), F32), v_own[128:], v_own[:128]], axis=0
    )
    proj_rows = both_shards_by_core(w_proj, fs).reshape(4, 3, 64, 768)
    proj_rows = jnp.concatenate(
        [proj_rows[:, :2], jnp.zeros((4, 1, 64, 768), BF16), proj_rows[:, 2:]], axis=1
    ).reshape(4, 256, 768)
    proj_ranks = [pick(proj_rows, rank ^ r) for r in range(4)]
    fc_halves = w_fc.reshape(384, 2, 1536)
    fc_shard = lax.dynamic_slice_in_dim(fc_halves, 384 * rank, 384, 2).reshape(384, 768)
    fc_cols = both_shards_by_core(fc_shard, fs).reshape(768, 768)
    out_shard = lax.dynamic_slice_in_dim(w_out, 384 * rank, 384, 0)
    out_rows = both_shards_by_core(out_shard, fs).reshape(768, 768)

    x = x_low.astype(F32)
    x_normed, x_scale = normalize(x)
    normed_one = (x_normed * gain_one + shift_one).astype(BF16)
    projected = dot(normed_one, w_cols) + qkv_bias
    q_scaled = (projected[:, :256].astype(BF16) * 0.125).astype(BF16).reshape(4, 128, 256)
    kv_own = projected[:, 256:].astype(BF16).reshape(4, 128, 384)
    kv_all = lax.all_gather(kv_own, SEQ_AXES, axis=0, tiled=False)
    attn, q_aug, lse = forward_attention(pos, q_scaled, kv_all)
    q_all = lax.all_gather(q_aug, SEQ_AXES, axis=0, tiled=False)

    attn_ranks = gather_ranks(attn)
    residual = x + proj_bias
    attn_full = jnp.concatenate(
        [
            jnp.concatenate([attn_ranks[r][k ^ r] for k in range(4)], axis=0) for r in range(4)
        ],
        axis=1,
    )
    residual = residual + dot(attn_full, jnp.concatenate(proj_ranks, axis=0))

    r_normed, r_scale = normalize(residual)
    normed_two = (r_normed * gain_two + shift_two).astype(BF16)
    hidden = dot(normed_two, fc_cols) + fc_bias
    cot_low = jnp.concatenate(gather_ranks(out_grad[0]), axis=0)
    grad_act = dot_nt(cot_low, out_rows)
    inner = GELU_F * (hidden + GELU_C * hidden * hidden * hidden)
    tanh = jnp.tanh(inner)
    activated = (0.5 * hidden * (1.0 + tanh)).astype(BF16)
    slope = 0.5 * (1.0 + tanh) + 0.5 * hidden * (1.0 - tanh * tanh) * GELU_F * (
        1.0 + 3.0 * GELU_C * hidden * hidden
    )
    grad_hidden = grad_act * slope
    grad_hidden_low = grad_hidden.astype(BF16)
    grad_normed_two = sum_ranks(dot_nt(grad_hidden_low, fc_cols).reshape(4, 128, 768))

    cot_own = out_grad[0].astype(F32)
    grad_residual = (
        norm_back(grad_normed_two, r_normed[:128], r_scale[:128], gain_two) + cot_own
    )
    grad_residual_low = jnp.concatenate(gather_ranks(grad_residual.astype(BF16)), axis=0)
    do_aug, delta = grad_rows(grad_residual_low, proj_ranks[0], attn)
    do_all = lax.all_gather(after(do_aug, q_all), SEQ_AXES, axis=0, tiled=False)
    grad_q = query_grad(pos, q_aug, do_aug, lse, delta, kv_all)

    activated, normed_two, grad_hidden_low, attn_late, grad_q, do_all = lax.optimization_barrier(
        (activated, normed_two, grad_hidden_low, attn, grad_q, do_all)
    )
    output = (
        sum_ranks(dot(activated, out_rows).reshape(4, 128, 768)) + out_bias + residual[:128]
    ).astype(BF16)
    grad_out_w = dot_tn(activated, cot_low).reshape(2, 384, 768)
    grad_fc_w = dot_tn(normed_two, grad_hidden_low).reshape(2, 384, 768)
    grad_proj_w = dot_tn(attn_late.reshape(512, 256), grad_residual_low)
    grad_proj_w = jnp.concatenate([grad_proj_w[:128], grad_proj_w[192:]], axis=0)
    extra = jnp.stack(
        [
            jnp.sum(grad_normed_two * r_normed[:128], axis=0),
            jnp.sum(grad_normed_two, axis=0),
            jnp.sum(grad_residual, axis=0),
            jnp.sum(cot_own, axis=0),
            jnp.sum(grad_hidden, axis=0),
        ]
        + [jnp.zeros((768,), F32)] * 11
    )
    early = reduce_pieces(
        jnp.concatenate([grad_out_w, grad_fc_w], axis=1)
        .reshape(2, 16, 48, 768)
        .transpose(1, 0, 2, 3)
        .reshape(16, 96, 768),
        jnp.concatenate(
            [grad_proj_w.reshape(16, 12, 768), extra[:, None], jnp.zeros((16, 3, 768), F32)], axis=1
        ),
        fs,
        False,
    )

    grad_kv = key_grad(pos, kv_own, q_all, do_all)
    grad_cols = jnp.concatenate([grad_q, grad_kv], axis=2).reshape(512, 640)
    grad_cols_low = grad_cols.astype(BF16)
    grad_qkv_w = dot_tn(normed_one, grad_cols_low).reshape(2, 16, 24, 640)
    partial_one = dot_nt(grad_cols_low, w_cols)
    late_extra = jnp.concatenate(
        [
            jnp.sum(grad_cols, axis=0),
            jnp.sum(partial_one * x_normed, axis=0),
            jnp.sum(partial_one, axis=0),
            jnp.zeros((640 * 15 - 1536,), F32),
        ]
    ).reshape(16, 1, 640)
    late = reduce_pieces(
        grad_qkv_w.transpose(1, 0, 2, 3).reshape(16, 48, 640), late_extra, fs, True
    )
    grad_normed_one = sum_ranks(partial_one.reshape(4, 128, 768))
    input_grad = (
        norm_back(grad_normed_one, x_normed[:128], x_scale[:128], gain_one) + grad_residual
    )

    def own_half(values):
        return lax.dynamic_slice_in_dim(values, 384 * fs, 384, 0)

    g_w_out, g_w_fc = unpack_mlp(early)
    early = early[:, :, 48:61].astype(F32)
    g_w_proj = lax.dynamic_slice_in_dim(early[:, :, :12], 2 * fs, 2, 1)
    g_w_proj = g_w_proj.transpose(1, 0, 2, 3).reshape(384, 768)
    sums = jnp.sum(early[:4, :, 12], axis=1)
    g_b_fc = pick(early[4, :, 12].reshape(4, 2, 384), fs, 1).reshape(1536)
    g_w_qkv = unpack_qkv(late)
    late = late[:4, :, 24].astype(F32)
    bias_row = late[0]
    g_q_bias = own_half(bias_row[:, :192].reshape(768))
    g_v_bias = own_half(
        jnp.concatenate([bias_row[:, 512:], bias_row[:, 448:512]], axis=1).reshape(768)
    )
    ln_one = jnp.sum(late[1:4], axis=1).reshape(1920)
    return (
        output[None],
        input_grad[None],
        own_half(ln_one[:768]),
        own_half(ln_one[768:1536]),
        g_w_qkv,
        g_q_bias,
        g_v_bias,
        g_w_proj,
        own_half(sums[2]),
        own_half(sums[0]),
        own_half(sums[1]),
        g_w_fc,
        g_b_fc,
        g_w_out,
        own_half(sums[3]),
    )


def solution(mesh):
    split = Mesh(
        mesh.devices.reshape(2, 2, 2, 2, 2, 2, 2),
        ("zl", "xh", "xl", "yh", "yl", "core", "fsdp"),
    )
    tokens = P("fsdp", CTX, None)
    vector = P("fsdp")
    matrix = P("fsdp", None)
    in_specs = (
        tokens,
        tokens,
        vector,
        vector,
        matrix,
        vector,
        vector,
        matrix,
        vector,
        vector,
        vector,
        matrix,
        vector,
        matrix,
        vector,
    )
    out_specs = (
        tokens,
        tokens,
        vector,
        vector,
        matrix,
        vector,
        vector,
        matrix,
        vector,
        vector,
        vector,
        matrix,
        vector,
        matrix,
        vector,
    )
    return jax.shard_map(body, mesh=split, in_specs=in_specs, out_specs=out_specs, check_vma=False)
```

```python
import jax
import jax.numpy as jnp
from jax import lax
from jax.experimental import pallas as pl
from jax.experimental.pallas import tpu as pltpu
from jax.sharding import Mesh, PartitionSpec as P

TP = ("zl", "xh")
SEQ_AXES = ("xl", "yh", "yl", "core")
BLOCKS = ("xl", "yh", "yl")
CTX = TP + SEQ_AXES
EPS = 1e-05
GELU_F = 0.7978845608028654
GELU_C = 0.044715
NEG = -1e30
F32 = jnp.float32
BF16 = jnp.bfloat16
NT = (((1,), (1,)), ((), ()))
VMEM_LIMIT = 56 * 1024 * 1024


def lane_half(shape):
    return lax.broadcasted_iota(jnp.int32, shape, len(shape) - 1) >= 64


def slot_only(values, slot):
    lane = lax.broadcasted_iota(jnp.int32, values.shape, 1)
    keep = jnp.logical_and(lane >= 64 * slot, lane < 64 * slot + 64)
    return jnp.where(keep, values, jnp.zeros_like(values))


def wide(values):
    return jnp.concatenate([values] * 4, axis=1)


def pieces(values):
    high = values.astype(BF16)
    rest = values - high.astype(F32)
    middle = rest.astype(BF16)
    low = (rest - middle.astype(F32)).astype(BF16)
    return (high, middle, low)


def chunk_rows(ref, rank, chunk):
    rows = ref[pl.ds(4 * lax.rem(chunk, 4), 4), rank ^ (chunk // 4)]
    return rows.reshape(512, rows.shape[-1])


def causal(scores, first_query, first_key, keys_in_rows):
    rows = lax.broadcasted_iota(jnp.int32, (128, 512), 0)
    cols = lax.broadcasted_iota(jnp.int32, (128, 512), 1)
    if keys_in_rows:
        allowed = first_key + rows <= first_query + cols
    else:
        allowed = first_key + cols <= first_query + rows
    return jnp.concatenate(
        [jnp.where(allowed, scores[128 * h : 128 * h + 128], NEG) for h in range(3)], axis=0
    )


def value_halves(product):
    return jnp.concatenate([product[:256, 128:], product[256:, :128]], axis=0)


def row_halves(product):
    return jnp.concatenate([product[:256, :128], product[256:, 128:]], axis=0)


def forward_kernel(pos_ref, q_ref, kv_ref, attn_ref, qaug_ref, lse_ref, m_ref, l_ref, acc_ref):
    seq = pos_ref[0]
    rank = pos_ref[1]

    def tile(k, carry):
        slot = rank ^ k
        block = k * 16 + seq
        q_rows = q_ref[slot]
        queries = jnp.concatenate([slot_only(q_rows, h) for h in range(3)], axis=0)
        m_ref[...] = jnp.full(m_ref.shape, NEG, F32)
        l_ref[...] = jnp.zeros(l_ref.shape, F32)
        acc_ref[...] = jnp.zeros(acc_ref.shape, F32)

        def step(chunk, masked):
            kv = chunk_rows(kv_ref, rank, chunk)
            scores = lax.dot_general(queries, kv[:, :256], NT, preferred_element_type=F32)
            if masked:
                scores = causal(scores, block * 128, chunk * 512, False)
            before = m_ref[...]
            after = jnp.maximum(before, jnp.max(scores, axis=1, keepdims=True))
            weights = jnp.exp(scores - wide(after))
            factor = jnp.exp(before - after)
            m_ref[...] = after
            partial = (weights[:, :128] + weights[:, 128:256]) + (
                weights[:, 256:384] + weights[:, 384:]
            )
            l_ref[...] = l_ref[...] * factor + partial
            acc_ref[...] = acc_ref[...] * factor + value_halves(
                jnp.dot(weights.astype(BF16), kv[:, 128:], preferred_element_type=F32)
            )

        last = block // 4

        def full(chunk, inner):
            step(chunk, False)
            return inner

        lax.fori_loop(0, last, full, 0)
        step(last, True)
        lane = lax.broadcasted_iota(jnp.int32, (128, 128), 1)
        extra = jnp.zeros((128, 128), BF16)
        total = jnp.sum(l_ref[...], axis=1, keepdims=True)
        log_sum = m_ref[...] + jnp.log(total)
        lse_ref[slot] = log_sum
        outs = acc_ref[...] / total
        for p, part in enumerate(pieces(-log_sum)):
            for h in range(3):
                extra = jnp.where(
                    lane == 64 + 3 * h + p, part[128 * h : 128 * h + 128], extra
                )
        attn_ref[slot, :, :128] = jnp.where(lane < 64, outs[:128], outs[128:256]).astype(BF16)
        attn_ref[slot, :, 128:] = jnp.where(lane < 64, 0.0, outs[256:]).astype(BF16)
        qaug_ref[slot, :, :128] = q_rows[:, :128]
        qaug_ref[slot, :, 128:] = jnp.where(lane < 64, q_rows[:, 128:], extra)
        return carry

    lax.fori_loop(0, 4, tile, 0)


def vmem_spec():
    return pl.BlockSpec(memory_space=pltpu.VMEM)


def forward_attention(pos, q, kv):
    return pl.pallas_call(
        forward_kernel,
        out_shape=(
            jax.ShapeDtypeStruct((4, 128, 256), BF16),
            jax.ShapeDtypeStruct((4, 128, 256), BF16),
            jax.ShapeDtypeStruct((4, 384, 128), F32),
        ),
        in_specs=[pl.BlockSpec(memory_space=pltpu.SMEM), vmem_spec(), vmem_spec()],
        out_specs=(vmem_spec(), vmem_spec(), vmem_spec()),
        scratch_shapes=[pltpu.VMEM((384, 128), F32)] * 3,
        compiler_params=pltpu.CompilerParams(vmem_limit_bytes=VMEM_LIMIT),
        cost_estimate=pl.CostEstimate(
            flops=3 * 512 * 4096 * 512, transcendentals=3 * 512 * 4096, bytes_accessed=8 * 2**20
        ),
        name="attention_forward",
    )(pos, q, kv)


def grad_rows_kernel(dr_ref, w_ref, attn_ref, do_ref, delta_ref):
    lane = lax.broadcasted_iota(jnp.int32, (512, 128), 1)
    grads = lax.dot_general(dr_ref[...], w_ref[...], NT, preferred_element_type=F32).astype(BF16)
    attn = attn_ref[...].reshape(512, 256).astype(F32)
    product = grads.astype(F32) * attn
    extra = jnp.zeros((512, 128), BF16)
    for h, run in enumerate((0, 1, 3)):
        delta = jnp.sum(slot_only(product, run), axis=1, keepdims=True)
        delta = jnp.broadcast_to(delta, (512, 128))
        for k in range(4):
            delta_ref[k, 128 * h : 128 * h + 128] = delta[128 * k : 128 * k + 128]
        for p, piece in enumerate(pieces(-delta)):
            extra = jnp.where(lane == 3 * h + p, piece, extra)
    do_ref[:, :, :128] = grads[:, :128].reshape(4, 128, 128)
    do_ref[:, :, 128:] = jnp.where(lane < 64, extra, grads[:, 128:]).reshape(4, 128, 128)


def grad_rows(dr_low, w_rows, attn):
    return pl.pallas_call(
        grad_rows_kernel,
        out_shape=(
            jax.ShapeDtypeStruct((4, 128, 256), BF16),
            jax.ShapeDtypeStruct((4, 384, 128), F32),
        ),
        in_specs=[vmem_spec(), vmem_spec(), vmem_spec()],
        out_specs=(vmem_spec(), vmem_spec()),
        compiler_params=pltpu.CompilerParams(vmem_limit_bytes=VMEM_LIMIT),
        name="attention_grad_rows",
    )(dr_low, w_rows, attn)


def query_grad_kernel(
    pos_ref, q_ref, do_ref, lse_ref, delta_ref, kv_ref, dq_ref, sum_ref, acc_ref
):
    seq = pos_ref[0]
    rank = pos_ref[1]

    def tile(k, carry):
        slot = rank ^ k
        block = k * 16 + seq
        q_rows = q_ref[slot]
        do_rows = do_ref[slot]
        queries = jnp.concatenate([slot_only(q_rows, h) for h in range(3)], axis=0)
        turned = jnp.concatenate([do_rows[:, 128:], do_rows[:, :128]], axis=1)
        grads = jnp.concatenate([slot_only(turned, run) for run in (2, 3, 1)], axis=0)
        acc_ref[...] = jnp.zeros(acc_ref.shape, F32)

        def step(chunk, masked):
            kv = chunk_rows(kv_ref, rank, chunk)
            scores = lax.dot_general(queries, kv[:, :256], NT, preferred_element_type=F32)
            scores = scores - wide(lse_ref[slot])
            if masked:
                scores = causal(scores, block * 128, chunk * 512, False)
            weights = jnp.exp(scores)
            grad_weights = lax.dot_general(grads, kv[:, 128:], NT, preferred_element_type=F32)
            grad_scores = (weights * (grad_weights - wide(delta_ref[slot]))).astype(BF16)
            acc_ref[...] += row_halves(
                jnp.dot(grad_scores, kv[:, :256], preferred_element_type=F32)
            )

        last = block // 4

        def full(chunk, inner):
            step(chunk, False)
            return inner

        lax.fori_loop(0, last, full, 0)
        step(last, True)
        lane = lax.broadcasted_iota(jnp.int32, (128, 128), 1)
        acc = acc_ref[...] * 0.125
        rows = jnp.concatenate(
            [
                jnp.where(lane < 64, acc[:128], acc[128:256]),
                jnp.where(lane < 64, acc[256:], 0.0),
            ],
            axis=1,
        )
        dq_ref[slot] = rows.astype(BF16)
        return carry + jnp.sum(rows, axis=0, keepdims=True)

    sum_ref[...] = lax.fori_loop(0, 4, tile, jnp.zeros((1, 256), F32))


def query_grad(pos, q, do, lse, delta, kv):
    return pl.pallas_call(
        query_grad_kernel,
        out_shape=(
            jax.ShapeDtypeStruct((4, 128, 256), BF16),
            jax.ShapeDtypeStruct((1, 256), F32),
        ),
        in_specs=[pl.BlockSpec(memory_space=pltpu.SMEM)] + [vmem_spec()] * 5,
        out_specs=(vmem_spec(), vmem_spec()),
        scratch_shapes=[pltpu.VMEM((384, 128), F32)],
        compiler_params=pltpu.CompilerParams(vmem_limit_bytes=VMEM_LIMIT),
        cost_estimate=pl.CostEstimate(
            flops=3 * 512 * 4096 * 768, transcendentals=3 * 512 * 4096, bytes_accessed=8 * 2**20
        ),
        name="attention_query_grad",
    )(pos, q, do, lse, delta, kv)


def key_grad_kernel(pos_ref, kv_ref, qg_ref, dog_ref, dkv_ref, sum_ref, dk_ref, dv_ref):
    seq = pos_ref[0]
    rank = pos_ref[1]

    def tile(k, carry):
        slot = rank ^ k
        block = k * 16 + seq
        rows = kv_ref[slot]
        lane = lax.broadcasted_iota(jnp.int32, (128, 256), 1)
        key_rows = rows[:, :256]
        value_rows = jnp.concatenate([rows[:, 256:], rows[:, 128:256]], axis=1)
        keys = []
        values = []
        for h, run in enumerate((0, 1, 3)):
            key_ones = jnp.logical_and(lane >= 192 + 3 * h, lane < 195 + 3 * h)
            value_ones = jnp.logical_and(lane >= 128 + 3 * h, lane < 131 + 3 * h)
            keys.append(jnp.where(key_ones, 1.0, slot_only(key_rows, h)).astype(BF16))
            values.append(jnp.where(value_ones, 1.0, slot_only(value_rows, run)).astype(BF16))
        keys = jnp.concatenate(keys, axis=0)
        values = jnp.concatenate(values, axis=0)
        dk_ref[...] = jnp.zeros(dk_ref.shape, F32)
        dv_ref[...] = jnp.zeros(dv_ref.shape, F32)

        def step(chunk, masked):
            q_rows = chunk_rows(qg_ref, rank, chunk)
            do_rows = chunk_rows(dog_ref, rank, chunk)
            scores = lax.dot_general(keys, q_rows, NT, preferred_element_type=F32)
            if masked:
                scores = causal(scores, chunk * 512, block * 128, True)
            weights = jnp.exp(scores)
            grad_weights = lax.dot_general(values, do_rows, NT, preferred_element_type=F32)
            grad_scores = (weights * grad_weights).astype(BF16)
            dv_ref[...] += row_halves(
                jnp.dot(weights.astype(BF16), do_rows, preferred_element_type=F32)
            )
            dk_ref[...] += row_halves(jnp.dot(grad_scores, q_rows, preferred_element_type=F32))

        first = block // 4

        def full(chunk, inner):
            step(chunk, False)
            return inner

        step(first, True)
        lax.fori_loop(first + 1, 16, full, 0)
        half = lax.broadcasted_iota(jnp.int32, (128, 128), 1) < 64
        grads = jnp.concatenate(
            [
                jnp.where(half, dk_ref[:128], dk_ref[128:256]),
                jnp.where(half, dk_ref[256:], dv_ref[256:]),
                jnp.where(half, dv_ref[:128], dv_ref[128:256]),
            ],
            axis=1,
        )
        dkv_ref[slot] = grads.astype(BF16)
        return carry + jnp.sum(grads, axis=0, keepdims=True)

    sum_ref[...] = lax.fori_loop(0, 4, tile, jnp.zeros((1, 384), F32))


def key_grad(pos, kv_own, q_all, do_all):
    return pl.pallas_call(
        key_grad_kernel,
        out_shape=(
            jax.ShapeDtypeStruct((4, 128, 384), BF16),
            jax.ShapeDtypeStruct((1, 384), F32),
        ),
        in_specs=[pl.BlockSpec(memory_space=pltpu.SMEM)] + [vmem_spec()] * 3,
        out_specs=(vmem_spec(), vmem_spec()),
        scratch_shapes=[pltpu.VMEM((384, 128), F32), pltpu.VMEM((384, 128), F32)],
        compiler_params=pltpu.CompilerParams(vmem_limit_bytes=VMEM_LIMIT),
        cost_estimate=pl.CostEstimate(
            flops=3 * 512 * 4096 * 1024, transcendentals=3 * 512 * 4096, bytes_accessed=10 * 2**20
        ),
        name="attention_key_grad",
    )(pos, kv_own, q_all, do_all)


def unpack_mlp_kernel(pos_ref, in_ref, out_w_ref, fc_w_ref):
    step = pl.program_id(0)
    rank = pos_ref[0]

    @pl.when(step < 8)
    def _():
        for g in range(4):
            out_w_ref[g, 0] = in_ref[0, rank ^ g, :48].astype(F32)

    @pl.when(step >= 8)
    def _():
        for g in range(4):
            rows = in_ref[0, rank ^ g, :48].astype(F32)
            fc_w_ref[0, :, 384 * g : 384 * g + 384] = rows[:, :384]
            fc_w_ref[0, :, 1536 + 384 * g : 1920 + 384 * g] = rows[:, 384:]


def unpack_mlp(pos, early):
    out_w, fc_w = pl.pallas_call(
        unpack_mlp_kernel,
        grid_spec=pltpu.PrefetchScalarGridSpec(
            num_scalar_prefetch=1,
            grid=(16,),
            in_specs=[pl.BlockSpec((1, 4, 64, 768), lambda s, pos: (s, 0, 0, 0))],
            out_specs=(
                pl.BlockSpec((4, 1, 48, 768), lambda s, pos: (0, jnp.minimum(s, 7), 0, 0)),
                pl.BlockSpec((1, 48, 3072), lambda s, pos: (jnp.maximum(s - 8, 0), 0, 0)),
            ),
        ),
        out_shape=(
            jax.ShapeDtypeStruct((4, 8, 48, 768), F32),
            jax.ShapeDtypeStruct((8, 48, 3072), F32),
        ),
        name="unpack_mlp",
    )(pos, early)
    return out_w.reshape(1536, 768), fc_w.reshape(384, 3072)


def unpack_qkv_kernel(pos_ref, in_ref, out_ref, extra_ref):
    rank = pos_ref[0]
    rows = [in_ref[0, 0, rank ^ g].astype(F32) for g in range(4)]
    out_ref[0, :, :768] = jnp.concatenate([r[:24, :192] for r in rows], axis=1)
    out_ref[0, :, 768:1536] = jnp.concatenate([r[:24, 256:448] for r in rows], axis=1)
    out_ref[0, :, 1536:] = jnp.concatenate(
        [part for r in rows for part in (r[:24, 512:], r[:24, 448:512])], axis=1
    )
    for g in range(4):
        extra_ref[0, g] = rows[g][24:]


def unpack_qkv(pos, late):
    grads, extra = pl.pallas_call(
        unpack_qkv_kernel,
        grid_spec=pltpu.PrefetchScalarGridSpec(
            num_scalar_prefetch=1,
            grid=(16,),
            in_specs=[
                pl.BlockSpec(
                    (1, 1, 4, 32, 640),
                    lambda s, pos: (lax.rem(s, 2) ^ pos[2], (s // 2) ^ pos[1], 0, 0, 0),
                )
            ],
            out_specs=(
                pl.BlockSpec((1, 24, 2304), lambda s, pos: (s, 0, 0)),
                pl.BlockSpec((1, 4, 8, 640), lambda s, pos: (s, 0, 0, 0)),
            ),
        ),
        out_shape=(
            jax.ShapeDtypeStruct((16, 24, 2304), F32),
            jax.ShapeDtypeStruct((16, 4, 8, 640), F32),
        ),
        name="unpack_qkv",
    )(pos, late)
    return grads.reshape(384, 2304), extra


def swap(values, axis):
    return lax.ppermute(values, axis, [(0, 1), (1, 0)])


def to_rank(values, offset):
    return lax.ppermute(values, TP, [(a, a ^ offset) for a in range(4)])


def gather_ranks(values):
    return [values] + [to_rank(values, r) for r in (1, 2, 3)]


def sum_ranks(partial):
    total = partial[0]
    for r in (1, 2, 3):
        total = total + to_rank(partial[r], r)
    return total


def pick(values, index, axis=0):
    return lax.dynamic_index_in_dim(values, index, axis, keepdims=False)


def normalize(values):
    center = jnp.mean(values, axis=-1, keepdims=True)
    centered = values - center
    scale = lax.rsqrt(jnp.mean(centered * centered, axis=-1, keepdims=True) + EPS)
    return (centered * scale, scale)


def norm_back(grad, normed, scale, gain):
    grad_normed = grad * gain
    first = jnp.mean(grad_normed, axis=-1, keepdims=True)
    second = jnp.mean(grad_normed * normed, axis=-1, keepdims=True)
    return scale * (grad_normed - first - normed * second)


def dot(a, b):
    return jnp.dot(a, b, preferred_element_type=F32)


def dot_nt(a, b):
    return jnp.einsum("ab,cb->ac", a, b, preferred_element_type=F32)


def dot_tn(a, b):
    return jnp.einsum("ta,tb->ab", a, b, preferred_element_type=F32)


def both_shards(own, fs):
    peer = swap(own, "fsdp")
    first = jnp.where(fs == 0, own, peer)
    second = jnp.where(fs == 0, peer, own)
    return jnp.stack([first, second])


def both_shards_by_core(own, fs):
    core = lax.axis_index("core")
    half = own.shape[0] // 2
    part = swap(lax.dynamic_slice_in_dim(own, half * core, half, 0), "fsdp")
    other = swap(part, "core")
    peer = jnp.concatenate(
        [jnp.where(core == 0, part, other), jnp.where(core == 0, other, part)], axis=0
    )
    first = jnp.where(fs == 0, own, peer)
    second = jnp.where(fs == 0, peer, own)
    return jnp.stack([first, second])


def after(values, *earlier):
    return lax.optimization_barrier((values, *earlier))[0]


def to_block(values, offset):
    return lax.ppermute(values, BLOCKS, [(a, a ^ offset) for a in range(8)])


def add_sequences(part, half, fs):
    rest = part[2 * half :]
    own = lax.dynamic_slice_in_dim(part, fs * half, half, 0)
    other = lax.dynamic_slice_in_dim(part, (1 - fs) * half, half, 0)
    total = jnp.concatenate([own, rest], axis=0) + swap(
        jnp.concatenate([other, rest], axis=0), "fsdp"
    )
    return total.astype(BF16)


def reduce_by_permute(local):
    core = lax.axis_index("core")
    block = lax.axis_index(BLOCKS)
    pair = local.reshape((8, 2) + local.shape[1:])
    pair = pick(pair, core, 1) + swap(pick(pair, 1 - core, 1), "core")
    moved = [to_block(pick(pair, block ^ r), r) for r in range(1, 8)]
    total = pick(pair, block)
    for values in moved:
        total = total + values
    return total


def body(
    block_in,
    out_grad,
    ln1_gain,
    ln1_bias,
    w_qkv,
    q_bias,
    v_bias,
    w_proj,
    b_proj,
    ln2_gain,
    ln2_bias,
    w_fc,
    b_fc,
    w_out,
    b_out,
):
    rank = lax.axis_index(TP)
    seq = lax.axis_index(SEQ_AXES)
    fs = lax.axis_index("fsdp")
    pos = jnp.stack([seq, rank]).astype(jnp.int32)

    x_low = jnp.concatenate(gather_ranks(block_in[0]), axis=0)
    w_q = lax.dynamic_slice_in_dim(w_qkv, 192 * rank, 192, 1)
    w_k = lax.dynamic_slice_in_dim(w_qkv, 768 + 192 * rank, 192, 1)
    w_v = lax.dynamic_slice_in_dim(w_qkv, 1536 + 192 * rank, 192, 1)
    qkv_shard = jnp.concatenate(
        [w_q, jnp.zeros((384, 64), BF16), w_k, w_v[:, 128:], w_v[:, :128]], axis=1
    )
    w_cols = both_shards(qkv_shard, fs).reshape(768, 640)
    vectors = (ln1_gain, ln1_bias, q_bias, v_bias, b_proj, ln2_gain, ln2_bias, b_out, b_fc)
    vectors = lax.optimization_barrier((qkv_shard,) + vectors)[1:]
    small = jnp.stack([v.astype(F32) for v in vectors[:8]])
    small = jnp.concatenate([small, vectors[8].astype(F32).reshape(4, 384)], axis=0)
    small = both_shards(small, fs)
    wide_vectors = small[:, :8].transpose(1, 0, 2).reshape(8, 768)
    gain_one, shift_one, query_bias, value_bias = wide_vectors[:4]
    proj_bias, gain_two, shift_two, out_bias = wide_vectors[4:]
    fc_bias = pick(small[:, 8:], rank, 1).reshape(768)
    q_own = lax.dynamic_slice_in_dim(query_bias, 192 * rank, 192, 0)
    v_own = lax.dynamic_slice_in_dim(value_bias, 192 * rank, 192, 0)
    qkv_bias = jnp.concatenate(
        [q_own, jnp.zeros((64 + 192,), F32), v_own[128:], v_own[:128]], axis=0
    )
    proj_rows = both_shards_by_core(w_proj, fs).reshape(4, 3, 64, 768)
    proj_rows = jnp.concatenate(
        [proj_rows[:, :2], jnp.zeros((4, 1, 64, 768), BF16), proj_rows[:, 2:]], axis=1
    ).reshape(4, 256, 768)
    proj_ranks = jnp.stack([pick(proj_rows, rank ^ r) for r in range(4)])
    fc_shard = jnp.concatenate(
        [
            lax.dynamic_slice_in_dim(w_fc, 384 * rank, 384, 1),
            lax.dynamic_slice_in_dim(w_fc, 1536 + 384 * rank, 384, 1),
        ],
        axis=1,
    )
    fc_cols = both_shards_by_core(fc_shard, fs).reshape(768, 768)
    out_shard = lax.dynamic_slice_in_dim(w_out, 384 * rank, 384, 0)
    out_rows = both_shards_by_core(out_shard, fs).reshape(768, 768)

    x = x_low.astype(F32)
    x_normed, x_scale = normalize(x)
    normed_one = (x_normed * gain_one + shift_one).astype(BF16)
    projected = dot(normed_one, w_cols) + qkv_bias
    q_scaled = (projected[:, :256].astype(BF16) * 0.125).astype(BF16).reshape(4, 128, 256)
    kv_own = projected[:, 256:].astype(BF16).reshape(4, 128, 384)
    kv_all = lax.all_gather(kv_own, SEQ_AXES, axis=0, tiled=False)
    kv_all, proj_ranks, fc_cols, out_rows, cot_low = lax.optimization_barrier(
        (kv_all, proj_ranks, fc_cols, out_rows, jnp.concatenate(gather_ranks(out_grad[0]), axis=0))
    )
    attn, q_aug, lse = forward_attention(pos, q_scaled, kv_all)

    attn_ranks = gather_ranks(attn)
    q_all = lax.all_gather(after(q_aug, *attn_ranks[1:]), SEQ_AXES, axis=0, tiled=False)
    residual = x + proj_bias
    attn_full = jnp.concatenate(
        [
            jnp.concatenate([attn_ranks[r][k ^ r] for k in range(4)], axis=0) for r in range(4)
        ],
        axis=1,
    )
    residual = residual + dot(attn_full, proj_ranks.reshape(1024, 768))

    r_normed, r_scale = normalize(residual)
    normed_two = (r_normed * gain_two + shift_two).astype(BF16)
    hidden = dot(normed_two, fc_cols) + fc_bias
    grad_act = dot_nt(cot_low, out_rows)
    inner = GELU_F * (hidden + GELU_C * hidden * hidden * hidden)
    tanh = jnp.tanh(inner)
    activated = (0.5 * hidden * (1.0 + tanh)).astype(BF16)
    slope = 0.5 * (1.0 + tanh) + 0.5 * hidden * (1.0 - tanh * tanh) * GELU_F * (
        1.0 + 3.0 * GELU_C * hidden * hidden
    )
    grad_hidden = grad_act * slope
    grad_hidden_low = grad_hidden.astype(BF16)
    grad_normed_two = sum_ranks(dot_nt(grad_hidden_low, fc_cols).reshape(4, 128, 768))

    cot_own = out_grad[0].astype(F32)
    grad_residual = (
        norm_back(grad_normed_two, r_normed[:128], r_scale[:128], gain_two) + cot_own
    )
    grad_residual_low = jnp.concatenate(gather_ranks(grad_residual.astype(BF16)), axis=0)
    do_aug, delta = grad_rows(grad_residual_low, proj_ranks[0], attn)
    do_all = lax.all_gather(after(do_aug, q_all), SEQ_AXES, axis=0, tiled=False)
    grad_q, grad_q_sum = query_grad(pos, q_aug, do_aug, lse, delta, kv_all)

    activated, normed_two, grad_hidden_low, attn_late, grad_q = lax.optimization_barrier(
        (activated, normed_two, grad_hidden_low, attn, grad_q)
    )
    out_partial = dot(activated, out_rows).reshape(4, 128, 768)
    grad_out_w = dot_tn(activated, cot_low).reshape(2, 384, 768)
    grad_fc_w = dot_tn(normed_two, grad_hidden_low).reshape(2, 384, 768)
    grad_proj_w = dot_tn(attn_late.reshape(512, 256), grad_residual_low)
    grad_proj_w = jnp.concatenate([grad_proj_w[:128], grad_proj_w[192:]], axis=0)
    extra = jnp.stack(
        [
            jnp.sum(grad_normed_two * r_normed[:128], axis=0),
            jnp.sum(grad_normed_two, axis=0),
            jnp.sum(grad_residual, axis=0),
            jnp.sum(cot_own, axis=0),
            jnp.sum(grad_hidden, axis=0),
        ]
        + [jnp.zeros((768,), F32)] * 11
    )
    local = jnp.concatenate(
        [
            jnp.concatenate([grad_out_w, grad_fc_w], axis=1)
            .reshape(2, 16, 48, 768)
            .transpose(1, 0, 2, 3)
            .reshape(16, 96, 768),
            grad_proj_w.reshape(16, 12, 768),
            extra[:, None],
            jnp.zeros((16, 3, 768), F32),
        ],
        axis=1,
    )
    local, do_all, out_partial = lax.optimization_barrier((local, do_all, out_partial))
    early = lax.psum_scatter(local, SEQ_AXES, scatter_dimension=0, tiled=False)
    out_moved = [to_rank(out_partial[r], r) for r in (1, 2, 3)]

    grad_kv, grad_kv_sum = key_grad(pos, kv_own, q_all, do_all)
    out_moved = after(tuple(out_moved), grad_kv)
    output = (
        out_partial[0] + out_moved[0] + out_moved[1] + out_moved[2] + out_bias + residual[:128]
    ).astype(BF16)

    grad_cols = jnp.concatenate([grad_q, grad_kv], axis=2).reshape(512, 640)
    grad_qkv_w = dot_tn(normed_one, grad_cols).reshape(2, 16, 24, 640)
    partial_one = dot_nt(grad_cols, w_cols)
    late_extra = jnp.concatenate(
        [
            grad_q_sum[0],
            grad_kv_sum[0],
            jnp.sum(partial_one * x_normed, axis=0),
            jnp.sum(partial_one, axis=0),
            jnp.zeros((640 * 15 - 1536,), F32),
        ]
    ).reshape(16, 1, 640)
    late_local = jnp.concatenate(
        [
            grad_qkv_w.transpose(1, 0, 2, 3).reshape(16, 48, 640),
            late_extra,
            jnp.zeros((16, 7, 640), F32),
        ],
        axis=1,
    )
    late = add_sequences(reduce_by_permute(late_local), 24, fs)

    early, late, partial_one = lax.optimization_barrier((early, late, partial_one))
    early = add_sequences(early, 48, fs)
    early_ranks = gather_ranks(early)
    late_ranks = gather_ranks(late)
    early = lax.all_gather(jnp.stack(early_ranks), SEQ_AXES, axis=0, tiled=False)
    late = jnp.stack(late_ranks)
    late = jnp.stack([late] + [to_block(late, r) for r in range(1, 8)])
    late = jnp.stack([late, swap(late, "core")])
    g_w_qkv, late_extra = unpack_qkv(
        jnp.stack([rank, lax.axis_index(BLOCKS), lax.axis_index("core")]).astype(jnp.int32), late
    )
    grad_normed_one = sum_ranks(partial_one.reshape(4, 128, 768))
    input_grad = (
        norm_back(grad_normed_one, x_normed[:128], x_scale[:128], gain_one) + grad_residual
    )
    early, g_w_qkv, input_grad = lax.optimization_barrier((early, g_w_qkv, input_grad))

    def own_half(values):
        return lax.dynamic_slice_in_dim(values, 384 * fs, 384, 0)

    g_w_out, g_w_fc = unpack_mlp(jnp.stack([rank]).astype(jnp.int32), early)
    early = early[:, :, 48:61].astype(F32)
    early = jnp.stack([pick(early, rank ^ g, 1) for g in range(4)], axis=1)
    g_w_proj = lax.dynamic_slice_in_dim(early[:, :, :12], 2 * fs, 2, 1)
    g_w_proj = g_w_proj.transpose(1, 0, 2, 3).reshape(384, 768)
    sums = jnp.sum(early[:4, :, 12], axis=1)
    g_b_fc = pick(early[4, :, 12].reshape(4, 2, 384), fs, 1).reshape(1536)
    late_rows = late_extra[:4, :, 0]
    bias_row = late_rows[0]
    g_q_bias = own_half(bias_row[:, :192].reshape(768))
    g_v_bias = own_half(
        jnp.concatenate([bias_row[:, 512:], bias_row[:, 448:512]], axis=1).reshape(768)
    )
    ln_one = jnp.sum(late_rows[1:], axis=1).reshape(1920)
    return (
        output[None],
        input_grad[None],
        own_half(ln_one[:768]),
        own_half(ln_one[768:1536]),
        g_w_qkv,
        g_q_bias,
        g_v_bias,
        g_w_proj,
        own_half(sums[2]),
        own_half(sums[0]),
        own_half(sums[1]),
        g_w_fc,
        g_b_fc,
        g_w_out,
        own_half(sums[3]),
    )


def solution(mesh):
    split = Mesh(
        mesh.devices.reshape(2, 2, 2, 2, 2, 2, 2),
        ("zl", "xh", "xl", "yh", "yl", "core", "fsdp"),
    )
    tokens = P("fsdp", CTX, None)
    vector = P("fsdp")
    matrix = P("fsdp", None)
    in_specs = (
        tokens,
        tokens,
        vector,
        vector,
        matrix,
        vector,
        vector,
        matrix,
        vector,
        vector,
        vector,
        matrix,
        vector,
        matrix,
        vector,
    )
    out_specs = (
        tokens,
        tokens,
        vector,
        vector,
        matrix,
        vector,
        vector,
        matrix,
        vector,
        vector,
        vector,
        matrix,
        vector,
        matrix,
        vector,
    )
    return jax.shard_map(body, mesh=split, in_specs=in_specs, out_specs=out_specs, check_vma=False)
```

```python
import jax
import jax.numpy as jnp
from jax import lax
from jax.experimental import pallas as pl
from jax.experimental.pallas import tpu as pltpu
from jax.sharding import Mesh, PartitionSpec as P

TP = ("zl", "xh")
SEQ_AXES = ("xl", "yh", "yl", "core")
BLOCKS = ("xl", "yh", "yl")
CTX = TP + SEQ_AXES
EPS = 1e-05
GELU_F = 0.7978845608028654
GELU_C = 0.044715
NEG = -1e30
F32 = jnp.float32
BF16 = jnp.bfloat16
NT = (((1,), (1,)), ((), ()))
VMEM_LIMIT = 56 * 1024 * 1024


def lane_half(shape):
    return lax.broadcasted_iota(jnp.int32, shape, len(shape) - 1) >= 64


def slot_only(values, slot):
    lane = lax.broadcasted_iota(jnp.int32, values.shape, 1)
    keep = jnp.logical_and(lane >= 64 * slot, lane < 64 * slot + 64)
    return jnp.where(keep, values, jnp.zeros_like(values))


def wide(values):
    return jnp.concatenate([values] * 4, axis=1)


def pieces(values):
    high = values.astype(BF16)
    rest = values - high.astype(F32)
    middle = rest.astype(BF16)
    low = (rest - middle.astype(F32)).astype(BF16)
    return (high, middle, low)


def chunk_rows(ref, rank, chunk):
    rows = ref[pl.ds(4 * lax.rem(chunk, 4), 4), rank ^ (chunk // 4)]
    return rows.reshape(512, rows.shape[-1])


def causal(scores, first_query, first_key, keys_in_rows):
    rows = lax.broadcasted_iota(jnp.int32, (128, 512), 0)
    cols = lax.broadcasted_iota(jnp.int32, (128, 512), 1)
    if keys_in_rows:
        allowed = first_key + rows <= first_query + cols
    else:
        allowed = first_key + cols <= first_query + rows
    return jnp.concatenate(
        [jnp.where(allowed, scores[128 * h : 128 * h + 128], NEG) for h in range(3)], axis=0
    )


def value_halves(product):
    return jnp.concatenate([product[:256, 128:], product[256:, :128]], axis=0)


def row_halves(product):
    return jnp.concatenate([product[:256, :128], product[256:, 128:]], axis=0)


def forward_kernel(pos_ref, q_ref, kv_ref, attn_ref, lse_ref, m_ref, l_ref, acc_ref):
    seq = pos_ref[0]
    rank = pos_ref[1]

    def tile(k, carry):
        slot = rank ^ k
        block = k * 16 + seq
        q_rows = q_ref[slot]
        queries = jnp.concatenate([slot_only(q_rows, h) for h in range(3)], axis=0)
        m_ref[...] = jnp.full(m_ref.shape, NEG, F32)
        l_ref[...] = jnp.zeros(l_ref.shape, F32)
        acc_ref[...] = jnp.zeros(acc_ref.shape, F32)

        def step(chunk, masked):
            kv = chunk_rows(kv_ref, rank, chunk)
            scores = lax.dot_general(queries, kv[:, :256], NT, preferred_element_type=F32)
            if masked:
                scores = causal(scores, block * 128, chunk * 512, False)
            before = m_ref[...]
            after = jnp.maximum(before, jnp.max(scores, axis=1, keepdims=True))
            weights = jnp.exp(scores - wide(after))
            factor = jnp.exp(before - after)
            m_ref[...] = after
            partial = (weights[:, :128] + weights[:, 128:256]) + (
                weights[:, 256:384] + weights[:, 384:]
            )
            l_ref[...] = l_ref[...] * factor + partial
            acc_ref[...] = acc_ref[...] * factor + value_halves(
                jnp.dot(weights.astype(BF16), kv[:, 128:], preferred_element_type=F32)
            )

        last = block // 4

        def full(chunk, inner):
            step(chunk, False)
            return inner

        lax.fori_loop(0, last, full, 0)
        step(last, True)
        lane = lax.broadcasted_iota(jnp.int32, (128, 128), 1)
        total = jnp.sum(l_ref[...], axis=1, keepdims=True)
        log_sum = m_ref[...] + jnp.log(total)
        lse_ref[slot] = log_sum
        outs = acc_ref[...] / total
        attn_ref[slot, :, :128] = jnp.where(lane < 64, outs[:128], outs[128:256]).astype(BF16)
        attn_ref[slot, :, 128:] = jnp.where(lane < 64, 0.0, outs[256:]).astype(BF16)
        return carry

    lax.fori_loop(0, 4, tile, 0)


def vmem_spec():
    return pl.BlockSpec(memory_space=pltpu.VMEM)


def forward_attention(pos, q, kv):
    return pl.pallas_call(
        forward_kernel,
        out_shape=(
            jax.ShapeDtypeStruct((4, 128, 256), BF16),
            jax.ShapeDtypeStruct((4, 384, 128), F32),
        ),
        in_specs=[pl.BlockSpec(memory_space=pltpu.SMEM), vmem_spec(), vmem_spec()],
        out_specs=(vmem_spec(), vmem_spec()),
        scratch_shapes=[pltpu.VMEM((384, 128), F32)] * 3,
        compiler_params=pltpu.CompilerParams(vmem_limit_bytes=VMEM_LIMIT),
        cost_estimate=pl.CostEstimate(
            flops=3 * 512 * 4096 * 512, transcendentals=3 * 512 * 4096, bytes_accessed=8 * 2**20
        ),
        name="attention_forward",
    )(pos, q, kv)


def grad_rows_kernel(dr_ref, w_ref, attn_ref, lse_ref, do_ref, delta_ref):
    lane = lax.broadcasted_iota(jnp.int32, (512, 128), 1)
    grads = lax.dot_general(dr_ref[...], w_ref[...], NT, preferred_element_type=F32).astype(BF16)
    attn = attn_ref[...].reshape(512, 256).astype(F32)
    product = grads.astype(F32) * attn
    extra = jnp.zeros((512, 128), BF16)
    for h, run in enumerate((0, 1, 3)):
        delta = jnp.sum(slot_only(product, run), axis=1, keepdims=True)
        delta = jnp.broadcast_to(delta, (512, 128))
        for k in range(4):
            delta_ref[k, 128 * h : 128 * h + 128] = delta[128 * k : 128 * k + 128]
        log_sum = jnp.concatenate([lse_ref[k, 128 * h : 128 * h + 128] for k in range(4)], axis=0)
        for p, (piece, other) in enumerate(zip(pieces(-delta), pieces(-log_sum))):
            extra = jnp.where(lane == 3 * h + p, piece, extra)
            extra = jnp.where(lane == 16 + 3 * h + p, other, extra)
    do_ref[:, :, :128] = grads[:, :128].reshape(4, 128, 128)
    do_ref[:, :, 128:] = jnp.where(lane < 64, extra, grads[:, 128:]).reshape(4, 128, 128)


def grad_rows(dr_low, w_rows, attn, lse):
    return pl.pallas_call(
        grad_rows_kernel,
        out_shape=(
            jax.ShapeDtypeStruct((4, 128, 256), BF16),
            jax.ShapeDtypeStruct((4, 384, 128), F32),
        ),
        in_specs=[vmem_spec()] * 4,
        out_specs=(vmem_spec(), vmem_spec()),
        compiler_params=pltpu.CompilerParams(vmem_limit_bytes=VMEM_LIMIT),
        name="attention_grad_rows",
    )(dr_low, w_rows, attn, lse)


def query_grad_kernel(
    pos_ref, q_ref, do_ref, lse_ref, delta_ref, kv_ref, dq_ref, sum_ref, acc_ref
):
    seq = pos_ref[0]
    rank = pos_ref[1]

    def tile(k, carry):
        slot = rank ^ k
        block = k * 16 + seq
        q_rows = q_ref[slot]
        do_rows = do_ref[slot]
        queries = jnp.concatenate([slot_only(q_rows, h) for h in range(3)], axis=0)
        turned = jnp.concatenate([do_rows[:, 128:], do_rows[:, :128]], axis=1)
        grads = jnp.concatenate([slot_only(turned, run) for run in (2, 3, 1)], axis=0)
        acc_ref[...] = jnp.zeros(acc_ref.shape, F32)

        def step(chunk, masked):
            kv = chunk_rows(kv_ref, rank, chunk)
            scores = lax.dot_general(queries, kv[:, :256], NT, preferred_element_type=F32)
            scores = scores - wide(lse_ref[slot])
            if masked:
                scores = causal(scores, block * 128, chunk * 512, False)
            weights = jnp.exp(scores)
            grad_weights = lax.dot_general(grads, kv[:, 128:], NT, preferred_element_type=F32)
            grad_scores = (weights * (grad_weights - wide(delta_ref[slot]))).astype(BF16)
            acc_ref[...] += row_halves(
                jnp.dot(grad_scores, kv[:, :256], preferred_element_type=F32)
            )

        last = block // 4

        def full(chunk, inner):
            step(chunk, False)
            return inner

        lax.fori_loop(0, last, full, 0)
        step(last, True)
        lane = lax.broadcasted_iota(jnp.int32, (128, 128), 1)
        acc = acc_ref[...] * 0.125
        rows = jnp.concatenate(
            [
                jnp.where(lane < 64, acc[:128], acc[128:256]),
                jnp.where(lane < 64, acc[256:], 0.0),
            ],
            axis=1,
        )
        dq_ref[slot] = rows.astype(BF16)
        return carry + jnp.sum(rows, axis=0, keepdims=True)

    sum_ref[...] = lax.fori_loop(0, 4, tile, jnp.zeros((1, 256), F32))


def query_grad(pos, q, do, lse, delta, kv):
    return pl.pallas_call(
        query_grad_kernel,
        out_shape=(
            jax.ShapeDtypeStruct((4, 128, 256), BF16),
            jax.ShapeDtypeStruct((1, 256), F32),
        ),
        in_specs=[pl.BlockSpec(memory_space=pltpu.SMEM)] + [vmem_spec()] * 5,
        out_specs=(vmem_spec(), vmem_spec()),
        scratch_shapes=[pltpu.VMEM((384, 128), F32)],
        compiler_params=pltpu.CompilerParams(vmem_limit_bytes=VMEM_LIMIT),
        cost_estimate=pl.CostEstimate(
            flops=3 * 512 * 4096 * 768, transcendentals=3 * 512 * 4096, bytes_accessed=8 * 2**20
        ),
        name="attention_query_grad",
    )(pos, q, do, lse, delta, kv)


def key_grad_kernel(
    pos_ref, kv_ref, qg_ref, dog_ref, dkv_ref, sum_ref, dk_ref, dv_ref, join_ref
):
    seq = pos_ref[0]
    rank = pos_ref[1]

    def join(chunk, carry):
        q_rows = chunk_rows(qg_ref, rank, chunk)[:, 128:]
        do_rows = chunk_rows(dog_ref, rank, chunk)[:, 128:]
        join_ref[chunk] = jnp.concatenate([q_rows[:, :64], do_rows[:, :64]], axis=1)
        return carry

    lax.fori_loop(seq // 4, 16, join, 0)

    def tile(k, carry):
        slot = rank ^ k
        block = k * 16 + seq
        rows = kv_ref[slot]
        lane = lax.broadcasted_iota(jnp.int32, (128, 256), 1)
        key_rows = rows[:, :256]
        value_rows = jnp.concatenate([rows[:, 256:], rows[:, 128:256]], axis=1)
        keys = []
        values = []
        for h, run in enumerate((0, 1, 3)):
            key_ones = jnp.logical_and(lane >= 208 + 3 * h, lane < 211 + 3 * h)
            value_ones = jnp.logical_and(lane >= 128 + 3 * h, lane < 131 + 3 * h)
            keys.append(jnp.where(key_ones, 1.0, slot_only(key_rows, h)).astype(BF16))
            values.append(jnp.where(value_ones, 1.0, slot_only(value_rows, run)).astype(BF16))
        keys = jnp.concatenate(keys, axis=0)
        values = jnp.concatenate(values, axis=0)
        dk_ref[...] = jnp.zeros(dk_ref.shape, F32)
        dv_ref[...] = jnp.zeros(dv_ref.shape, F32)

        def step(chunk, masked):
            q_rows = chunk_rows(qg_ref, rank, chunk)[:, :128]
            q_rows = jnp.concatenate([q_rows, join_ref[chunk]], axis=1)
            do_rows = chunk_rows(dog_ref, rank, chunk)
            scores = lax.dot_general(keys, q_rows, NT, preferred_element_type=F32)
            if masked:
                scores = causal(scores, chunk * 512, block * 128, True)
            weights = jnp.exp(scores)
            grad_weights = lax.dot_general(values, do_rows, NT, preferred_element_type=F32)
            grad_scores = (weights * grad_weights).astype(BF16)
            dv_ref[...] += row_halves(
                jnp.dot(weights.astype(BF16), do_rows, preferred_element_type=F32)
            )
            dk_ref[...] += row_halves(jnp.dot(grad_scores, q_rows, preferred_element_type=F32))

        first = block // 4

        def full(chunk, inner):
            step(chunk, False)
            return inner

        step(first, True)
        lax.fori_loop(first + 1, 16, full, 0)
        half = lax.broadcasted_iota(jnp.int32, (128, 128), 1) < 64
        grads = jnp.concatenate(
            [
                jnp.where(half, dk_ref[:128], dk_ref[128:256]),
                jnp.where(half, dk_ref[256:], dv_ref[256:]),
                jnp.where(half, dv_ref[:128], dv_ref[128:256]),
            ],
            axis=1,
        )
        dkv_ref[slot] = grads.astype(BF16)
        return carry + jnp.sum(grads, axis=0, keepdims=True)

    sum_ref[...] = lax.fori_loop(0, 4, tile, jnp.zeros((1, 384), F32))


def key_grad(pos, kv_own, q_all, do_all):
    return pl.pallas_call(
        key_grad_kernel,
        out_shape=(
            jax.ShapeDtypeStruct((4, 128, 384), BF16),
            jax.ShapeDtypeStruct((1, 384), F32),
        ),
        in_specs=[pl.BlockSpec(memory_space=pltpu.SMEM)] + [vmem_spec()] * 3,
        out_specs=(vmem_spec(), vmem_spec()),
        scratch_shapes=[
            pltpu.VMEM((384, 128), F32),
            pltpu.VMEM((384, 128), F32),
            pltpu.VMEM((16, 512, 128), BF16),
        ],
        compiler_params=pltpu.CompilerParams(vmem_limit_bytes=VMEM_LIMIT),
        cost_estimate=pl.CostEstimate(
            flops=3 * 512 * 4096 * 1024, transcendentals=3 * 512 * 4096, bytes_accessed=10 * 2**20
        ),
        name="attention_key_grad",
    )(pos, kv_own, q_all, do_all)


def first_grads_kernel(
    norm_ref, hat_ref, q_ref, kv_ref, w_ref, q_sum_ref, kv_sum_ref, local_ref, dh_ref
):
    cols = jnp.concatenate([q_ref[...].reshape(512, 256), kv_ref[...].reshape(512, 384)], axis=1)
    for half in range(2):
        grads = jnp.dot(
            norm_ref[384 * half : 384 * half + 384], cols, preferred_element_type=F32
        )
        for block in range(16):
            local_ref[block % 2, block // 2, 24 * half : 24 * half + 24] = grads[
                24 * block : 24 * block + 24
            ]
    gain = jnp.zeros((1, 768), F32)
    shift = jnp.zeros((1, 768), F32)
    for k in range(4):
        rows = slice(128 * k, 128 * k + 128)
        part = lax.dot_general(cols[rows], w_ref[...], NT, preferred_element_type=F32)
        dh_ref[k] = part
        gain = gain + jnp.sum(part * hat_ref[rows], axis=0, keepdims=True)
        shift = shift + jnp.sum(part, axis=0, keepdims=True)
    extra = (
        jnp.concatenate([q_sum_ref[...], kv_sum_ref[...]], axis=1),
        gain[:, :640],
        jnp.concatenate([gain[:, 640:], shift[:, :512]], axis=1),
        jnp.concatenate([shift[:, 512:], jnp.zeros((1, 384), F32)], axis=1),
    )
    top = lax.broadcasted_iota(jnp.int32, (8, 640), 0) == 0
    for block in range(16):
        rows = jnp.zeros((8, 640), F32)
        if block < 4:
            rows = jnp.where(top, extra[block], rows)
        local_ref[block % 2, block // 2, 48:] = rows


def first_grads(norm_t, hat, dq, dkv, w_cols, q_sum, kv_sum):
    return pl.pallas_call(
        first_grads_kernel,
        out_shape=(
            jax.ShapeDtypeStruct((2, 8, 56, 640), F32),
            jax.ShapeDtypeStruct((4, 128, 768), F32),
        ),
        in_specs=[vmem_spec()] * 7,
        out_specs=(vmem_spec(), vmem_spec()),
        compiler_params=pltpu.CompilerParams(vmem_limit_bytes=VMEM_LIMIT),
        name="first_grads",
    )(norm_t, hat, dq, dkv, w_cols, q_sum, kv_sum)


def unpack_kernel(pos_ref, in_ref, out_w_ref, fc_w_ref, qkv_ref, extra_ref):
    step = pl.program_id(0)
    rank = pos_ref[0]

    @pl.when(step < 8)
    def _():
        for g in range(4):
            out_w_ref[g, 0] = in_ref[0, rank ^ g, :48].astype(F32)

    @pl.when(step >= 8)
    def _():
        for g in range(4):
            rows = in_ref[0, rank ^ g, :48].astype(F32)
            fc_w_ref[0, :, 384 * g : 384 * g + 384] = rows[:, :384]
            fc_w_ref[0, :, 1536 + 384 * g : 1920 + 384 * g] = rows[:, 384:]

    rows = [in_ref[0, rank ^ g, 48:].astype(F32) for g in range(4)]
    qkv_ref[0, :, :768] = jnp.concatenate([r[:24, :192] for r in rows], axis=1)
    qkv_ref[0, :, 768:1536] = jnp.concatenate([r[:24, 256:448] for r in rows], axis=1)
    qkv_ref[0, :, 1536:] = jnp.concatenate(
        [part for r in rows for part in (r[:24, 512:640], r[:24, 448:512])], axis=1
    )
    for g in range(4):
        extra_ref[0, g] = rows[g][24:]


def unpack(pos, totals):
    out_w, fc_w, qkv_w, extra = pl.pallas_call(
        unpack_kernel,
        grid_spec=pltpu.PrefetchScalarGridSpec(
            num_scalar_prefetch=1,
            grid=(16,),
            in_specs=[pl.BlockSpec((1, 4, 96, 768), lambda s, pos: (s, 0, 0, 0))],
            out_specs=(
                pl.BlockSpec((4, 1, 48, 768), lambda s, pos: (0, jnp.minimum(s, 7), 0, 0)),
                pl.BlockSpec((1, 48, 3072), lambda s, pos: (jnp.maximum(s - 8, 0), 0, 0)),
                pl.BlockSpec((1, 24, 2304), lambda s, pos: (s, 0, 0)),
                pl.BlockSpec((1, 4, 24, 768), lambda s, pos: (s, 0, 0, 0)),
            ),
        ),
        out_shape=(
            jax.ShapeDtypeStruct((4, 8, 48, 768), F32),
            jax.ShapeDtypeStruct((8, 48, 3072), F32),
            jax.ShapeDtypeStruct((16, 24, 2304), F32),
            jax.ShapeDtypeStruct((16, 4, 24, 768), F32),
        ),
        name="unpack_grads",
    )(pos, totals)
    return out_w.reshape(1536, 768), fc_w.reshape(384, 3072), qkv_w.reshape(384, 2304), extra


def swap(values, axis):
    return lax.ppermute(values, axis, [(0, 1), (1, 0)])


def to_rank(values, offset):
    return lax.ppermute(values, TP, [(a, a ^ offset) for a in range(4)])


def gather_ranks(values):
    return [values] + [to_rank(values, r) for r in (1, 2, 3)]


def sum_ranks(partial):
    total = partial[0]
    for r in (1, 2, 3):
        total = total + to_rank(partial[r], r)
    return total


def pick(values, index, axis=0):
    return lax.dynamic_index_in_dim(values, index, axis, keepdims=False)


def normalize(values):
    center = jnp.mean(values, axis=-1, keepdims=True)
    centered = values - center
    scale = lax.rsqrt(jnp.mean(centered * centered, axis=-1, keepdims=True) + EPS)
    return (centered * scale, scale)


def norm_back(grad, normed, scale, gain):
    grad_normed = grad * gain
    first = jnp.mean(grad_normed, axis=-1, keepdims=True)
    second = jnp.mean(grad_normed * normed, axis=-1, keepdims=True)
    return scale * (grad_normed - first - normed * second)


def dot(a, b):
    return jnp.dot(a, b, preferred_element_type=F32)


def dot_nt(a, b):
    return jnp.einsum("ab,cb->ac", a, b, preferred_element_type=F32)


def dot_tn(a, b):
    return jnp.einsum("ta,tb->ab", a, b, preferred_element_type=F32)


def both_shards(own, fs):
    peer = swap(own, "fsdp")
    first = jnp.where(fs == 0, own, peer)
    second = jnp.where(fs == 0, peer, own)
    return jnp.stack([first, second])


def both_shards_by_core(own, fs):
    core = lax.axis_index("core")
    half = own.shape[0] // 2
    part = swap(lax.dynamic_slice_in_dim(own, half * core, half, 0), "fsdp")
    other = swap(part, "core")
    peer = jnp.concatenate(
        [jnp.where(core == 0, part, other), jnp.where(core == 0, other, part)], axis=0
    )
    first = jnp.where(fs == 0, own, peer)
    second = jnp.where(fs == 0, peer, own)
    return jnp.stack([first, second])


def after(values, *earlier):
    return lax.optimization_barrier((values, *earlier))[0]


def to_block(values, offset):
    return lax.ppermute(values, BLOCKS, [(a, a ^ offset) for a in range(8)])


def reduce_by_permute(local):
    core = lax.axis_index("core")
    block = lax.axis_index(BLOCKS)
    pair = pick(local, core) + swap(pick(local, 1 - core), "core")
    moved = [to_block(pick(pair, block ^ r), r) for r in range(1, 8)]
    total = pick(pair, block)
    for values in moved:
        total = total + values
    return total


def body(
    block_in,
    out_grad,
    ln1_gain,
    ln1_bias,
    w_qkv,
    q_bias,
    v_bias,
    w_proj,
    b_proj,
    ln2_gain,
    ln2_bias,
    w_fc,
    b_fc,
    w_out,
    b_out,
):
    rank = lax.axis_index(TP)
    seq = lax.axis_index(SEQ_AXES)
    fs = lax.axis_index("fsdp")
    pos = jnp.stack([seq, rank]).astype(jnp.int32)

    x_low = jnp.concatenate(gather_ranks(block_in[0]), axis=0)
    w_q = lax.dynamic_slice_in_dim(w_qkv, 192 * rank, 192, 1)
    w_k = lax.dynamic_slice_in_dim(w_qkv, 768 + 192 * rank, 192, 1)
    w_v = lax.dynamic_slice_in_dim(w_qkv, 1536 + 192 * rank, 192, 1)
    qkv_shard = jnp.concatenate(
        [w_q, jnp.zeros((384, 64), BF16), w_k, w_v[:, 128:], w_v[:, :128]], axis=1
    )
    w_cols = both_shards(qkv_shard, fs).reshape(768, 640)
    vectors = (ln1_gain, ln1_bias, q_bias, v_bias, b_proj, ln2_gain, ln2_bias, b_out, b_fc)
    vectors = lax.optimization_barrier((qkv_shard,) + vectors)[1:]
    small = jnp.stack([v.astype(F32) for v in vectors[:8]])
    small = jnp.concatenate([small, vectors[8].astype(F32).reshape(4, 384)], axis=0)
    small = both_shards(small, fs)
    wide_vectors = small[:, :8].transpose(1, 0, 2).reshape(8, 768)
    gain_one, shift_one, query_bias, value_bias = wide_vectors[:4]
    proj_bias, gain_two, shift_two, out_bias = wide_vectors[4:]
    fc_bias = pick(small[:, 8:], rank, 1).reshape(768)
    q_own = lax.dynamic_slice_in_dim(query_bias, 192 * rank, 192, 0)
    v_own = lax.dynamic_slice_in_dim(value_bias, 192 * rank, 192, 0)
    qkv_bias = jnp.concatenate(
        [q_own, jnp.zeros((64 + 192,), F32), v_own[128:], v_own[:128]], axis=0
    )
    proj_rows = both_shards_by_core(w_proj, fs).reshape(4, 3, 64, 768)
    proj_rows = jnp.concatenate(
        [proj_rows[:, :2], jnp.zeros((4, 1, 64, 768), BF16), proj_rows[:, 2:]], axis=1
    ).reshape(4, 256, 768)
    proj_ranks = jnp.stack([pick(proj_rows, rank ^ r) for r in range(4)])
    fc_shard = jnp.concatenate(
        [
            lax.dynamic_slice_in_dim(w_fc, 384 * rank, 384, 1),
            lax.dynamic_slice_in_dim(w_fc, 1536 + 384 * rank, 384, 1),
        ],
        axis=1,
    )
    fc_cols = both_shards_by_core(fc_shard, fs).reshape(768, 768)
    out_shard = lax.dynamic_slice_in_dim(w_out, 384 * rank, 384, 0)
    out_rows = both_shards_by_core(out_shard, fs).reshape(768, 768)

    x = x_low.astype(F32)
    x_normed, x_scale = normalize(x)
    normed_one = (x_normed * gain_one + shift_one).astype(BF16)
    projected = dot(normed_one, w_cols) + qkv_bias
    q_scaled = (projected[:, :256].astype(BF16) * 0.125).astype(BF16).reshape(4, 128, 256)
    kv_own = projected[:, 256:].astype(BF16).reshape(4, 128, 384)
    kv_all = lax.all_gather(kv_own, SEQ_AXES, axis=0, tiled=False)
    q_all = lax.all_gather(after(q_scaled, kv_all), SEQ_AXES, axis=0, tiled=False)
    normed_one_t = normed_one.T
    kv_all, proj_ranks, fc_cols, out_rows, cot_low, normed_one_t = lax.optimization_barrier(
        (
            kv_all,
            proj_ranks,
            fc_cols,
            out_rows,
            jnp.concatenate(gather_ranks(out_grad[0]), axis=0),
            normed_one_t,
        )
    )
    attn, lse = forward_attention(pos, q_scaled, kv_all)

    attn_ranks = gather_ranks(attn)
    residual = x + proj_bias
    attn_full = jnp.concatenate(
        [
            jnp.concatenate([attn_ranks[r][k ^ r] for k in range(4)], axis=0) for r in range(4)
        ],
        axis=1,
    )
    residual = residual + dot(attn_full, proj_ranks.reshape(1024, 768))

    r_normed, r_scale = normalize(residual)
    normed_two = (r_normed * gain_two + shift_two).astype(BF16)
    hidden = dot(normed_two, fc_cols) + fc_bias
    grad_act = dot_nt(cot_low, out_rows)
    inner = GELU_F * (hidden + GELU_C * hidden * hidden * hidden)
    tanh = jnp.tanh(inner)
    activated = (0.5 * hidden * (1.0 + tanh)).astype(BF16)
    slope = 0.5 * (1.0 + tanh) + 0.5 * hidden * (1.0 - tanh * tanh) * GELU_F * (
        1.0 + 3.0 * GELU_C * hidden * hidden
    )
    grad_hidden = grad_act * slope
    grad_hidden_low = grad_hidden.astype(BF16)
    partial_two = dot_nt(grad_hidden_low, fc_cols).reshape(4, 128, 768)
    moved_two = tuple(to_rank(partial_two[r], r) for r in (1, 2, 3))
    grad_out_w = dot_tn(activated, cot_low).reshape(2, 384, 768)
    grad_fc_w = dot_tn(normed_two, grad_hidden_low).reshape(2, 384, 768)
    moved_two, grad_out_w, grad_fc_w = lax.optimization_barrier(
        (moved_two, grad_out_w, grad_fc_w)
    )
    grad_normed_two = partial_two[0] + moved_two[0] + moved_two[1] + moved_two[2]

    cot_own = out_grad[0].astype(F32)
    grad_residual = (
        norm_back(grad_normed_two, r_normed[:128], r_scale[:128], gain_two) + cot_own
    )
    grad_residual_low = jnp.concatenate(gather_ranks(grad_residual.astype(BF16)), axis=0)
    do_aug, delta = grad_rows(grad_residual_low, proj_ranks[0], attn, lse)
    do_all = lax.all_gather(after(do_aug, q_all), SEQ_AXES, axis=0, tiled=False)
    grad_q, grad_q_sum = query_grad(pos, q_scaled, do_aug, lse, delta, kv_all)

    (
        activated,
        attn_late,
        grad_q,
        grad_normed_two,
        grad_residual,
        grad_hidden,
        cot_own,
    ) = lax.optimization_barrier(
        (activated, attn, grad_q, grad_normed_two, grad_residual, grad_hidden, cot_own)
    )
    out_partial = dot(activated, out_rows).reshape(4, 128, 768)
    grad_proj_w = dot_tn(attn_late.reshape(512, 256), grad_residual_low)
    grad_proj_w = jnp.concatenate([grad_proj_w[:128], grad_proj_w[192:]], axis=0)
    extra = jnp.stack(
        [
            jnp.sum(grad_normed_two * r_normed[:128], axis=0),
            jnp.sum(grad_normed_two, axis=0),
            jnp.sum(grad_residual, axis=0),
            jnp.sum(cot_own, axis=0),
            jnp.sum(grad_hidden, axis=0),
        ]
        + [jnp.zeros((768,), F32)] * 11
    )
    local = jnp.concatenate(
        [
            jnp.concatenate([grad_out_w, grad_fc_w], axis=1)
            .reshape(2, 16, 48, 768)
            .transpose(1, 0, 2, 3)
            .reshape(16, 96, 768),
            grad_proj_w.reshape(16, 12, 768),
            extra[:, None],
            jnp.zeros((16, 3, 768), F32),
        ],
        axis=1,
    )
    local, do_all, out_partial = lax.optimization_barrier((local, do_all, out_partial))
    early = lax.psum_scatter(local, SEQ_AXES, scatter_dimension=0, tiled=False)
    out_moved = [to_rank(out_partial[r], r) for r in (1, 2, 3)]

    grad_kv, grad_kv_sum = key_grad(pos, kv_own, q_all, do_all)
    out_moved = after(tuple(out_moved), grad_kv)
    output = (
        out_partial[0] + out_moved[0] + out_moved[1] + out_moved[2] + out_bias + residual[:128]
    ).astype(BF16)

    late_local, partial_one = first_grads(
        normed_one_t, x_normed, grad_q, grad_kv, w_cols, grad_q_sum, grad_kv_sum
    )
    late = reduce_by_permute(late_local)

    early, late, partial_one = lax.optimization_barrier((early, late, partial_one))
    late = jnp.concatenate([late, jnp.zeros((56, 128), F32)], axis=1)

    def rows_of(which):
        return jnp.concatenate(
            [
                lax.dynamic_slice_in_dim(early, 48 * which, 48, 0),
                lax.dynamic_slice_in_dim(late, 24 * which, 24, 0),
                late[48:],
                early[96:],
            ],
            axis=0,
        )

    totals = (rows_of(fs) + swap(rows_of(1 - fs), "fsdp")).astype(BF16)
    totals = jnp.stack(gather_ranks(totals))
    totals = lax.all_gather(totals, SEQ_AXES, axis=0, tiled=False)
    grad_normed_one = sum_ranks(partial_one)
    input_grad = (
        norm_back(grad_normed_one, x_normed[:128], x_scale[:128], gain_one) + grad_residual
    )
    totals, input_grad, output = lax.optimization_barrier((totals, input_grad, output))
    g_w_out, g_w_fc, g_w_qkv, extra = unpack(jnp.stack([rank]).astype(jnp.int32), totals)

    def own_half(values):
        return lax.dynamic_slice_in_dim(values, 384 * fs, 384, 0)

    early = extra[:, :, 8:]
    late_rows = extra[:4, :, 0, :640]
    g_w_proj = lax.dynamic_slice_in_dim(early[:, :, :12], 2 * fs, 2, 1)
    g_w_proj = g_w_proj.transpose(1, 0, 2, 3).reshape(384, 768)
    sums = jnp.sum(early[:4, :, 12], axis=1)
    g_b_fc = pick(early[4, :, 12].reshape(4, 2, 384), fs, 1).reshape(1536)
    bias_row = late_rows[0]
    g_q_bias = own_half(bias_row[:, :192].reshape(768))
    g_v_bias = own_half(
        jnp.concatenate([bias_row[:, 512:], bias_row[:, 448:512]], axis=1).reshape(768)
    )
    ln_one = jnp.sum(late_rows[1:], axis=1).reshape(1920)
    return (
        output[None],
        input_grad[None],
        own_half(ln_one[:768]),
        own_half(ln_one[768:1536]),
        g_w_qkv,
        g_q_bias,
        g_v_bias,
        g_w_proj,
        own_half(sums[2]),
        own_half(sums[0]),
        own_half(sums[1]),
        g_w_fc,
        g_b_fc,
        g_w_out,
        own_half(sums[3]),
    )


def solution(mesh):
    split = Mesh(
        mesh.devices.reshape(2, 2, 2, 2, 2, 2, 2),
        ("zl", "xh", "xl", "yh", "yl", "core", "fsdp"),
    )
    tokens = P("fsdp", CTX, None)
    vector = P("fsdp")
    matrix = P("fsdp", None)
    in_specs = (
        tokens,
        tokens,
        vector,
        vector,
        matrix,
        vector,
        vector,
        matrix,
        vector,
        vector,
        vector,
        matrix,
        vector,
        matrix,
        vector,
    )
    out_specs = (
        tokens,
        tokens,
        vector,
        vector,
        matrix,
        vector,
        vector,
        matrix,
        vector,
        vector,
        vector,
        matrix,
        vector,
        matrix,
        vector,
    )
    return jax.shard_map(body, mesh=split, in_specs=in_specs, out_specs=out_specs, check_vma=False)
```

```python
import jax
import jax.numpy as jnp
from jax import lax
from jax.experimental import pallas as pl
from jax.experimental.pallas import tpu as pltpu
from jax.sharding import Mesh, PartitionSpec as P

TP = ("zl", "xh")
SEQ_AXES = ("xl", "yh", "yl", "core")
BLOCKS = ("xl", "yh", "yl")
CTX = TP + SEQ_AXES
EPS = 1e-05
GELU_F = 0.7978845608028654
GELU_C = 0.044715
NEG = -1e30
F32 = jnp.float32
BF16 = jnp.bfloat16
NT = (((1,), (1,)), ((), ()))
VMEM_LIMIT = 56 * 1024 * 1024


def lane_half(shape):
    return lax.broadcasted_iota(jnp.int32, shape, len(shape) - 1) >= 64


def slot_only(values, slot):
    lane = lax.broadcasted_iota(jnp.int32, values.shape, 1)
    keep = jnp.logical_and(lane >= 64 * slot, lane < 64 * slot + 64)
    return jnp.where(keep, values, jnp.zeros_like(values))


def wide(values):
    return jnp.concatenate([values] * 4, axis=1)


def pieces(values):
    high = values.astype(BF16)
    rest = values - high.astype(F32)
    middle = rest.astype(BF16)
    low = (rest - middle.astype(F32)).astype(BF16)
    return (high, middle, low)


def chunk_rows(ref, rank, chunk):
    rows = ref[pl.ds(4 * lax.rem(chunk, 4), 4), rank ^ (chunk // 4)]
    return rows.reshape(512, rows.shape[-1])


def causal(scores, first_query, first_key, keys_in_rows):
    rows = lax.broadcasted_iota(jnp.int32, (128, 512), 0)
    cols = lax.broadcasted_iota(jnp.int32, (128, 512), 1)
    if keys_in_rows:
        allowed = first_key + rows <= first_query + cols
    else:
        allowed = first_key + cols <= first_query + rows
    return jnp.concatenate(
        [jnp.where(allowed, scores[128 * h : 128 * h + 128], NEG) for h in range(3)], axis=0
    )


def value_halves(product):
    return jnp.concatenate([product[:256, 128:], product[256:, :128]], axis=0)


def row_halves(product):
    return jnp.concatenate([product[:256, :128], product[256:, 128:]], axis=0)


def forward_kernel(pos_ref, q_ref, kv_ref, attn_ref, lse_ref, m_ref, l_ref, acc_ref):
    seq = pos_ref[0]
    rank = pos_ref[1]

    def tile(k, carry):
        slot = rank ^ k
        block = k * 16 + seq
        q_rows = q_ref[slot]
        queries = jnp.concatenate([slot_only(q_rows, h) for h in range(3)], axis=0)
        m_ref[...] = jnp.full(m_ref.shape, NEG, F32)
        l_ref[...] = jnp.zeros(l_ref.shape, F32)
        acc_ref[...] = jnp.zeros(acc_ref.shape, F32)

        def step(chunk, masked):
            kv = chunk_rows(kv_ref, rank, chunk)
            scores = lax.dot_general(queries, kv[:, :256], NT, preferred_element_type=F32)
            if masked:
                scores = causal(scores, block * 128, chunk * 512, False)
            before = m_ref[...]
            after = jnp.maximum(before, jnp.max(scores, axis=1, keepdims=True))
            weights = jnp.exp(scores - wide(after))
            factor = jnp.exp(before - after)
            m_ref[...] = after
            partial = (weights[:, :128] + weights[:, 128:256]) + (
                weights[:, 256:384] + weights[:, 384:]
            )
            l_ref[...] = l_ref[...] * factor + partial
            acc_ref[...] = acc_ref[...] * factor + value_halves(
                jnp.dot(weights.astype(BF16), kv[:, 128:], preferred_element_type=F32)
            )

        last = block // 4

        def full(chunk, inner):
            step(chunk, False)
            return inner

        lax.fori_loop(0, last, full, 0)
        step(last, True)
        lane = lax.broadcasted_iota(jnp.int32, (128, 128), 1)
        total = jnp.sum(l_ref[...], axis=1, keepdims=True)
        log_sum = m_ref[...] + jnp.log(total)
        lse_ref[slot] = log_sum
        outs = acc_ref[...] / total
        attn_ref[slot, :, :128] = jnp.where(lane < 64, outs[:128], outs[128:256]).astype(BF16)
        attn_ref[slot, :, 128:] = jnp.where(lane < 64, 0.0, outs[256:]).astype(BF16)
        return carry

    lax.fori_loop(0, 4, tile, 0)


def vmem_spec():
    return pl.BlockSpec(memory_space=pltpu.VMEM)


def forward_attention(pos, q, kv):
    return pl.pallas_call(
        forward_kernel,
        out_shape=(
            jax.ShapeDtypeStruct((4, 128, 256), BF16),
            jax.ShapeDtypeStruct((4, 384, 128), F32),
        ),
        in_specs=[pl.BlockSpec(memory_space=pltpu.SMEM), vmem_spec(), vmem_spec()],
        out_specs=(vmem_spec(), vmem_spec()),
        scratch_shapes=[pltpu.VMEM((384, 128), F32)] * 3,
        compiler_params=pltpu.CompilerParams(vmem_limit_bytes=VMEM_LIMIT),
        cost_estimate=pl.CostEstimate(
            flops=3 * 512 * 4096 * 512, transcendentals=3 * 512 * 4096, bytes_accessed=8 * 2**20
        ),
        name="attention_forward",
    )(pos, q, kv)


def grad_rows_kernel(dr_ref, w_ref, attn_ref, lse_ref, do_ref, delta_ref):
    lane = lax.broadcasted_iota(jnp.int32, (512, 128), 1)
    grads = lax.dot_general(dr_ref[...], w_ref[...], NT, preferred_element_type=F32).astype(BF16)
    attn = attn_ref[...].reshape(512, 256).astype(F32)
    product = grads.astype(F32) * attn
    extra = jnp.zeros((512, 128), BF16)
    for h, run in enumerate((0, 1, 3)):
        delta = jnp.sum(slot_only(product, run), axis=1, keepdims=True)
        delta = jnp.broadcast_to(delta, (512, 128))
        for k in range(4):
            delta_ref[k, 128 * h : 128 * h + 128] = delta[128 * k : 128 * k + 128]
        log_sum = jnp.concatenate([lse_ref[k, 128 * h : 128 * h + 128] for k in range(4)], axis=0)
        for p, (piece, other) in enumerate(zip(pieces(-delta), pieces(-log_sum))):
            extra = jnp.where(lane == 3 * h + p, piece, extra)
            extra = jnp.where(lane == 16 + 3 * h + p, other, extra)
    do_ref[:, :, :128] = grads[:, :128].reshape(4, 128, 128)
    do_ref[:, :, 128:] = jnp.where(lane < 64, extra, grads[:, 128:]).reshape(4, 128, 128)


def grad_rows(dr_low, w_rows, attn, lse):
    return pl.pallas_call(
        grad_rows_kernel,
        out_shape=(
            jax.ShapeDtypeStruct((4, 128, 256), BF16),
            jax.ShapeDtypeStruct((4, 384, 128), F32),
        ),
        in_specs=[vmem_spec()] * 4,
        out_specs=(vmem_spec(), vmem_spec()),
        compiler_params=pltpu.CompilerParams(vmem_limit_bytes=VMEM_LIMIT),
        name="attention_grad_rows",
    )(dr_low, w_rows, attn, lse)


def query_grad_kernel(
    pos_ref, q_ref, do_ref, lse_ref, delta_ref, kv_ref, dq_ref, sum_ref, acc_ref
):
    seq = pos_ref[0]
    rank = pos_ref[1]

    def tile(k, carry):
        slot = rank ^ k
        block = k * 16 + seq
        q_rows = q_ref[slot]
        do_rows = do_ref[slot]
        queries = jnp.concatenate([slot_only(q_rows, h) for h in range(3)], axis=0)
        turned = jnp.concatenate([do_rows[:, 128:], do_rows[:, :128]], axis=1)
        grads = jnp.concatenate([slot_only(turned, run) for run in (2, 3, 1)], axis=0)
        acc_ref[...] = jnp.zeros(acc_ref.shape, F32)

        def step(chunk, masked):
            kv = chunk_rows(kv_ref, rank, chunk)
            scores = lax.dot_general(queries, kv[:, :256], NT, preferred_element_type=F32)
            scores = scores - wide(lse_ref[slot])
            if masked:
                scores = causal(scores, block * 128, chunk * 512, False)
            weights = jnp.exp(scores)
            grad_weights = lax.dot_general(grads, kv[:, 128:], NT, preferred_element_type=F32)
            grad_scores = (weights * (grad_weights - wide(delta_ref[slot]))).astype(BF16)
            acc_ref[...] += row_halves(
                jnp.dot(grad_scores, kv[:, :256], preferred_element_type=F32)
            )

        last = block // 4

        def full(chunk, inner):
            step(chunk, False)
            return inner

        lax.fori_loop(0, last, full, 0)
        step(last, True)
        lane = lax.broadcasted_iota(jnp.int32, (128, 128), 1)
        acc = acc_ref[...] * 0.125
        rows = jnp.concatenate(
            [
                jnp.where(lane < 64, acc[:128], acc[128:256]),
                jnp.where(lane < 64, acc[256:], 0.0),
            ],
            axis=1,
        )
        dq_ref[slot] = rows.astype(BF16)
        return carry + jnp.sum(rows, axis=0, keepdims=True)

    sum_ref[...] = lax.fori_loop(0, 4, tile, jnp.zeros((1, 256), F32))


def query_grad(pos, q, do, lse, delta, kv):
    return pl.pallas_call(
        query_grad_kernel,
        out_shape=(
            jax.ShapeDtypeStruct((4, 128, 256), BF16),
            jax.ShapeDtypeStruct((1, 256), F32),
        ),
        in_specs=[pl.BlockSpec(memory_space=pltpu.SMEM)] + [vmem_spec()] * 5,
        out_specs=(vmem_spec(), vmem_spec()),
        scratch_shapes=[pltpu.VMEM((384, 128), F32)],
        compiler_params=pltpu.CompilerParams(vmem_limit_bytes=VMEM_LIMIT),
        cost_estimate=pl.CostEstimate(
            flops=3 * 512 * 4096 * 768, transcendentals=3 * 512 * 4096, bytes_accessed=8 * 2**20
        ),
        name="attention_query_grad",
    )(pos, q, do, lse, delta, kv)


def key_grad_kernel(
    pos_ref, kv_ref, qg_ref, dog_ref, dkv_ref, sum_ref, dk_ref, dv_ref, join_ref
):
    seq = pos_ref[0]
    rank = pos_ref[1]

    def join(chunk, carry):
        q_rows = chunk_rows(qg_ref, rank, chunk)[:, 128:]
        do_rows = chunk_rows(dog_ref, rank, chunk)[:, 128:]
        join_ref[chunk] = jnp.concatenate([q_rows[:, :64], do_rows[:, :64]], axis=1)
        return carry

    lax.fori_loop(seq // 4, 16, join, 0)

    def tile(k, carry):
        slot = rank ^ k
        block = k * 16 + seq
        rows = kv_ref[slot]
        lane = lax.broadcasted_iota(jnp.int32, (128, 256), 1)
        key_rows = rows[:, :256]
        value_rows = jnp.concatenate([rows[:, 256:], rows[:, 128:256]], axis=1)
        keys = []
        values = []
        for h, run in enumerate((0, 1, 3)):
            key_ones = jnp.logical_and(lane >= 208 + 3 * h, lane < 211 + 3 * h)
            value_ones = jnp.logical_and(lane >= 128 + 3 * h, lane < 131 + 3 * h)
            keys.append(jnp.where(key_ones, 1.0, slot_only(key_rows, h)).astype(BF16))
            values.append(jnp.where(value_ones, 1.0, slot_only(value_rows, run)).astype(BF16))
        keys = jnp.concatenate(keys, axis=0)
        values = jnp.concatenate(values, axis=0)
        dk_ref[...] = jnp.zeros(dk_ref.shape, F32)
        dv_ref[...] = jnp.zeros(dv_ref.shape, F32)

        def step(chunk, masked):
            q_rows = chunk_rows(qg_ref, rank, chunk)[:, :128]
            q_rows = jnp.concatenate([q_rows, join_ref[chunk]], axis=1)
            do_rows = chunk_rows(dog_ref, rank, chunk)
            scores = lax.dot_general(keys, q_rows, NT, preferred_element_type=F32)
            if masked:
                scores = causal(scores, chunk * 512, block * 128, True)
            weights = jnp.exp(scores)
            grad_weights = lax.dot_general(values, do_rows, NT, preferred_element_type=F32)
            grad_scores = (weights * grad_weights).astype(BF16)
            dv_ref[...] += row_halves(
                jnp.dot(weights.astype(BF16), do_rows, preferred_element_type=F32)
            )
            dk_ref[...] += row_halves(jnp.dot(grad_scores, q_rows, preferred_element_type=F32))

        first = block // 4

        def full(chunk, inner):
            step(chunk, False)
            return inner

        step(first, True)
        lax.fori_loop(first + 1, 16, full, 0)
        half = lax.broadcasted_iota(jnp.int32, (128, 128), 1) < 64
        grads = jnp.concatenate(
            [
                jnp.where(half, dk_ref[:128], dk_ref[128:256]),
                jnp.where(half, dk_ref[256:], dv_ref[256:]),
                jnp.where(half, dv_ref[:128], dv_ref[128:256]),
            ],
            axis=1,
        )
        dkv_ref[slot] = grads.astype(BF16)
        return carry + jnp.sum(grads, axis=0, keepdims=True)

    sum_ref[...] = lax.fori_loop(0, 4, tile, jnp.zeros((1, 384), F32))


def key_grad(pos, kv_own, q_all, do_all):
    return pl.pallas_call(
        key_grad_kernel,
        out_shape=(
            jax.ShapeDtypeStruct((4, 128, 384), BF16),
            jax.ShapeDtypeStruct((1, 384), F32),
        ),
        in_specs=[pl.BlockSpec(memory_space=pltpu.SMEM)] + [vmem_spec()] * 3,
        out_specs=(vmem_spec(), vmem_spec()),
        scratch_shapes=[
            pltpu.VMEM((384, 128), F32),
            pltpu.VMEM((384, 128), F32),
            pltpu.VMEM((16, 512, 128), BF16),
        ],
        compiler_params=pltpu.CompilerParams(vmem_limit_bytes=VMEM_LIMIT),
        cost_estimate=pl.CostEstimate(
            flops=3 * 512 * 4096 * 1024, transcendentals=3 * 512 * 4096, bytes_accessed=10 * 2**20
        ),
        name="attention_key_grad",
    )(pos, kv_own, q_all, do_all)


def first_grads_kernel(
    norm_ref, hat_ref, q_ref, kv_ref, w_ref, q_sum_ref, kv_sum_ref, local_ref, own_ref, other_ref
):
    cols = jnp.concatenate([q_ref[...].reshape(512, 256), kv_ref[...].reshape(512, 384)], axis=1)
    for half in range(2):
        grads = jnp.dot(
            norm_ref[384 * half : 384 * half + 384], cols, preferred_element_type=F32
        )
        for block in range(16):
            local_ref[block % 2, block // 2, 24 * half : 24 * half + 24] = grads[
                24 * block : 24 * block + 24
            ]
    gain = jnp.zeros((1, 768), F32)
    shift = jnp.zeros((1, 768), F32)
    for k in range(4):
        rows = slice(128 * k, 128 * k + 128)
        part = lax.dot_general(cols[rows], w_ref[...], NT, preferred_element_type=F32)
        if k == 0:
            own_ref[...] = part
        else:
            other_ref[k - 1] = part.astype(BF16)
        gain = gain + jnp.sum(part * hat_ref[rows], axis=0, keepdims=True)
        shift = shift + jnp.sum(part, axis=0, keepdims=True)
    extra = (
        jnp.concatenate([q_sum_ref[...], kv_sum_ref[...]], axis=1),
        gain[:, :640],
        jnp.concatenate([gain[:, 640:], shift[:, :512]], axis=1),
        jnp.concatenate([shift[:, 512:], jnp.zeros((1, 384), F32)], axis=1),
    )
    top = lax.broadcasted_iota(jnp.int32, (8, 640), 0) == 0
    for block in range(16):
        rows = jnp.zeros((8, 640), F32)
        if block < 4:
            rows = jnp.where(top, extra[block], rows)
        local_ref[block % 2, block // 2, 48:] = rows


def first_grads(norm_t, hat, dq, dkv, w_cols, q_sum, kv_sum):
    return pl.pallas_call(
        first_grads_kernel,
        out_shape=(
            jax.ShapeDtypeStruct((2, 8, 56, 640), F32),
            jax.ShapeDtypeStruct((128, 768), F32),
            jax.ShapeDtypeStruct((3, 128, 768), BF16),
        ),
        in_specs=[vmem_spec()] * 7,
        out_specs=(vmem_spec(), vmem_spec(), vmem_spec()),
        compiler_params=pltpu.CompilerParams(vmem_limit_bytes=VMEM_LIMIT),
        name="first_grads",
    )(norm_t, hat, dq, dkv, w_cols, q_sum, kv_sum)


def unpack_kernel(pos_ref, in_ref, out_w_ref, fc_w_ref, qkv_ref, proj_ref, sum_ref):
    step = pl.program_id(0)
    rank = pos_ref[0]

    @pl.when(step < 8)
    def _():
        for g in range(4):
            out_w_ref[g, 0] = in_ref[0, rank ^ g, :48].astype(F32)

    @pl.when(step >= 8)
    def _():
        for g in range(4):
            rows = in_ref[0, rank ^ g, :48].astype(F32)
            fc_w_ref[0, :, 384 * g : 384 * g + 384] = rows[:, :384]
            fc_w_ref[0, :, 1536 + 384 * g : 1920 + 384 * g] = rows[:, 384:]

    rows = [in_ref[0, rank ^ g, 48:].astype(F32) for g in range(4)]
    qkv_ref[0, :, :768] = jnp.concatenate([r[:24, :192] for r in rows], axis=1)
    qkv_ref[0, :, 768:1536] = jnp.concatenate([r[:24, 256:448] for r in rows], axis=1)
    qkv_ref[0, :, 1536:] = jnp.concatenate(
        [part for r in rows for part in (r[:24, 512:640], r[:24, 448:512])], axis=1
    )
    for g in range(2):
        proj_ref[g, 0] = in_ref[0, rank ^ (2 * pos_ref[1] + g), 80:].astype(F32)[:12]
    first = [r[24:25] for r in rows]
    second = [r[44:45] for r in rows]
    sum_ref[0] = jnp.concatenate(
        [
            (first[0] + first[1]) + (first[2] + first[3]),
            (second[0] + second[1]) + (second[2] + second[3]),
            jnp.zeros((6, 768), F32),
        ]
        + first
        + second,
        axis=0,
    )


def unpack(pos, totals):
    out_w, fc_w, qkv_w, proj_w, sums = pl.pallas_call(
        unpack_kernel,
        grid_spec=pltpu.PrefetchScalarGridSpec(
            num_scalar_prefetch=1,
            grid=(16,),
            in_specs=[pl.BlockSpec((1, 4, 96, 768), lambda s, pos: (s, 0, 0, 0))],
            out_specs=(
                pl.BlockSpec((4, 1, 48, 768), lambda s, pos: (0, jnp.minimum(s, 7), 0, 0)),
                pl.BlockSpec((1, 48, 3072), lambda s, pos: (jnp.maximum(s - 8, 0), 0, 0)),
                pl.BlockSpec((1, 24, 2304), lambda s, pos: (s, 0, 0)),
                pl.BlockSpec((2, 1, 12, 768), lambda s, pos: (0, s, 0, 0)),
                pl.BlockSpec((1, 16, 768), lambda s, pos: (s, 0, 0)),
            ),
        ),
        out_shape=(
            jax.ShapeDtypeStruct((4, 8, 48, 768), F32),
            jax.ShapeDtypeStruct((8, 48, 3072), F32),
            jax.ShapeDtypeStruct((16, 24, 2304), F32),
            jax.ShapeDtypeStruct((2, 16, 12, 768), F32),
            jax.ShapeDtypeStruct((16, 16, 768), F32),
        ),
        name="unpack_grads",
    )(pos, totals)
    return (
        out_w.reshape(1536, 768),
        fc_w.reshape(384, 3072),
        qkv_w.reshape(384, 2304),
        proj_w.reshape(384, 768),
        sums,
    )


def swap(values, axis):
    return lax.ppermute(values, axis, [(0, 1), (1, 0)])


def to_rank(values, offset):
    return lax.ppermute(values, TP, [(a, a ^ offset) for a in range(4)])


def gather_ranks(values):
    return [values] + [to_rank(values, r) for r in (1, 2, 3)]


def pick(values, index, axis=0):
    return lax.dynamic_index_in_dim(values, index, axis, keepdims=False)


def normalize(values):
    center = jnp.mean(values, axis=-1, keepdims=True)
    centered = values - center
    scale = lax.rsqrt(jnp.mean(centered * centered, axis=-1, keepdims=True) + EPS)
    return (centered * scale, scale)


def norm_back(grad, normed, scale, gain):
    grad_normed = grad * gain
    first = jnp.mean(grad_normed, axis=-1, keepdims=True)
    second = jnp.mean(grad_normed * normed, axis=-1, keepdims=True)
    return scale * (grad_normed - first - normed * second)


def dot(a, b):
    return jnp.dot(a, b, preferred_element_type=F32)


def dot_nt(a, b):
    return jnp.einsum("ab,cb->ac", a, b, preferred_element_type=F32)


def dot_tn(a, b):
    return jnp.einsum("ta,tb->ab", a, b, preferred_element_type=F32)


def both_shards(own, fs):
    peer = swap(own, "fsdp")
    first = jnp.where(fs == 0, own, peer)
    second = jnp.where(fs == 0, peer, own)
    return jnp.stack([first, second])


def fetch_by_core(own):
    core = lax.axis_index("core")
    half = own.shape[0] // 2
    part = swap(lax.dynamic_slice_in_dim(own, half * core, half, 0), "fsdp")
    return (part, swap(part, "core"))


def join_shards(own, fetched, fs):
    core = lax.axis_index("core")
    part, other = fetched
    peer = jnp.concatenate(
        [jnp.where(core == 0, part, other), jnp.where(core == 0, other, part)], axis=0
    )
    first = jnp.where(fs == 0, own, peer)
    second = jnp.where(fs == 0, peer, own)
    return jnp.stack([first, second])


def after(values, *earlier):
    return lax.optimization_barrier((values, *earlier))[0]


def to_block(values, offset):
    return lax.ppermute(values, BLOCKS, [(a, a ^ offset) for a in range(8)])


def reduce_by_permute(local):
    core = lax.axis_index("core")
    block = lax.axis_index(BLOCKS)
    pair = pick(local, core) + swap(pick(local, 1 - core), "core")
    moved = [to_block(pick(pair, block ^ r), r) for r in range(1, 8)]
    total = pick(pair, block)
    for values in moved:
        total = total + values
    return total


def body(
    block_in,
    out_grad,
    ln1_gain,
    ln1_bias,
    w_qkv,
    q_bias,
    v_bias,
    w_proj,
    b_proj,
    ln2_gain,
    ln2_bias,
    w_fc,
    b_fc,
    w_out,
    b_out,
):
    rank = lax.axis_index(TP)
    seq = lax.axis_index(SEQ_AXES)
    fs = lax.axis_index("fsdp")
    pos = jnp.stack([seq, rank]).astype(jnp.int32)

    x_low = jnp.concatenate(gather_ranks(block_in[0]), axis=0)
    w_q = lax.dynamic_slice_in_dim(w_qkv, 192 * rank, 192, 1)
    w_k = lax.dynamic_slice_in_dim(w_qkv, 768 + 192 * rank, 192, 1)
    w_v = lax.dynamic_slice_in_dim(w_qkv, 1536 + 192 * rank, 192, 1)
    qkv_shard = jnp.concatenate(
        [w_q, jnp.zeros((384, 64), BF16), w_k, w_v[:, 128:], w_v[:, :128]], axis=1
    )
    w_cols = both_shards(qkv_shard, fs).reshape(768, 640)
    vectors = (ln1_gain, ln1_bias, q_bias, v_bias, b_proj, ln2_gain, ln2_bias, b_out, b_fc)
    vectors = lax.optimization_barrier((qkv_shard,) + vectors)[1:]
    small = jnp.stack([v.astype(F32) for v in vectors[:8]])
    small = jnp.concatenate([small, vectors[8].astype(F32).reshape(4, 384)], axis=0)
    small = both_shards(small, fs)
    wide_vectors = small[:, :8].transpose(1, 0, 2).reshape(8, 768)
    gain_one, shift_one, query_bias, value_bias = wide_vectors[:4]
    proj_bias, gain_two, shift_two, out_bias = wide_vectors[4:]
    fc_bias = pick(small[:, 8:], rank, 1).reshape(768)
    q_own = lax.dynamic_slice_in_dim(query_bias, 192 * rank, 192, 0)
    v_own = lax.dynamic_slice_in_dim(value_bias, 192 * rank, 192, 0)
    qkv_bias = jnp.concatenate(
        [q_own, jnp.zeros((64 + 192,), F32), v_own[128:], v_own[:128]], axis=0
    )
    fc_shard = jnp.concatenate(
        [
            lax.dynamic_slice_in_dim(w_fc, 384 * rank, 384, 1),
            lax.dynamic_slice_in_dim(w_fc, 1536 + 384 * rank, 384, 1),
        ],
        axis=1,
    )
    out_shard = lax.dynamic_slice_in_dim(w_out, 384 * rank, 384, 0)
    fetched = (fetch_by_core(w_proj), fetch_by_core(fc_shard), fetch_by_core(out_shard))

    x = x_low.astype(F32)
    x_normed, x_scale = normalize(x)
    normed_one = (x_normed * gain_one + shift_one).astype(BF16)
    projected = dot(normed_one, w_cols) + qkv_bias
    q_scaled = (projected[:, :256].astype(BF16) * 0.125).astype(BF16).reshape(4, 128, 256)
    kv_own = projected[:, 256:].astype(BF16).reshape(4, 128, 384)
    kv_all = lax.all_gather(kv_own, SEQ_AXES, axis=0, tiled=False)
    q_all = lax.all_gather(after(q_scaled, kv_all), SEQ_AXES, axis=0, tiled=False)
    normed_one_t = normed_one.T
    cot_ranks = tuple(gather_ranks(out_grad[0]))
    kv_all, fetched, cot_ranks, normed_one_t = lax.optimization_barrier(
        (kv_all, fetched, cot_ranks, normed_one_t)
    )
    attn, lse = forward_attention(pos, q_scaled, kv_all)

    attn_ranks = gather_ranks(attn)
    proj_rows = join_shards(w_proj, fetched[0], fs).reshape(4, 3, 64, 768)
    proj_rows = jnp.concatenate(
        [proj_rows[:, :2], jnp.zeros((4, 1, 64, 768), BF16), proj_rows[:, 2:]], axis=1
    ).reshape(4, 256, 768)
    proj_ranks = jnp.stack([pick(proj_rows, rank ^ r) for r in range(4)])
    fc_cols = join_shards(fc_shard, fetched[1], fs).reshape(768, 768)
    out_rows = join_shards(out_shard, fetched[2], fs).reshape(768, 768)
    cot_low = jnp.concatenate(cot_ranks, axis=0)
    residual = x + proj_bias
    attn_full = jnp.concatenate(
        [
            jnp.concatenate([attn_ranks[r][k ^ r] for k in range(4)], axis=0) for r in range(4)
        ],
        axis=1,
    )
    residual = residual + dot(attn_full, proj_ranks.reshape(1024, 768))

    r_normed, r_scale = normalize(residual)
    normed_two = (r_normed * gain_two + shift_two).astype(BF16)
    hidden = dot(normed_two, fc_cols) + fc_bias
    grad_act = dot_nt(cot_low, out_rows)
    inner = GELU_F * (hidden + GELU_C * hidden * hidden * hidden)
    tanh = jnp.tanh(inner)
    activated = (0.5 * hidden * (1.0 + tanh)).astype(BF16)
    slope = 0.5 * (1.0 + tanh) + 0.5 * hidden * (1.0 - tanh * tanh) * GELU_F * (
        1.0 + 3.0 * GELU_C * hidden * hidden
    )
    grad_hidden = grad_act * slope
    grad_hidden_low = grad_hidden.astype(BF16)
    partial_two = dot_nt(grad_hidden_low, fc_cols).reshape(4, 128, 768)
    moved_two = tuple(to_rank(partial_two[r], r) for r in (1, 2, 3))
    grad_out_w = dot_tn(activated, cot_low).reshape(2, 384, 768)
    grad_fc_w = dot_tn(normed_two, grad_hidden_low).reshape(2, 384, 768)
    moved_two, grad_out_w, grad_fc_w = lax.optimization_barrier(
        (moved_two, grad_out_w, grad_fc_w)
    )
    grad_normed_two = partial_two[0] + moved_two[0] + moved_two[1] + moved_two[2]

    cot_own = out_grad[0].astype(F32)
    grad_residual = (
        norm_back(grad_normed_two, r_normed[:128], r_scale[:128], gain_two) + cot_own
    )
    residual_ranks = tuple(gather_ranks(grad_residual.astype(BF16)))
    local = jnp.pad(
        jnp.concatenate([grad_out_w, grad_fc_w], axis=1)
        .reshape(2, 16, 48, 768)
        .transpose(1, 0, 2, 3)
        .reshape(16, 96, 768),
        ((0, 0), (0, 16), (0, 0)),
    )
    residual_ranks, local = lax.optimization_barrier((residual_ranks, local))
    grad_residual_low = jnp.concatenate(residual_ranks, axis=0)
    do_aug, delta = grad_rows(grad_residual_low, proj_ranks[0], attn, lse)
    do_all = lax.all_gather(after(do_aug, q_all), SEQ_AXES, axis=0, tiled=False)
    grad_q, grad_q_sum = query_grad(pos, q_scaled, do_aug, lse, delta, kv_all)

    (
        activated,
        attn_late,
        grad_q,
        grad_normed_two,
        grad_residual,
        grad_hidden,
        cot_own,
    ) = lax.optimization_barrier(
        (activated, attn, grad_q, grad_normed_two, grad_residual, grad_hidden, cot_own)
    )
    out_partial = dot(activated, out_rows).reshape(4, 128, 768)
    grad_proj_w = dot_tn(attn_late.reshape(512, 256), grad_residual_low)
    grad_proj_w = jnp.concatenate([grad_proj_w[:128], grad_proj_w[192:]], axis=0)
    extra = jnp.stack(
        [
            jnp.sum(grad_normed_two * r_normed[:128], axis=0),
            jnp.sum(grad_normed_two, axis=0),
            jnp.sum(grad_residual, axis=0),
            jnp.sum(cot_own, axis=0),
            jnp.sum(grad_hidden, axis=0),
        ]
        + [jnp.zeros((768,), F32)] * 11
    )
    shared = jnp.concatenate(
        [grad_proj_w.reshape(16, 12, 768), extra[:, None], jnp.zeros((16, 3, 768), F32)], axis=1
    )
    local = lax.dynamic_update_slice(local, shared, (0, 96, 0))
    out_low = out_partial[1:].astype(BF16)
    out_low = (None,) + tuple(out_low)
    local, do_all, out_low = lax.optimization_barrier((local, do_all, out_low))
    early = lax.psum_scatter(local, SEQ_AXES, scatter_dimension=0, tiled=False)
    out_moved = tuple(to_rank(out_low[r], r) for r in (1, 2, 3))

    grad_kv, grad_kv_sum = key_grad(pos, kv_own, q_all, do_all)
    grad_kv, out_moved = lax.optimization_barrier((grad_kv, out_moved))
    late_local, partial_one, partial_low = first_grads(
        normed_one_t, x_normed, grad_q, grad_kv, w_cols, grad_q_sum, grad_kv_sum
    )
    late = reduce_by_permute(late_local)
    low_one, late = lax.optimization_barrier((partial_low, late))
    one_moved = tuple(to_rank(low_one[r - 1], r) for r in (1, 2, 3))

    early, late, one_moved = lax.optimization_barrier((early, late, one_moved))
    late = jnp.concatenate([late, jnp.zeros((56, 128), F32)], axis=1)

    def rows_of(which):
        return jnp.concatenate(
            [
                lax.dynamic_slice_in_dim(early, 48 * which, 48, 0),
                lax.dynamic_slice_in_dim(late, 24 * which, 24, 0),
                late[48:],
                early[96:],
            ],
            axis=0,
        )

    totals = (rows_of(fs) + swap(rows_of(1 - fs), "fsdp")).astype(BF16)
    totals = jnp.stack(gather_ranks(totals))
    totals = lax.all_gather(totals, SEQ_AXES, axis=0, tiled=False)
    output = (
        out_partial[0]
        + out_moved[0].astype(F32)
        + out_moved[1].astype(F32)
        + out_moved[2].astype(F32)
        + out_bias
        + residual[:128]
    ).astype(BF16)
    grad_normed_one = (
        partial_one
        + one_moved[0].astype(F32)
        + one_moved[1].astype(F32)
        + one_moved[2].astype(F32)
    )
    input_grad = (
        norm_back(grad_normed_one, x_normed[:128], x_scale[:128], gain_one) + grad_residual
    )
    totals, input_grad, output = lax.optimization_barrier((totals, input_grad, output))
    g_w_out, g_w_fc, g_w_qkv, g_w_proj, sums = unpack(
        jnp.stack([rank, fs]).astype(jnp.int32), totals
    )

    def own_half(values):
        return lax.dynamic_slice_in_dim(values, 384 * fs, 384, values.ndim - 1)

    mlp_sums = own_half(sums[:4, 1])
    g_b_fc = pick(sums[4, 12:].reshape(4, 2, 384), fs, 1).reshape(1536)
    bias_row = sums[0, 8:12]
    g_q_bias = own_half(bias_row[:, :192].reshape(768))
    g_v_bias = own_half(
        jnp.concatenate([bias_row[:, 512:640], bias_row[:, 448:512]], axis=1).reshape(768)
    )
    ln_one = own_half(sums[1:4, 0, :640].reshape(1920)[:1536].reshape(2, 768))
    return (
        output[None],
        input_grad[None],
        ln_one[0],
        ln_one[1],
        g_w_qkv,
        g_q_bias,
        g_v_bias,
        g_w_proj,
        mlp_sums[2],
        mlp_sums[0],
        mlp_sums[1],
        g_w_fc,
        g_b_fc,
        g_w_out,
        mlp_sums[3],
    )


def solution(mesh):
    split = Mesh(
        mesh.devices.reshape(2, 2, 2, 2, 2, 2, 2),
        ("zl", "xh", "xl", "yh", "yl", "core", "fsdp"),
    )
    tokens = P("fsdp", CTX, None)
    vector = P("fsdp")
    matrix = P("fsdp", None)
    in_specs = (
        tokens,
        tokens,
        vector,
        vector,
        matrix,
        vector,
        vector,
        matrix,
        vector,
        vector,
        vector,
        matrix,
        vector,
        matrix,
        vector,
    )
    out_specs = (
        tokens,
        tokens,
        vector,
        vector,
        matrix,
        vector,
        vector,
        matrix,
        vector,
        vector,
        vector,
        matrix,
        vector,
        matrix,
        vector,
    )
    return jax.shard_map(body, mesh=split, in_specs=in_specs, out_specs=out_specs, check_vma=False)
```

```python
import jax
import jax.numpy as jnp
from jax import lax
from jax.experimental import pallas as pl
from jax.experimental.pallas import tpu as pltpu
from jax.sharding import Mesh, PartitionSpec as P

TP = ("zl", "xh")
SEQ_AXES = ("xl", "yh", "yl", "core")
BLOCKS = ("xl", "yh", "yl")
CTX = TP + SEQ_AXES
EPS = 1e-05
GELU_F = 0.7978845608028654
GELU_C = 0.044715
NEG = -1e30
F32 = jnp.float32
BF16 = jnp.bfloat16
NT = (((1,), (1,)), ((), ()))
VMEM_LIMIT = 56 * 1024 * 1024


def lane_half(shape):
    return lax.broadcasted_iota(jnp.int32, shape, len(shape) - 1) >= 64


def slot_only(values, slot):
    lane = lax.broadcasted_iota(jnp.int32, values.shape, 1)
    keep = jnp.logical_and(lane >= 64 * slot, lane < 64 * slot + 64)
    return jnp.where(keep, values, jnp.zeros_like(values))


def wide(values):
    return jnp.concatenate([values] * 4, axis=1)


def pieces(values):
    high = values.astype(BF16)
    rest = values - high.astype(F32)
    middle = rest.astype(BF16)
    low = (rest - middle.astype(F32)).astype(BF16)
    return (high, middle, low)


def chunk_rows(ref, rank, chunk):
    rows = ref[pl.ds(4 * lax.rem(chunk, 4), 4), rank ^ (chunk // 4)]
    return rows.reshape(512, rows.shape[-1])


def causal(scores, first_query, first_key, keys_in_rows):
    rows = lax.broadcasted_iota(jnp.int32, (128, 512), 0)
    cols = lax.broadcasted_iota(jnp.int32, (128, 512), 1)
    if keys_in_rows:
        allowed = first_key + rows <= first_query + cols
    else:
        allowed = first_key + cols <= first_query + rows
    return jnp.concatenate(
        [jnp.where(allowed, scores[128 * h : 128 * h + 128], NEG) for h in range(3)], axis=0
    )


def value_halves(product):
    return jnp.concatenate([product[:256, 128:], product[256:, :128]], axis=0)


def row_halves(product):
    return jnp.concatenate([product[:256, :128], product[256:, 128:]], axis=0)


def forward_kernel(pos_ref, q_ref, kv_ref, attn_ref, lse_ref, m_ref, l_ref, acc_ref):
    seq = pos_ref[0]
    rank = pos_ref[1]

    def tile(k, carry):
        slot = rank ^ k
        block = k * 16 + seq
        q_rows = q_ref[slot]
        queries = jnp.concatenate([slot_only(q_rows, h) for h in range(3)], axis=0)
        m_ref[...] = jnp.full(m_ref.shape, NEG, F32)
        l_ref[...] = jnp.zeros(l_ref.shape, F32)
        acc_ref[...] = jnp.zeros(acc_ref.shape, F32)

        def step(chunk, masked):
            kv = chunk_rows(kv_ref, rank, chunk)
            scores = lax.dot_general(queries, kv[:, :256], NT, preferred_element_type=F32)
            if masked:
                scores = causal(scores, block * 128, chunk * 512, False)
            before = m_ref[...]
            after = jnp.maximum(before, jnp.max(scores, axis=1, keepdims=True))
            weights = jnp.exp(scores - wide(after))
            factor = jnp.exp(before - after)
            m_ref[...] = after
            partial = (weights[:, :128] + weights[:, 128:256]) + (
                weights[:, 256:384] + weights[:, 384:]
            )
            l_ref[...] = l_ref[...] * factor + partial
            acc_ref[...] = acc_ref[...] * factor + value_halves(
                jnp.dot(weights.astype(BF16), kv[:, 128:], preferred_element_type=F32)
            )

        last = block // 4

        def full(chunk, inner):
            step(chunk, False)
            return inner

        lax.fori_loop(0, last, full, 0)
        step(last, True)
        lane = lax.broadcasted_iota(jnp.int32, (128, 128), 1)
        total = jnp.sum(l_ref[...], axis=1, keepdims=True)
        log_sum = m_ref[...] + jnp.log(total)
        lse_ref[slot] = log_sum
        outs = acc_ref[...] / total
        attn_ref[slot, :, :128] = jnp.where(lane < 64, outs[:128], outs[128:256]).astype(BF16)
        attn_ref[slot, :, 128:] = jnp.where(lane < 64, 0.0, outs[256:]).astype(BF16)
        return carry

    lax.fori_loop(0, 4, tile, 0)


def vmem_spec():
    return pl.BlockSpec(memory_space=pltpu.VMEM)


def forward_attention(pos, q, kv):
    return pl.pallas_call(
        forward_kernel,
        out_shape=(
            jax.ShapeDtypeStruct((4, 128, 256), BF16),
            jax.ShapeDtypeStruct((4, 384, 128), F32),
        ),
        in_specs=[pl.BlockSpec(memory_space=pltpu.SMEM), vmem_spec(), vmem_spec()],
        out_specs=(vmem_spec(), vmem_spec()),
        scratch_shapes=[pltpu.VMEM((384, 128), F32)] * 3,
        compiler_params=pltpu.CompilerParams(vmem_limit_bytes=VMEM_LIMIT),
        cost_estimate=pl.CostEstimate(
            flops=3 * 512 * 4096 * 512, transcendentals=3 * 512 * 4096, bytes_accessed=8 * 2**20
        ),
        name="attention_forward",
    )(pos, q, kv)


def grad_rows_kernel(dr_ref, w_ref, attn_ref, lse_ref, do_ref, delta_ref):
    lane = lax.broadcasted_iota(jnp.int32, (512, 128), 1)
    grads = lax.dot_general(dr_ref[...], w_ref[...], NT, preferred_element_type=F32).astype(BF16)
    attn = attn_ref[...].reshape(512, 256).astype(F32)
    product = grads.astype(F32) * attn
    extra = jnp.zeros((512, 128), BF16)
    for h, run in enumerate((0, 1, 3)):
        delta = jnp.sum(slot_only(product, run), axis=1, keepdims=True)
        delta = jnp.broadcast_to(delta, (512, 128))
        for k in range(4):
            delta_ref[k, 128 * h : 128 * h + 128] = delta[128 * k : 128 * k + 128]
        log_sum = jnp.concatenate([lse_ref[k, 128 * h : 128 * h + 128] for k in range(4)], axis=0)
        for p, (piece, other) in enumerate(zip(pieces(-delta), pieces(-log_sum))):
            extra = jnp.where(lane == 3 * h + p, piece, extra)
            extra = jnp.where(lane == 16 + 3 * h + p, other, extra)
    do_ref[:, :, :128] = grads[:, :128].reshape(4, 128, 128)
    do_ref[:, :, 128:] = jnp.where(lane < 64, extra, grads[:, 128:]).reshape(4, 128, 128)


def grad_rows(dr_low, w_rows, attn, lse):
    return pl.pallas_call(
        grad_rows_kernel,
        out_shape=(
            jax.ShapeDtypeStruct((4, 128, 256), BF16),
            jax.ShapeDtypeStruct((4, 384, 128), F32),
        ),
        in_specs=[vmem_spec()] * 4,
        out_specs=(vmem_spec(), vmem_spec()),
        compiler_params=pltpu.CompilerParams(vmem_limit_bytes=VMEM_LIMIT),
        name="attention_grad_rows",
    )(dr_low, w_rows, attn, lse)


def query_grad_kernel(
    pos_ref, q_ref, do_ref, lse_ref, delta_ref, kv_ref, dq_ref, sum_ref, acc_ref
):
    seq = pos_ref[0]
    rank = pos_ref[1]

    def tile(k, carry):
        slot = rank ^ k
        block = k * 16 + seq
        q_rows = q_ref[slot]
        do_rows = do_ref[slot]
        queries = jnp.concatenate([slot_only(q_rows, h) for h in range(3)], axis=0)
        turned = jnp.concatenate([do_rows[:, 128:], do_rows[:, :128]], axis=1)
        grads = jnp.concatenate([slot_only(turned, run) for run in (2, 3, 1)], axis=0)
        acc_ref[...] = jnp.zeros(acc_ref.shape, F32)

        def step(chunk, masked):
            kv = chunk_rows(kv_ref, rank, chunk)
            scores = lax.dot_general(queries, kv[:, :256], NT, preferred_element_type=F32)
            scores = scores - wide(lse_ref[slot])
            if masked:
                scores = causal(scores, block * 128, chunk * 512, False)
            weights = jnp.exp(scores)
            grad_weights = lax.dot_general(grads, kv[:, 128:], NT, preferred_element_type=F32)
            grad_scores = (weights * (grad_weights - wide(delta_ref[slot]))).astype(BF16)
            acc_ref[...] += row_halves(
                jnp.dot(grad_scores, kv[:, :256], preferred_element_type=F32)
            )

        last = block // 4

        def full(chunk, inner):
            step(chunk, False)
            return inner

        lax.fori_loop(0, last, full, 0)
        step(last, True)
        lane = lax.broadcasted_iota(jnp.int32, (128, 128), 1)
        acc = acc_ref[...] * 0.125
        rows = jnp.concatenate(
            [
                jnp.where(lane < 64, acc[:128], acc[128:256]),
                jnp.where(lane < 64, acc[256:], 0.0),
            ],
            axis=1,
        )
        dq_ref[slot] = rows.astype(BF16)
        return carry + jnp.sum(rows, axis=0, keepdims=True)

    sum_ref[...] = lax.fori_loop(0, 4, tile, jnp.zeros((1, 256), F32))


def query_grad(pos, q, do, lse, delta, kv):
    return pl.pallas_call(
        query_grad_kernel,
        out_shape=(
            jax.ShapeDtypeStruct((4, 128, 256), BF16),
            jax.ShapeDtypeStruct((1, 256), F32),
        ),
        in_specs=[pl.BlockSpec(memory_space=pltpu.SMEM)] + [vmem_spec()] * 5,
        out_specs=(vmem_spec(), vmem_spec()),
        scratch_shapes=[pltpu.VMEM((384, 128), F32)],
        compiler_params=pltpu.CompilerParams(vmem_limit_bytes=VMEM_LIMIT),
        cost_estimate=pl.CostEstimate(
            flops=3 * 512 * 4096 * 768, transcendentals=3 * 512 * 4096, bytes_accessed=8 * 2**20
        ),
        name="attention_query_grad",
    )(pos, q, do, lse, delta, kv)


def key_grad_kernel(
    pos_ref, kv_ref, qg_ref, dog_ref, dkv_ref, sum_ref, dk_ref, dv_ref, join_ref
):
    seq = pos_ref[0]
    rank = pos_ref[1]

    def join(chunk, carry):
        q_rows = chunk_rows(qg_ref, rank, chunk)[:, 128:]
        do_rows = chunk_rows(dog_ref, rank, chunk)[:, 128:]
        join_ref[chunk] = jnp.concatenate([q_rows[:, :64], do_rows[:, :64]], axis=1)
        return carry

    lax.fori_loop(seq // 4, 16, join, 0)

    def tile(k, carry):
        slot = rank ^ k
        block = k * 16 + seq
        rows = kv_ref[slot]
        lane = lax.broadcasted_iota(jnp.int32, (128, 256), 1)
        key_rows = rows[:, :256]
        value_rows = jnp.concatenate([rows[:, 256:], rows[:, 128:256]], axis=1)
        keys = []
        values = []
        for h, run in enumerate((0, 1, 3)):
            key_ones = jnp.logical_and(lane >= 208 + 3 * h, lane < 211 + 3 * h)
            value_ones = jnp.logical_and(lane >= 128 + 3 * h, lane < 131 + 3 * h)
            keys.append(jnp.where(key_ones, 1.0, slot_only(key_rows, h)).astype(BF16))
            values.append(jnp.where(value_ones, 1.0, slot_only(value_rows, run)).astype(BF16))
        keys = jnp.concatenate(keys, axis=0)
        values = jnp.concatenate(values, axis=0)
        dk_ref[...] = jnp.zeros(dk_ref.shape, F32)
        dv_ref[...] = jnp.zeros(dv_ref.shape, F32)

        def step(chunk, masked):
            q_rows = chunk_rows(qg_ref, rank, chunk)[:, :128]
            q_rows = jnp.concatenate([q_rows, join_ref[chunk]], axis=1)
            do_rows = chunk_rows(dog_ref, rank, chunk)
            scores = lax.dot_general(keys, q_rows, NT, preferred_element_type=F32)
            if masked:
                scores = causal(scores, chunk * 512, block * 128, True)
            weights = jnp.exp(scores)
            grad_weights = lax.dot_general(values, do_rows, NT, preferred_element_type=F32)
            grad_scores = (weights * grad_weights).astype(BF16)
            dv_ref[...] += row_halves(
                jnp.dot(weights.astype(BF16), do_rows, preferred_element_type=F32)
            )
            dk_ref[...] += row_halves(jnp.dot(grad_scores, q_rows, preferred_element_type=F32))

        first = block // 4

        def full(chunk, inner):
            step(chunk, False)
            return inner

        step(first, True)
        lax.fori_loop(first + 1, 16, full, 0)
        half = lax.broadcasted_iota(jnp.int32, (128, 128), 1) < 64
        grads = jnp.concatenate(
            [
                jnp.where(half, dk_ref[:128], dk_ref[128:256]),
                jnp.where(half, dk_ref[256:], dv_ref[256:]),
                jnp.where(half, dv_ref[:128], dv_ref[128:256]),
            ],
            axis=1,
        )
        dkv_ref[slot] = grads.astype(BF16)
        return carry + jnp.sum(grads, axis=0, keepdims=True)

    sum_ref[...] = lax.fori_loop(0, 4, tile, jnp.zeros((1, 384), F32))


def key_grad(pos, kv_own, q_all, do_all):
    return pl.pallas_call(
        key_grad_kernel,
        out_shape=(
            jax.ShapeDtypeStruct((4, 128, 384), BF16),
            jax.ShapeDtypeStruct((1, 384), F32),
        ),
        in_specs=[pl.BlockSpec(memory_space=pltpu.SMEM)] + [vmem_spec()] * 3,
        out_specs=(vmem_spec(), vmem_spec()),
        scratch_shapes=[
            pltpu.VMEM((384, 128), F32),
            pltpu.VMEM((384, 128), F32),
            pltpu.VMEM((16, 512, 128), BF16),
        ],
        compiler_params=pltpu.CompilerParams(vmem_limit_bytes=VMEM_LIMIT),
        cost_estimate=pl.CostEstimate(
            flops=3 * 512 * 4096 * 1024, transcendentals=3 * 512 * 4096, bytes_accessed=10 * 2**20
        ),
        name="attention_key_grad",
    )(pos, kv_own, q_all, do_all)


def first_grads_kernel(
    norm_ref, hat_ref, q_ref, kv_ref, w_ref, q_sum_ref, kv_sum_ref, local_ref, own_ref, other_ref
):
    cols = jnp.concatenate([q_ref[...].reshape(512, 256), kv_ref[...].reshape(512, 384)], axis=1)
    for half in range(2):
        grads = jnp.dot(
            norm_ref[384 * half : 384 * half + 384], cols, preferred_element_type=F32
        )
        for block in range(16):
            local_ref[block % 2, block // 2, 24 * half : 24 * half + 24] = grads[
                24 * block : 24 * block + 24
            ]
    gain = jnp.zeros((1, 768), F32)
    shift = jnp.zeros((1, 768), F32)
    for k in range(4):
        rows = slice(128 * k, 128 * k + 128)
        part = lax.dot_general(cols[rows], w_ref[...], NT, preferred_element_type=F32)
        if k == 0:
            own_ref[...] = part
        else:
            other_ref[k - 1] = part.astype(BF16)
        gain = gain + jnp.sum(part * hat_ref[rows], axis=0, keepdims=True)
        shift = shift + jnp.sum(part, axis=0, keepdims=True)
    extra = (
        jnp.concatenate([q_sum_ref[...], kv_sum_ref[...]], axis=1),
        gain[:, :640],
        jnp.concatenate([gain[:, 640:], shift[:, :512]], axis=1),
        jnp.concatenate([shift[:, 512:], jnp.zeros((1, 384), F32)], axis=1),
    )
    top = lax.broadcasted_iota(jnp.int32, (8, 640), 0) == 0
    for block in range(16):
        rows = jnp.zeros((8, 640), F32)
        if block < 4:
            rows = jnp.where(top, extra[block], rows)
        local_ref[block % 2, block // 2, 48:] = rows


def first_grads(norm_t, hat, dq, dkv, w_cols, q_sum, kv_sum):
    return pl.pallas_call(
        first_grads_kernel,
        out_shape=(
            jax.ShapeDtypeStruct((2, 8, 56, 640), F32),
            jax.ShapeDtypeStruct((128, 768), F32),
            jax.ShapeDtypeStruct((3, 128, 768), BF16),
        ),
        in_specs=[vmem_spec()] * 7,
        out_specs=(vmem_spec(), vmem_spec(), vmem_spec()),
        compiler_params=pltpu.CompilerParams(vmem_limit_bytes=VMEM_LIMIT),
        name="first_grads",
    )(norm_t, hat, dq, dkv, w_cols, q_sum, kv_sum)


def unpack_kernel(pos_ref, in_ref, out_w_ref, fc_w_ref, qkv_ref, proj_ref, sum_ref):
    step = pl.program_id(0)
    rank = pos_ref[0]

    @pl.when(step < 8)
    def _():
        for g in range(4):
            out_w_ref[g, 0] = in_ref[0, rank ^ g, :48].astype(F32)

    @pl.when(step >= 8)
    def _():
        for g in range(4):
            rows = in_ref[0, rank ^ g, :48].astype(F32)
            fc_w_ref[0, :, 384 * g : 384 * g + 384] = rows[:, :384]
            fc_w_ref[0, :, 1536 + 384 * g : 1920 + 384 * g] = rows[:, 384:]

    rows = [in_ref[0, rank ^ g, 48:].astype(F32) for g in range(4)]
    qkv_ref[0, :, :768] = jnp.concatenate([r[:24, :192] for r in rows], axis=1)
    qkv_ref[0, :, 768:1536] = jnp.concatenate([r[:24, 256:448] for r in rows], axis=1)
    qkv_ref[0, :, 1536:] = jnp.concatenate(
        [part for r in rows for part in (r[:24, 512:640], r[:24, 448:512])], axis=1
    )
    for g in range(2):
        proj_ref[g, 0] = in_ref[0, rank ^ (2 * pos_ref[1] + g), 48:].astype(F32)[24:36]
    first = [r[37:38] for r in rows]
    second = [r[36:37] for r in rows]
    sum_ref[0] = jnp.concatenate(
        [
            (first[0] + first[1]) + (first[2] + first[3]),
            (second[0] + second[1]) + (second[2] + second[3]),
            jnp.zeros((6, 768), F32),
        ]
        + first
        + second,
        axis=0,
    )


def unpack(pos, totals):
    out_w, fc_w, qkv_w, proj_w, sums = pl.pallas_call(
        unpack_kernel,
        grid_spec=pltpu.PrefetchScalarGridSpec(
            num_scalar_prefetch=1,
            grid=(16,),
            in_specs=[pl.BlockSpec((1, 4, 88, 768), lambda s, pos: (s, 0, 0, 0))],
            out_specs=(
                pl.BlockSpec((4, 1, 48, 768), lambda s, pos: (0, jnp.minimum(s, 7), 0, 0)),
                pl.BlockSpec((1, 48, 3072), lambda s, pos: (jnp.maximum(s - 8, 0), 0, 0)),
                pl.BlockSpec((1, 24, 2304), lambda s, pos: (s, 0, 0)),
                pl.BlockSpec((2, 1, 12, 768), lambda s, pos: (0, s, 0, 0)),
                pl.BlockSpec((1, 16, 768), lambda s, pos: (s, 0, 0)),
            ),
        ),
        out_shape=(
            jax.ShapeDtypeStruct((4, 8, 48, 768), F32),
            jax.ShapeDtypeStruct((8, 48, 3072), F32),
            jax.ShapeDtypeStruct((16, 24, 2304), F32),
            jax.ShapeDtypeStruct((2, 16, 12, 768), F32),
            jax.ShapeDtypeStruct((16, 16, 768), F32),
        ),
        name="unpack_grads",
    )(pos, totals)
    return (
        out_w.reshape(1536, 768),
        fc_w.reshape(384, 3072),
        qkv_w.reshape(384, 2304),
        proj_w.reshape(384, 768),
        sums,
    )


def swap(values, axis):
    return lax.ppermute(values, axis, [(0, 1), (1, 0)])


def to_rank(values, offset):
    return lax.ppermute(values, TP, [(a, a ^ offset) for a in range(4)])


def gather_ranks(values):
    return [values] + [to_rank(values, r) for r in (1, 2, 3)]


def pick(values, index, axis=0):
    return lax.dynamic_index_in_dim(values, index, axis, keepdims=False)


def normalize(values):
    center = jnp.mean(values, axis=-1, keepdims=True)
    centered = values - center
    scale = lax.rsqrt(jnp.mean(centered * centered, axis=-1, keepdims=True) + EPS)
    return (centered * scale, scale)


def norm_back(grad, normed, scale, gain):
    grad_normed = grad * gain
    first = jnp.mean(grad_normed, axis=-1, keepdims=True)
    second = jnp.mean(grad_normed * normed, axis=-1, keepdims=True)
    return scale * (grad_normed - first - normed * second)


def dot(a, b):
    return jnp.dot(a, b, preferred_element_type=F32)


def dot_nt(a, b):
    return jnp.einsum("ab,cb->ac", a, b, preferred_element_type=F32)


def dot_tn(a, b):
    return jnp.einsum("ta,tb->ab", a, b, preferred_element_type=F32)


def both_shards(own, fs):
    peer = swap(own, "fsdp")
    first = jnp.where(fs == 0, own, peer)
    second = jnp.where(fs == 0, peer, own)
    return jnp.stack([first, second])


def fetch_by_core(own):
    core = lax.axis_index("core")
    half = own.shape[0] // 2
    part = swap(lax.dynamic_slice_in_dim(own, half * core, half, 0), "fsdp")
    return (part, swap(part, "core"))


def join_shards(own, fetched, fs):
    core = lax.axis_index("core")
    part, other = fetched
    peer = jnp.concatenate(
        [jnp.where(core == 0, part, other), jnp.where(core == 0, other, part)], axis=0
    )
    first = jnp.where(fs == 0, own, peer)
    second = jnp.where(fs == 0, peer, own)
    return jnp.stack([first, second])


def after(values, *earlier):
    return lax.optimization_barrier((values, *earlier))[0]


def to_block(values, offset):
    return lax.ppermute(values, BLOCKS, [(a, a ^ offset) for a in range(8)])


def reduce_by_permute(local):
    core = lax.axis_index("core")
    block = lax.axis_index(BLOCKS)
    pair = pick(local, core) + swap(pick(local, 1 - core), "core")
    low = pair.astype(BF16)
    moved = [to_block(pick(low, block ^ r), r) for r in range(1, 8)]
    total = pick(pair, block)
    for values in moved:
        total = total + values.astype(F32)
    return total


def body(
    block_in,
    out_grad,
    ln1_gain,
    ln1_bias,
    w_qkv,
    q_bias,
    v_bias,
    w_proj,
    b_proj,
    ln2_gain,
    ln2_bias,
    w_fc,
    b_fc,
    w_out,
    b_out,
):
    rank = lax.axis_index(TP)
    seq = lax.axis_index(SEQ_AXES)
    fs = lax.axis_index("fsdp")
    pos = jnp.stack([seq, rank]).astype(jnp.int32)

    x_low = jnp.concatenate(gather_ranks(block_in[0]), axis=0)

    def head_columns(which):
        w_q = lax.dynamic_slice_in_dim(w_qkv, 192 * which, 192, 1)
        w_k = lax.dynamic_slice_in_dim(w_qkv, 768 + 192 * which, 192, 1)
        w_v = lax.dynamic_slice_in_dim(w_qkv, 1536 + 192 * which, 192, 1)
        return jnp.concatenate(
            [w_q, jnp.zeros((384, 64), BF16), w_k, w_v[:, 128:], w_v[:, :128]], axis=1
        )

    qkv_shard = head_columns(rank ^ 2)
    qkv_peer = lax.ppermute(qkv_shard, ("zl", "fsdp"), [(a, 3 - a) for a in range(4)])
    vectors = (ln1_gain, ln1_bias, q_bias, v_bias, b_proj, ln2_gain, ln2_bias, b_out, b_fc)
    vectors = lax.optimization_barrier((qkv_shard,) + vectors)[1:]
    small = jnp.stack([v.astype(F32) for v in vectors[:8]])
    small = jnp.concatenate([small, vectors[8].astype(F32).reshape(4, 384)], axis=0)
    small = both_shards(small, fs)
    qkv_own = head_columns(rank)
    w_cols = jnp.concatenate(
        [jnp.where(fs == 0, qkv_own, qkv_peer), jnp.where(fs == 0, qkv_peer, qkv_own)], axis=0
    )
    wide_vectors = small[:, :8].transpose(1, 0, 2).reshape(8, 768)
    gain_one, shift_one, query_bias, value_bias = wide_vectors[:4]
    proj_bias, gain_two, shift_two, out_bias = wide_vectors[4:]
    fc_bias = pick(small[:, 8:], rank, 1).reshape(768)
    q_own = lax.dynamic_slice_in_dim(query_bias, 192 * rank, 192, 0)
    v_own = lax.dynamic_slice_in_dim(value_bias, 192 * rank, 192, 0)
    qkv_bias = jnp.concatenate(
        [q_own, jnp.zeros((64 + 192,), F32), v_own[128:], v_own[:128]], axis=0
    )
    fc_shard = jnp.concatenate(
        [
            lax.dynamic_slice_in_dim(w_fc, 384 * rank, 384, 1),
            lax.dynamic_slice_in_dim(w_fc, 1536 + 384 * rank, 384, 1),
        ],
        axis=1,
    )
    out_shard = lax.dynamic_slice_in_dim(w_out, 384 * rank, 384, 0)
    fetched = (fetch_by_core(w_proj), fetch_by_core(fc_shard), fetch_by_core(out_shard))

    x = x_low.astype(F32)
    x_normed, x_scale = normalize(x)
    normed_one = (x_normed * gain_one + shift_one).astype(BF16)
    projected = dot(normed_one, w_cols) + qkv_bias
    q_scaled = (projected[:, :256].astype(BF16) * 0.125).astype(BF16).reshape(4, 128, 256)
    kv_own = projected[:, 256:].astype(BF16).reshape(4, 128, 384)
    kv_all = lax.all_gather(kv_own, SEQ_AXES, axis=0, tiled=False)
    q_all = lax.all_gather(after(q_scaled, kv_all), SEQ_AXES, axis=0, tiled=False)
    normed_one_t = normed_one.T
    cot_ranks = tuple(gather_ranks(out_grad[0]))
    kv_all, fetched, cot_ranks, normed_one_t = lax.optimization_barrier(
        (kv_all, fetched, cot_ranks, normed_one_t)
    )
    attn, lse = forward_attention(pos, q_scaled, kv_all)

    attn_ranks, q_all = lax.optimization_barrier((tuple(gather_ranks(attn)), q_all))
    proj_rows = join_shards(w_proj, fetched[0], fs).reshape(4, 3, 64, 768)
    proj_rows = jnp.concatenate(
        [proj_rows[:, :2], jnp.zeros((4, 1, 64, 768), BF16), proj_rows[:, 2:]], axis=1
    ).reshape(4, 256, 768)
    proj_ranks = jnp.stack([pick(proj_rows, rank ^ r) for r in range(4)])
    fc_cols = join_shards(fc_shard, fetched[1], fs).reshape(768, 768)
    out_rows = join_shards(out_shard, fetched[2], fs).reshape(768, 768)
    cot_low = jnp.concatenate(cot_ranks, axis=0)
    residual = x + proj_bias
    attn_full = jnp.concatenate(
        [
            jnp.concatenate([attn_ranks[r][k ^ r] for k in range(4)], axis=0) for r in range(4)
        ],
        axis=1,
    )
    residual = residual + dot(attn_full, proj_ranks.reshape(1024, 768))

    r_normed, r_scale = normalize(residual)
    normed_two = (r_normed * gain_two + shift_two).astype(BF16)
    hidden = dot(normed_two, fc_cols) + fc_bias
    grad_act = dot_nt(cot_low, out_rows)
    inner = GELU_F * (hidden + GELU_C * hidden * hidden * hidden)
    tanh = jnp.tanh(inner)
    activated = (0.5 * hidden * (1.0 + tanh)).astype(BF16)
    slope = 0.5 * (1.0 + tanh) + 0.5 * hidden * (1.0 - tanh * tanh) * GELU_F * (
        1.0 + 3.0 * GELU_C * hidden * hidden
    )
    grad_hidden = grad_act * slope
    grad_hidden_low = grad_hidden.astype(BF16)
    partial_two = dot_nt(grad_hidden_low, fc_cols).reshape(4, 128, 768)
    moved_two = tuple(to_rank(partial_two[r], r) for r in (1, 2, 3))
    grad_out_w = dot_tn(activated, cot_low).reshape(2, 384, 768)
    grad_fc_w = dot_tn(normed_two, grad_hidden_low).reshape(2, 384, 768)
    moved_two, grad_out_w, grad_fc_w = lax.optimization_barrier(
        (moved_two, grad_out_w, grad_fc_w)
    )
    grad_normed_two = partial_two[0] + moved_two[0] + moved_two[1] + moved_two[2]

    cot_own = out_grad[0].astype(F32)
    grad_residual = (
        norm_back(grad_normed_two, r_normed[:128], r_scale[:128], gain_two) + cot_own
    )
    residual_ranks = tuple(gather_ranks(grad_residual.astype(BF16)))
    local = jnp.pad(
        jnp.concatenate([grad_out_w, grad_fc_w], axis=1)
        .reshape(2, 16, 48, 768)
        .transpose(1, 0, 2, 3)
        .reshape(16, 96, 768),
        ((0, 0), (0, 16), (0, 0)),
    )
    residual_ranks, local = lax.optimization_barrier((residual_ranks, local))
    grad_residual_low = jnp.concatenate(residual_ranks, axis=0)
    do_aug, delta = grad_rows(grad_residual_low, proj_ranks[0], attn, lse)
    do_all = lax.all_gather(after(do_aug, q_all), SEQ_AXES, axis=0, tiled=False)
    grad_q, grad_q_sum = query_grad(pos, q_scaled, do_aug, lse, delta, kv_all)

    (
        activated,
        attn_late,
        grad_q,
        grad_normed_two,
        grad_residual,
        grad_hidden,
        cot_own,
    ) = lax.optimization_barrier(
        (activated, attn, grad_q, grad_normed_two, grad_residual, grad_hidden, cot_own)
    )
    out_partial = dot(activated, out_rows).reshape(4, 128, 768)
    grad_proj_w = dot_tn(attn_late.reshape(512, 256), grad_residual_low)
    grad_proj_w = jnp.concatenate([grad_proj_w[:128], grad_proj_w[192:]], axis=0)
    extra = jnp.stack(
        [
            jnp.sum(grad_normed_two * r_normed[:128], axis=0),
            jnp.sum(grad_normed_two, axis=0),
            jnp.sum(grad_residual, axis=0),
            jnp.sum(cot_own, axis=0),
            jnp.sum(grad_hidden, axis=0),
        ]
        + [jnp.zeros((768,), F32)] * 11
    )
    shared = jnp.concatenate(
        [grad_proj_w.reshape(16, 12, 768), extra[:, None], jnp.zeros((16, 3, 768), F32)], axis=1
    )
    local = lax.dynamic_update_slice(local, shared, (0, 96, 0))
    out_low = out_partial[1:].astype(BF16)
    out_low = (None,) + tuple(out_low)
    local, do_all, out_low = lax.optimization_barrier((local, do_all, out_low))
    early = lax.psum_scatter(local, SEQ_AXES, scatter_dimension=0, tiled=False)
    out_moved = tuple(to_rank(out_low[r], r) for r in (1, 2, 3))

    grad_kv, grad_kv_sum = key_grad(pos, kv_own, q_all, do_all)
    grad_kv, out_moved = lax.optimization_barrier((grad_kv, out_moved))
    late_local, partial_one, partial_low = first_grads(
        normed_one_t, x_normed, grad_q, grad_kv, w_cols, grad_q_sum, grad_kv_sum
    )
    late = reduce_by_permute(late_local)
    low_one, late = lax.optimization_barrier((partial_low, late))
    one_moved = tuple(to_rank(low_one[r - 1], r) for r in (1, 2, 3))

    early, late, one_moved = lax.optimization_barrier((early, late, one_moved))
    late = jnp.concatenate([late, jnp.zeros((56, 128), F32)], axis=1)

    def rows_of(which):
        return jnp.concatenate(
            [
                lax.dynamic_slice_in_dim(early, 48 * which, 48, 0),
                lax.dynamic_slice_in_dim(late, 24 * which, 24, 0),
                early[96:109],
                late[48:51],
            ],
            axis=0,
        )

    totals = rows_of(fs) + swap(rows_of(1 - fs).astype(BF16), "fsdp").astype(F32)
    totals = totals.astype(BF16)
    totals = jnp.stack(gather_ranks(totals))
    totals = lax.all_gather(totals, SEQ_AXES, axis=0, tiled=False)
    output = (
        out_partial[0]
        + out_moved[0].astype(F32)
        + out_moved[1].astype(F32)
        + out_moved[2].astype(F32)
        + out_bias
        + residual[:128]
    ).astype(BF16)
    grad_normed_one = (
        partial_one
        + one_moved[0].astype(F32)
        + one_moved[1].astype(F32)
        + one_moved[2].astype(F32)
    )
    input_grad = (
        norm_back(grad_normed_one, x_normed[:128], x_scale[:128], gain_one) + grad_residual
    )
    totals, input_grad, output = lax.optimization_barrier((totals, input_grad, output))
    g_w_out, g_w_fc, g_w_qkv, g_w_proj, sums = unpack(
        jnp.stack([rank, fs]).astype(jnp.int32), totals
    )

    def own_half(values):
        return lax.dynamic_slice_in_dim(values, 384 * fs, 384, values.ndim - 1)

    mlp_sums = own_half(sums[:4, 1])
    g_b_fc = pick(sums[4, 12:].reshape(4, 2, 384), fs, 1).reshape(1536)
    bias_row = sums[0, 8:12]
    g_q_bias = own_half(bias_row[:, :192].reshape(768))
    g_v_bias = own_half(
        jnp.concatenate([bias_row[:, 512:640], bias_row[:, 448:512]], axis=1).reshape(768)
    )
    ln_one = own_half(sums[1:4, 0, :640].reshape(1920)[:1536].reshape(2, 768))
    return (
        output[None],
        input_grad[None],
        ln_one[0],
        ln_one[1],
        g_w_qkv,
        g_q_bias,
        g_v_bias,
        g_w_proj,
        mlp_sums[2],
        mlp_sums[0],
        mlp_sums[1],
        g_w_fc,
        g_b_fc,
        g_w_out,
        mlp_sums[3],
    )


def solution(mesh):
    split = Mesh(
        mesh.devices.reshape(2, 2, 2, 2, 2, 2, 2),
        ("zl", "xh", "xl", "yh", "yl", "core", "fsdp"),
    )
    tokens = P("fsdp", CTX, None)
    vector = P("fsdp")
    matrix = P("fsdp", None)
    in_specs = (
        tokens,
        tokens,
        vector,
        vector,
        matrix,
        vector,
        vector,
        matrix,
        vector,
        vector,
        vector,
        matrix,
        vector,
        matrix,
        vector,
    )
    out_specs = (
        tokens,
        tokens,
        vector,
        vector,
        matrix,
        vector,
        vector,
        matrix,
        vector,
        vector,
        vector,
        matrix,
        vector,
        matrix,
        vector,
    )
    return jax.shard_map(body, mesh=split, in_specs=in_specs, out_specs=out_specs, check_vma=False)
```

```python
import jax
import jax.numpy as jnp
from jax import lax
from jax.experimental import pallas as pl
from jax.experimental.pallas import tpu as pltpu
from jax.sharding import Mesh, PartitionSpec as P

TP = ("zl", "xh")
SEQ_AXES = ("xl", "yh", "yl", "core")
BLOCKS = ("xl", "yh", "yl")
CTX = TP + SEQ_AXES
EPS = 1e-05
GELU_F = 0.7978845608028654
GELU_C = 0.044715
NEG = -1e30
F32 = jnp.float32
BF16 = jnp.bfloat16
NT = (((1,), (1,)), ((), ()))
VMEM_LIMIT = 56 * 1024 * 1024


def lane_half(shape):
    return lax.broadcasted_iota(jnp.int32, shape, len(shape) - 1) >= 64


def slot_only(values, slot):
    lane = lax.broadcasted_iota(jnp.int32, values.shape, 1)
    keep = jnp.logical_and(lane >= 64 * slot, lane < 64 * slot + 64)
    return jnp.where(keep, values, jnp.zeros_like(values))


def wide(values):
    return jnp.concatenate([values] * 4, axis=1)


def pieces(values):
    high = values.astype(BF16)
    rest = values - high.astype(F32)
    middle = rest.astype(BF16)
    low = (rest - middle.astype(F32)).astype(BF16)
    return (high, middle, low)


def chunk_rows(ref, rank, chunk):
    rows = ref[pl.ds(4 * lax.rem(chunk, 4), 4), rank ^ (chunk // 4)]
    return rows.reshape(512, rows.shape[-1])


def causal(scores, first_query, first_key, keys_in_rows):
    rows = lax.broadcasted_iota(jnp.int32, (128, 512), 0)
    cols = lax.broadcasted_iota(jnp.int32, (128, 512), 1)
    if keys_in_rows:
        allowed = first_key + rows <= first_query + cols
    else:
        allowed = first_key + cols <= first_query + rows
    return jnp.concatenate(
        [jnp.where(allowed, scores[128 * h : 128 * h + 128], NEG) for h in range(3)], axis=0
    )


def value_halves(product):
    return jnp.concatenate([product[:256, 128:], product[256:, :128]], axis=0)


def row_halves(product):
    return jnp.concatenate([product[:256, :128], product[256:, 128:]], axis=0)


def forward_kernel(pos_ref, q_ref, kv_ref, attn_ref, lse_ref, m_ref, l_ref, acc_ref):
    seq = pos_ref[0]
    rank = pos_ref[1]

    def tile(k, carry):
        slot = rank ^ k
        block = k * 16 + seq
        q_rows = q_ref[slot]
        queries = jnp.concatenate([slot_only(q_rows, h) for h in range(3)], axis=0)
        m_ref[...] = jnp.full(m_ref.shape, NEG, F32)
        l_ref[...] = jnp.zeros(l_ref.shape, F32)
        acc_ref[...] = jnp.zeros(acc_ref.shape, F32)

        def step(chunk, masked):
            kv = chunk_rows(kv_ref, rank, chunk)
            scores = lax.dot_general(queries, kv[:, :256], NT, preferred_element_type=F32)
            if masked:
                scores = causal(scores, block * 128, chunk * 512, False)
            before = m_ref[...]
            after = jnp.maximum(before, jnp.max(scores, axis=1, keepdims=True))
            weights = jnp.exp(scores - wide(after))
            factor = jnp.exp(before - after)
            m_ref[...] = after
            partial = (weights[:, :128] + weights[:, 128:256]) + (
                weights[:, 256:384] + weights[:, 384:]
            )
            l_ref[...] = l_ref[...] * factor + partial
            acc_ref[...] = acc_ref[...] * factor + value_halves(
                jnp.dot(weights.astype(BF16), kv[:, 128:], preferred_element_type=F32)
            )

        last = block // 4

        def full(chunk, inner):
            step(chunk, False)
            return inner

        lax.fori_loop(0, last, full, 0)
        step(last, True)
        lane = lax.broadcasted_iota(jnp.int32, (128, 128), 1)
        total = jnp.sum(l_ref[...], axis=1, keepdims=True)
        log_sum = m_ref[...] + jnp.log(total)
        lse_ref[slot] = log_sum
        outs = acc_ref[...] / total
        attn_ref[slot, :, :128] = jnp.where(lane < 64, outs[:128], outs[128:256]).astype(BF16)
        attn_ref[slot, :, 128:] = jnp.where(lane < 64, 0.0, outs[256:]).astype(BF16)
        return carry

    lax.fori_loop(0, 4, tile, 0)


def vmem_spec():
    return pl.BlockSpec(memory_space=pltpu.VMEM)


def forward_attention(pos, q, kv):
    return pl.pallas_call(
        forward_kernel,
        out_shape=(
            jax.ShapeDtypeStruct((4, 128, 256), BF16),
            jax.ShapeDtypeStruct((4, 384, 128), F32),
        ),
        in_specs=[pl.BlockSpec(memory_space=pltpu.SMEM), vmem_spec(), vmem_spec()],
        out_specs=(vmem_spec(), vmem_spec()),
        scratch_shapes=[pltpu.VMEM((384, 128), F32)] * 3,
        compiler_params=pltpu.CompilerParams(vmem_limit_bytes=VMEM_LIMIT),
        cost_estimate=pl.CostEstimate(
            flops=3 * 512 * 4096 * 512, transcendentals=3 * 512 * 4096, bytes_accessed=8 * 2**20
        ),
        name="attention_forward",
    )(pos, q, kv)


def grad_rows_kernel(dr_ref, w_ref, attn_ref, lse_ref, do_ref, delta_ref):
    lane = lax.broadcasted_iota(jnp.int32, (512, 128), 1)
    grads = lax.dot_general(dr_ref[...], w_ref[...], NT, preferred_element_type=F32).astype(BF16)
    attn = attn_ref[...].reshape(512, 256).astype(F32)
    product = grads.astype(F32) * attn
    extra = jnp.zeros((512, 128), BF16)
    for h, run in enumerate((0, 1, 3)):
        delta = jnp.sum(slot_only(product, run), axis=1, keepdims=True)
        delta = jnp.broadcast_to(delta, (512, 128))
        for k in range(4):
            delta_ref[k, 128 * h : 128 * h + 128] = delta[128 * k : 128 * k + 128]
        log_sum = jnp.concatenate([lse_ref[k, 128 * h : 128 * h + 128] for k in range(4)], axis=0)
        for p, (piece, other) in enumerate(zip(pieces(-delta), pieces(-log_sum))):
            extra = jnp.where(lane == 3 * h + p, piece, extra)
            extra = jnp.where(lane == 16 + 3 * h + p, other, extra)
    do_ref[:, :, :128] = grads[:, :128].reshape(4, 128, 128)
    do_ref[:, :, 128:] = jnp.where(lane < 64, extra, grads[:, 128:]).reshape(4, 128, 128)


def grad_rows(dr_low, w_rows, attn, lse):
    return pl.pallas_call(
        grad_rows_kernel,
        out_shape=(
            jax.ShapeDtypeStruct((4, 128, 256), BF16),
            jax.ShapeDtypeStruct((4, 384, 128), F32),
        ),
        in_specs=[vmem_spec()] * 4,
        out_specs=(vmem_spec(), vmem_spec()),
        compiler_params=pltpu.CompilerParams(vmem_limit_bytes=VMEM_LIMIT),
        name="attention_grad_rows",
    )(dr_low, w_rows, attn, lse)


def query_grad_kernel(
    pos_ref, q_ref, do_ref, lse_ref, delta_ref, kv_ref, dq_ref, sum_ref, acc_ref
):
    seq = pos_ref[0]
    rank = pos_ref[1]

    def tile(k, carry):
        slot = rank ^ k
        block = k * 16 + seq
        q_rows = q_ref[slot]
        do_rows = do_ref[slot]
        queries = jnp.concatenate([slot_only(q_rows, h) for h in range(3)], axis=0)
        turned = jnp.concatenate([do_rows[:, 128:], do_rows[:, :128]], axis=1)
        grads = jnp.concatenate([slot_only(turned, run) for run in (2, 3, 1)], axis=0)
        acc_ref[...] = jnp.zeros(acc_ref.shape, F32)

        def step(chunk, masked):
            kv = chunk_rows(kv_ref, rank, chunk)
            scores = lax.dot_general(queries, kv[:, :256], NT, preferred_element_type=F32)
            scores = scores - wide(lse_ref[slot])
            if masked:
                scores = causal(scores, block * 128, chunk * 512, False)
            weights = jnp.exp(scores)
            grad_weights = lax.dot_general(grads, kv[:, 128:], NT, preferred_element_type=F32)
            grad_scores = (weights * (grad_weights - wide(delta_ref[slot]))).astype(BF16)
            acc_ref[...] += row_halves(
                jnp.dot(grad_scores, kv[:, :256], preferred_element_type=F32)
            )

        last = block // 4

        def full(chunk, inner):
            step(chunk, False)
            return inner

        lax.fori_loop(0, last, full, 0)
        step(last, True)
        lane = lax.broadcasted_iota(jnp.int32, (128, 128), 1)
        acc = acc_ref[...] * 0.125
        rows = jnp.concatenate(
            [
                jnp.where(lane < 64, acc[:128], acc[128:256]),
                jnp.where(lane < 64, acc[256:], 0.0),
            ],
            axis=1,
        )
        dq_ref[slot] = rows.astype(BF16)
        return carry + jnp.sum(rows, axis=0, keepdims=True)

    sum_ref[...] = lax.fori_loop(0, 4, tile, jnp.zeros((1, 256), F32))


def query_grad(pos, q, do, lse, delta, kv):
    return pl.pallas_call(
        query_grad_kernel,
        out_shape=(
            jax.ShapeDtypeStruct((4, 128, 256), BF16),
            jax.ShapeDtypeStruct((1, 256), F32),
        ),
        in_specs=[pl.BlockSpec(memory_space=pltpu.SMEM)] + [vmem_spec()] * 5,
        out_specs=(vmem_spec(), vmem_spec()),
        scratch_shapes=[pltpu.VMEM((384, 128), F32)],
        compiler_params=pltpu.CompilerParams(vmem_limit_bytes=VMEM_LIMIT),
        cost_estimate=pl.CostEstimate(
            flops=3 * 512 * 4096 * 768, transcendentals=3 * 512 * 4096, bytes_accessed=8 * 2**20
        ),
        name="attention_query_grad",
    )(pos, q, do, lse, delta, kv)


def key_grad_kernel(
    pos_ref, kv_ref, qg_ref, dog_ref, dkv_ref, sum_ref, dk_ref, dv_ref, join_ref
):
    seq = pos_ref[0]
    rank = pos_ref[1]

    def join(chunk, carry):
        q_rows = chunk_rows(qg_ref, rank, chunk)[:, 128:]
        do_rows = chunk_rows(dog_ref, rank, chunk)[:, 128:]
        join_ref[chunk] = jnp.concatenate([q_rows[:, :64], do_rows[:, :64]], axis=1)
        return carry

    lax.fori_loop(seq // 4, 16, join, 0)

    def tile(k, carry):
        slot = rank ^ k
        block = k * 16 + seq
        rows = kv_ref[slot]
        lane = lax.broadcasted_iota(jnp.int32, (128, 256), 1)
        key_rows = rows[:, :256]
        value_rows = jnp.concatenate([rows[:, 256:], rows[:, 128:256]], axis=1)
        keys = []
        values = []
        for h, run in enumerate((0, 1, 3)):
            key_ones = jnp.logical_and(lane >= 208 + 3 * h, lane < 211 + 3 * h)
            value_ones = jnp.logical_and(lane >= 128 + 3 * h, lane < 131 + 3 * h)
            keys.append(jnp.where(key_ones, 1.0, slot_only(key_rows, h)).astype(BF16))
            values.append(jnp.where(value_ones, 1.0, slot_only(value_rows, run)).astype(BF16))
        keys = jnp.concatenate(keys, axis=0)
        values = jnp.concatenate(values, axis=0)
        dk_ref[...] = jnp.zeros(dk_ref.shape, F32)
        dv_ref[...] = jnp.zeros(dv_ref.shape, F32)

        def step(chunk, masked):
            q_rows = chunk_rows(qg_ref, rank, chunk)[:, :128]
            q_rows = jnp.concatenate([q_rows, join_ref[chunk]], axis=1)
            do_rows = chunk_rows(dog_ref, rank, chunk)
            scores = lax.dot_general(keys, q_rows, NT, preferred_element_type=F32)
            if masked:
                scores = causal(scores, chunk * 512, block * 128, True)
            weights = jnp.exp(scores)
            grad_weights = lax.dot_general(values, do_rows, NT, preferred_element_type=F32)
            grad_scores = (weights * grad_weights).astype(BF16)
            dv_ref[...] += row_halves(
                jnp.dot(weights.astype(BF16), do_rows, preferred_element_type=F32)
            )
            dk_ref[...] += row_halves(jnp.dot(grad_scores, q_rows, preferred_element_type=F32))

        first = block // 4

        def full(chunk, inner):
            step(chunk, False)
            return inner

        step(first, True)
        lax.fori_loop(first + 1, 16, full, 0)
        half = lax.broadcasted_iota(jnp.int32, (128, 128), 1) < 64
        grads = jnp.concatenate(
            [
                jnp.where(half, dk_ref[:128], dk_ref[128:256]),
                jnp.where(half, dk_ref[256:], dv_ref[256:]),
                jnp.where(half, dv_ref[:128], dv_ref[128:256]),
            ],
            axis=1,
        )
        dkv_ref[slot] = grads.astype(BF16)
        return carry + jnp.sum(grads, axis=0, keepdims=True)

    sum_ref[...] = lax.fori_loop(0, 4, tile, jnp.zeros((1, 384), F32))


def key_grad(pos, kv_own, q_all, do_all):
    return pl.pallas_call(
        key_grad_kernel,
        out_shape=(
            jax.ShapeDtypeStruct((4, 128, 384), BF16),
            jax.ShapeDtypeStruct((1, 384), F32),
        ),
        in_specs=[pl.BlockSpec(memory_space=pltpu.SMEM)] + [vmem_spec()] * 3,
        out_specs=(vmem_spec(), vmem_spec()),
        scratch_shapes=[
            pltpu.VMEM((384, 128), F32),
            pltpu.VMEM((384, 128), F32),
            pltpu.VMEM((16, 512, 128), BF16),
        ],
        compiler_params=pltpu.CompilerParams(vmem_limit_bytes=VMEM_LIMIT),
        cost_estimate=pl.CostEstimate(
            flops=3 * 512 * 4096 * 1024, transcendentals=3 * 512 * 4096, bytes_accessed=10 * 2**20
        ),
        name="attention_key_grad",
    )(pos, kv_own, q_all, do_all)


def first_grads_kernel(
    norm_ref, hat_ref, q_ref, kv_ref, w_ref, q_sum_ref, kv_sum_ref, local_ref, own_ref, other_ref
):
    cols = jnp.concatenate([q_ref[...].reshape(512, 256), kv_ref[...].reshape(512, 384)], axis=1)
    for half in range(2):
        grads = jnp.dot(
            norm_ref[384 * half : 384 * half + 384], cols, preferred_element_type=F32
        )
        for block in range(16):
            local_ref[block % 2, block // 2, 24 * half : 24 * half + 24] = grads[
                24 * block : 24 * block + 24
            ]
    gain = jnp.zeros((1, 768), F32)
    shift = jnp.zeros((1, 768), F32)
    for k in range(4):
        rows = slice(128 * k, 128 * k + 128)
        part = lax.dot_general(cols[rows], w_ref[...], NT, preferred_element_type=F32)
        if k == 0:
            own_ref[...] = part
        else:
            other_ref[k - 1] = part.astype(BF16)
        gain = gain + jnp.sum(part * hat_ref[rows], axis=0, keepdims=True)
        shift = shift + jnp.sum(part, axis=0, keepdims=True)
    extra = (
        jnp.concatenate([q_sum_ref[...], kv_sum_ref[...]], axis=1),
        gain[:, :640],
        jnp.concatenate([gain[:, 640:], shift[:, :512]], axis=1),
        jnp.concatenate([shift[:, 512:], jnp.zeros((1, 384), F32)], axis=1),
    )
    top = lax.broadcasted_iota(jnp.int32, (8, 640), 0) == 0
    for block in range(16):
        rows = jnp.zeros((8, 640), F32)
        if block < 4:
            rows = jnp.where(top, extra[block], rows)
        local_ref[block % 2, block // 2, 48:] = rows


def first_grads(norm_t, hat, dq, dkv, w_cols, q_sum, kv_sum):
    return pl.pallas_call(
        first_grads_kernel,
        out_shape=(
            jax.ShapeDtypeStruct((2, 8, 56, 640), F32),
            jax.ShapeDtypeStruct((128, 768), F32),
            jax.ShapeDtypeStruct((3, 128, 768), BF16),
        ),
        in_specs=[vmem_spec()] * 7,
        out_specs=(vmem_spec(), vmem_spec(), vmem_spec()),
        compiler_params=pltpu.CompilerParams(vmem_limit_bytes=VMEM_LIMIT),
        name="first_grads",
    )(norm_t, hat, dq, dkv, w_cols, q_sum, kv_sum)


def unpack_kernel(pos_ref, in_ref, out_w_ref, fc_w_ref, qkv_ref, proj_ref, sum_ref):
    step = pl.program_id(0)
    rank = pos_ref[0]

    @pl.when(step < 8)
    def _():
        for g in range(4):
            out_w_ref[g, 0] = in_ref[0, rank ^ g, :48].astype(F32)

    @pl.when(step >= 8)
    def _():
        for g in range(4):
            rows = in_ref[0, rank ^ g, :48].astype(F32)
            fc_w_ref[0, :, 384 * g : 384 * g + 384] = rows[:, :384]
            fc_w_ref[0, :, 1536 + 384 * g : 1920 + 384 * g] = rows[:, 384:]

    rows = [in_ref[0, rank ^ g, 48:].astype(F32) for g in range(4)]
    qkv_ref[0, :, :768] = jnp.concatenate([r[:24, :192] for r in rows], axis=1)
    qkv_ref[0, :, 768:1536] = jnp.concatenate([r[:24, 256:448] for r in rows], axis=1)
    qkv_ref[0, :, 1536:] = jnp.concatenate(
        [part for r in rows for part in (r[:24, 512:640], r[:24, 448:512])], axis=1
    )
    for g in range(2):
        proj_ref[g, 0] = in_ref[0, rank ^ (2 * pos_ref[1] + g), 48:].astype(F32)[24:36]
    first = [r[37:38] for r in rows]
    second = [r[36:37] for r in rows]
    sum_ref[0] = jnp.concatenate(
        [
            (first[0] + first[1]) + (first[2] + first[3]),
            (second[0] + second[1]) + (second[2] + second[3]),
            jnp.zeros((6, 768), F32),
        ]
        + first
        + second,
        axis=0,
    )


def unpack(pos, totals):
    out_w, fc_w, qkv_w, proj_w, sums = pl.pallas_call(
        unpack_kernel,
        grid_spec=pltpu.PrefetchScalarGridSpec(
            num_scalar_prefetch=1,
            grid=(16,),
            in_specs=[pl.BlockSpec((1, 4, 88, 768), lambda s, pos: (s, 0, 0, 0))],
            out_specs=(
                pl.BlockSpec((4, 1, 48, 768), lambda s, pos: (0, jnp.minimum(s, 7), 0, 0)),
                pl.BlockSpec((1, 48, 3072), lambda s, pos: (jnp.maximum(s - 8, 0), 0, 0)),
                pl.BlockSpec((1, 24, 2304), lambda s, pos: (s, 0, 0)),
                pl.BlockSpec((2, 1, 12, 768), lambda s, pos: (0, s, 0, 0)),
                pl.BlockSpec((1, 16, 768), lambda s, pos: (s, 0, 0)),
            ),
        ),
        out_shape=(
            jax.ShapeDtypeStruct((4, 8, 48, 768), F32),
            jax.ShapeDtypeStruct((8, 48, 3072), F32),
            jax.ShapeDtypeStruct((16, 24, 2304), F32),
            jax.ShapeDtypeStruct((2, 16, 12, 768), F32),
            jax.ShapeDtypeStruct((16, 16, 768), F32),
        ),
        name="unpack_grads",
    )(pos, totals)
    return (
        out_w.reshape(1536, 768),
        fc_w.reshape(384, 3072),
        qkv_w.reshape(384, 2304),
        proj_w.reshape(384, 768),
        sums,
    )


def swap(values, axis):
    return lax.ppermute(values, axis, [(0, 1), (1, 0)])


def to_rank(values, offset):
    return lax.ppermute(values, TP, [(a, a ^ offset) for a in range(4)])


def gather_ranks(values):
    return [values] + [to_rank(values, r) for r in (1, 2, 3)]


def pick(values, index, axis=0):
    return lax.dynamic_index_in_dim(values, index, axis, keepdims=False)


def normalize(values):
    center = jnp.mean(values, axis=-1, keepdims=True)
    centered = values - center
    scale = lax.rsqrt(jnp.mean(centered * centered, axis=-1, keepdims=True) + EPS)
    return (centered * scale, scale)


def norm_back(grad, normed, scale, gain):
    grad_normed = grad * gain
    first = jnp.mean(grad_normed, axis=-1, keepdims=True)
    second = jnp.mean(grad_normed * normed, axis=-1, keepdims=True)
    return scale * (grad_normed - first - normed * second)


def dot(a, b):
    return jnp.dot(a, b, preferred_element_type=F32)


def dot_nt(a, b):
    return jnp.einsum("ab,cb->ac", a, b, preferred_element_type=F32)


def dot_tn(a, b):
    return jnp.einsum("ta,tb->ab", a, b, preferred_element_type=F32)


def both_shards(own, fs):
    peer = swap(own, "fsdp")
    first = jnp.where(fs == 0, own, peer)
    second = jnp.where(fs == 0, peer, own)
    return jnp.stack([first, second])


def fetch_by_core(own):
    core = lax.axis_index("core")
    half = own.shape[0] // 2
    part = swap(lax.dynamic_slice_in_dim(own, half * core, half, 0), "fsdp")
    return (part, swap(part, "core"))


def join_shards(own, fetched, fs):
    core = lax.axis_index("core")
    part, other = fetched
    peer = jnp.concatenate(
        [jnp.where(core == 0, part, other), jnp.where(core == 0, other, part)], axis=0
    )
    first = jnp.where(fs == 0, own, peer)
    second = jnp.where(fs == 0, peer, own)
    return jnp.stack([first, second])


def after(values, *earlier):
    return lax.optimization_barrier((values, *earlier))[0]


def to_block(values, offset):
    return lax.ppermute(values, BLOCKS, [(a, a ^ offset) for a in range(8)])


def reduce_by_permute(local):
    core = lax.axis_index("core")
    block = lax.axis_index(BLOCKS)
    pair = pick(local, core) + swap(pick(local, 1 - core), "core")
    moved = [to_block(pick(pair, block ^ r), r) for r in range(1, 8)]
    total = pick(pair, block)
    for values in moved:
        total = total + values
    return total


def body(
    block_in,
    out_grad,
    ln1_gain,
    ln1_bias,
    w_qkv,
    q_bias,
    v_bias,
    w_proj,
    b_proj,
    ln2_gain,
    ln2_bias,
    w_fc,
    b_fc,
    w_out,
    b_out,
):
    rank = lax.axis_index(TP)
    seq = lax.axis_index(SEQ_AXES)
    fs = lax.axis_index("fsdp")
    pos = jnp.stack([seq, rank]).astype(jnp.int32)

    x_low = jnp.concatenate(gather_ranks(block_in[0]), axis=0)

    def head_columns(which):
        w_q = lax.dynamic_slice_in_dim(w_qkv, 192 * which, 192, 1)
        w_k = lax.dynamic_slice_in_dim(w_qkv, 768 + 192 * which, 192, 1)
        w_v = lax.dynamic_slice_in_dim(w_qkv, 1536 + 192 * which, 192, 1)
        return jnp.concatenate(
            [w_q, jnp.zeros((384, 64), BF16), w_k, w_v[:, 128:], w_v[:, :128]], axis=1
        )

    qkv_shard = head_columns(rank ^ 2)
    qkv_peer = lax.ppermute(qkv_shard, ("zl", "fsdp"), [(a, 3 - a) for a in range(4)])
    vectors = (ln1_gain, ln1_bias, q_bias, v_bias, b_proj, ln2_gain, ln2_bias, b_out, b_fc)
    vectors = lax.optimization_barrier((qkv_shard,) + vectors)[1:]
    small = jnp.stack([v.astype(F32) for v in vectors[:8]])
    small = jnp.concatenate([small, vectors[8].astype(F32).reshape(4, 384)], axis=0)
    small = both_shards(small, fs)
    qkv_own = head_columns(rank)
    w_cols = jnp.concatenate(
        [jnp.where(fs == 0, qkv_own, qkv_peer), jnp.where(fs == 0, qkv_peer, qkv_own)], axis=0
    )
    wide_vectors = small[:, :8].transpose(1, 0, 2).reshape(8, 768)
    gain_one, shift_one, query_bias, value_bias = wide_vectors[:4]
    proj_bias, gain_two, shift_two, out_bias = wide_vectors[4:]
    fc_bias = pick(small[:, 8:], rank, 1).reshape(768)
    q_own = lax.dynamic_slice_in_dim(query_bias, 192 * rank, 192, 0)
    v_own = lax.dynamic_slice_in_dim(value_bias, 192 * rank, 192, 0)
    qkv_bias = jnp.concatenate(
        [q_own, jnp.zeros((64 + 192,), F32), v_own[128:], v_own[:128]], axis=0
    )
    fc_shard = jnp.concatenate(
        [
            lax.dynamic_slice_in_dim(w_fc, 384 * rank, 384, 1),
            lax.dynamic_slice_in_dim(w_fc, 1536 + 384 * rank, 384, 1),
        ],
        axis=1,
    )
    out_shard = lax.dynamic_slice_in_dim(w_out, 384 * rank, 384, 0)
    fetched = (fetch_by_core(w_proj), fetch_by_core(fc_shard), fetch_by_core(out_shard))

    x = x_low.astype(F32)
    x_normed, x_scale = normalize(x)
    normed_one = (x_normed * gain_one + shift_one).astype(BF16)
    projected = dot(normed_one, w_cols) + qkv_bias
    q_scaled = (projected[:, :256].astype(BF16) * 0.125).astype(BF16).reshape(4, 128, 256)
    kv_own = projected[:, 256:].astype(BF16).reshape(4, 128, 384)
    kv_all = lax.all_gather(kv_own, SEQ_AXES, axis=0, tiled=False)
    q_all = lax.all_gather(q_scaled, SEQ_AXES, axis=0, tiled=False)
    normed_one_t = normed_one.T
    cot_ranks = tuple(gather_ranks(out_grad[0]))
    kv_all, fetched, cot_ranks, normed_one_t = lax.optimization_barrier(
        (kv_all, fetched, cot_ranks, normed_one_t)
    )
    attn, lse = forward_attention(pos, q_scaled, kv_all)

    attn_ranks, q_all = lax.optimization_barrier((tuple(gather_ranks(attn)), q_all))
    proj_rows = join_shards(w_proj, fetched[0], fs).reshape(4, 3, 64, 768)
    proj_rows = jnp.concatenate(
        [proj_rows[:, :2], jnp.zeros((4, 1, 64, 768), BF16), proj_rows[:, 2:]], axis=1
    ).reshape(4, 256, 768)
    proj_ranks = jnp.stack([pick(proj_rows, rank ^ r) for r in range(4)])
    fc_cols = join_shards(fc_shard, fetched[1], fs).reshape(768, 768)
    out_rows = join_shards(out_shard, fetched[2], fs).reshape(768, 768)
    cot_low = jnp.concatenate(cot_ranks, axis=0)
    residual = x + proj_bias
    attn_full = jnp.concatenate(
        [
            jnp.concatenate([attn_ranks[r][k ^ r] for k in range(4)], axis=0) for r in range(4)
        ],
        axis=1,
    )
    residual = residual + dot(attn_full, proj_ranks.reshape(1024, 768))

    r_normed, r_scale = normalize(residual)
    normed_two = (r_normed * gain_two + shift_two).astype(BF16)
    hidden = dot(normed_two, fc_cols) + fc_bias
    grad_act = dot_nt(cot_low, out_rows)
    inner = GELU_F * (hidden + GELU_C * hidden * hidden * hidden)
    tanh = jnp.tanh(inner)
    activated = (0.5 * hidden * (1.0 + tanh)).astype(BF16)
    slope = 0.5 * (1.0 + tanh) + 0.5 * hidden * (1.0 - tanh * tanh) * GELU_F * (
        1.0 + 3.0 * GELU_C * hidden * hidden
    )
    grad_hidden = grad_act * slope
    grad_hidden_low = grad_hidden.astype(BF16)
    partial_two = dot_nt(grad_hidden_low, fc_cols).reshape(4, 128, 768)
    moved_two = tuple(to_rank(partial_two[r], r) for r in (1, 2, 3))
    grad_out_w = dot_tn(activated, cot_low).reshape(2, 384, 768)
    grad_fc_w = dot_tn(normed_two, grad_hidden_low).reshape(2, 384, 768)
    moved_two, grad_out_w, grad_fc_w = lax.optimization_barrier(
        (moved_two, grad_out_w, grad_fc_w)
    )
    grad_normed_two = partial_two[0] + moved_two[0] + moved_two[1] + moved_two[2]

    cot_own = out_grad[0].astype(F32)
    grad_residual = (
        norm_back(grad_normed_two, r_normed[:128], r_scale[:128], gain_two) + cot_own
    )
    residual_ranks = tuple(gather_ranks(grad_residual.astype(BF16)))
    local = jnp.pad(
        jnp.concatenate([grad_out_w, grad_fc_w], axis=1)
        .reshape(2, 16, 48, 768)
        .transpose(1, 0, 2, 3)
        .reshape(16, 96, 768),
        ((0, 0), (0, 16), (0, 0)),
    )
    residual_ranks, local = lax.optimization_barrier((residual_ranks, local))
    grad_residual_low = jnp.concatenate(residual_ranks, axis=0)
    do_aug, delta = grad_rows(grad_residual_low, proj_ranks[0], attn, lse)
    do_all = lax.all_gather(after(do_aug, q_all), SEQ_AXES, axis=0, tiled=False)
    grad_q, grad_q_sum = query_grad(pos, q_scaled, do_aug, lse, delta, kv_all)

    (
        activated,
        attn_late,
        grad_q,
        grad_normed_two,
        grad_residual,
        grad_hidden,
        cot_own,
    ) = lax.optimization_barrier(
        (activated, attn, grad_q, grad_normed_two, grad_residual, grad_hidden, cot_own)
    )
    out_partial = dot(activated, out_rows).reshape(4, 128, 768)
    grad_proj_w = dot_tn(attn_late.reshape(512, 256), grad_residual_low)
    grad_proj_w = jnp.concatenate([grad_proj_w[:128], grad_proj_w[192:]], axis=0)
    extra = jnp.stack(
        [
            jnp.sum(grad_normed_two * r_normed[:128], axis=0),
            jnp.sum(grad_normed_two, axis=0),
            jnp.sum(grad_residual, axis=0),
            jnp.sum(cot_own, axis=0),
            jnp.sum(grad_hidden, axis=0),
        ]
        + [jnp.zeros((768,), F32)] * 11
    )
    shared = jnp.concatenate(
        [grad_proj_w.reshape(16, 12, 768), extra[:, None], jnp.zeros((16, 3, 768), F32)], axis=1
    )
    local = lax.dynamic_update_slice(local, shared, (0, 96, 0))
    out_low = out_partial[1:].astype(BF16)
    out_low = (None,) + tuple(out_low)
    local, do_all, out_low = lax.optimization_barrier((local, do_all, out_low))
    early = lax.psum_scatter(local, SEQ_AXES, scatter_dimension=0, tiled=False)
    out_moved = tuple(to_rank(out_low[r], r) for r in (1, 2, 3))

    grad_kv, grad_kv_sum = key_grad(pos, kv_own, q_all, do_all)
    grad_kv, out_moved = lax.optimization_barrier((grad_kv, out_moved))
    late_local, partial_one, partial_low = first_grads(
        normed_one_t, x_normed, grad_q, grad_kv, w_cols, grad_q_sum, grad_kv_sum
    )
    late = reduce_by_permute(late_local)
    low_one, late = lax.optimization_barrier((partial_low, late))
    one_moved = tuple(to_rank(low_one[r - 1], r) for r in (1, 2, 3))

    early, late, one_moved = lax.optimization_barrier((early, late, one_moved))
    late = jnp.concatenate([late, jnp.zeros((56, 128), F32)], axis=1)

    def rows_of(which):
        return jnp.concatenate(
            [
                lax.dynamic_slice_in_dim(early, 48 * which, 48, 0),
                lax.dynamic_slice_in_dim(late, 24 * which, 24, 0),
                early[96:109],
                late[48:51],
            ],
            axis=0,
        )

    totals = (rows_of(fs) + swap(rows_of(1 - fs), "fsdp")).astype(BF16)
    totals = jnp.stack(gather_ranks(totals))
    totals = lax.all_gather(totals, SEQ_AXES, axis=0, tiled=False)
    output = (
        out_partial[0]
        + out_moved[0].astype(F32)
        + out_moved[1].astype(F32)
        + out_moved[2].astype(F32)
        + out_bias
        + residual[:128]
    ).astype(BF16)
    grad_normed_one = (
        partial_one
        + one_moved[0].astype(F32)
        + one_moved[1].astype(F32)
        + one_moved[2].astype(F32)
    )
    input_grad = (
        norm_back(grad_normed_one, x_normed[:128], x_scale[:128], gain_one) + grad_residual
    )
    totals, input_grad, output = lax.optimization_barrier((totals, input_grad, output))
    g_w_out, g_w_fc, g_w_qkv, g_w_proj, sums = unpack(
        jnp.stack([rank, fs]).astype(jnp.int32), totals
    )

    def own_half(values):
        return lax.dynamic_slice_in_dim(values, 384 * fs, 384, values.ndim - 1)

    mlp_sums = own_half(sums[:4, 1])
    g_b_fc = pick(sums[4, 12:].reshape(4, 2, 384), fs, 1).reshape(1536)
    bias_row = sums[0, 8:12]
    g_q_bias = own_half(bias_row[:, :192].reshape(768))
    g_v_bias = own_half(
        jnp.concatenate([bias_row[:, 512:640], bias_row[:, 448:512]], axis=1).reshape(768)
    )
    ln_one = own_half(sums[1:4, 0, :640].reshape(1920)[:1536].reshape(2, 768))
    return (
        output[None],
        input_grad[None],
        ln_one[0],
        ln_one[1],
        g_w_qkv,
        g_q_bias,
        g_v_bias,
        g_w_proj,
        mlp_sums[2],
        mlp_sums[0],
        mlp_sums[1],
        g_w_fc,
        g_b_fc,
        g_w_out,
        mlp_sums[3],
    )


def solution(mesh):
    split = Mesh(
        mesh.devices.reshape(2, 2, 2, 2, 2, 2, 2),
        ("zl", "xh", "xl", "yh", "yl", "core", "fsdp"),
    )
    tokens = P("fsdp", CTX, None)
    vector = P("fsdp")
    matrix = P("fsdp", None)
    in_specs = (
        tokens,
        tokens,
        vector,
        vector,
        matrix,
        vector,
        vector,
        matrix,
        vector,
        vector,
        vector,
        matrix,
        vector,
        matrix,
        vector,
    )
    out_specs = (
        tokens,
        tokens,
        vector,
        vector,
        matrix,
        vector,
        vector,
        matrix,
        vector,
        vector,
        vector,
        matrix,
        vector,
        matrix,
        vector,
    )
    return jax.shard_map(body, mesh=split, in_specs=in_specs, out_specs=out_specs, check_vma=False)
```

```python
import jax
import jax.numpy as jnp
from jax import lax
from jax.experimental import pallas as pl
from jax.experimental.pallas import tpu as pltpu
from jax.sharding import Mesh, PartitionSpec as P

TP = ("zl", "xh")
SEQ_AXES = ("xl", "yh", "yl", "core")
BLOCKS = ("xl", "yh", "yl")
CTX = TP + SEQ_AXES
EPS = 1e-05
GELU_F = 0.7978845608028654
GELU_C = 0.044715
NEG = -1e30
F32 = jnp.float32
BF16 = jnp.bfloat16
NT = (((1,), (1,)), ((), ()))
VMEM_LIMIT = 56 * 1024 * 1024


def lane_half(shape):
    return lax.broadcasted_iota(jnp.int32, shape, len(shape) - 1) >= 64


def slot_only(values, slot):
    lane = lax.broadcasted_iota(jnp.int32, values.shape, 1)
    keep = jnp.logical_and(lane >= 64 * slot, lane < 64 * slot + 64)
    return jnp.where(keep, values, jnp.zeros_like(values))


def wide(values):
    return jnp.concatenate([values] * 4, axis=1)


def pieces(values):
    high = values.astype(BF16)
    rest = values - high.astype(F32)
    middle = rest.astype(BF16)
    low = (rest - middle.astype(F32)).astype(BF16)
    return (high, middle, low)


def chunk_rows(ref, rank, chunk):
    rows = ref[pl.ds(4 * lax.rem(chunk, 4), 4), rank ^ (chunk // 4)]
    return rows.reshape(512, rows.shape[-1])


def causal(scores, first_query, first_key, keys_in_rows):
    rows = lax.broadcasted_iota(jnp.int32, (128, 512), 0)
    cols = lax.broadcasted_iota(jnp.int32, (128, 512), 1)
    if keys_in_rows:
        allowed = first_key + rows <= first_query + cols
    else:
        allowed = first_key + cols <= first_query + rows
    return jnp.concatenate(
        [jnp.where(allowed, scores[128 * h : 128 * h + 128], NEG) for h in range(3)], axis=0
    )


def value_halves(product):
    return jnp.concatenate([product[:256, 128:], product[256:, :128]], axis=0)


def row_halves(product):
    return jnp.concatenate([product[:256, :128], product[256:, 128:]], axis=0)


def forward_kernel(pos_ref, q_ref, kv_ref, attn_ref, lse_ref, m_ref, l_ref, acc_ref):
    seq = pos_ref[0]
    rank = pos_ref[1]

    def tile(k, carry):
        slot = rank ^ k
        block = k * 16 + seq
        q_rows = q_ref[slot]
        queries = jnp.concatenate([slot_only(q_rows, h) for h in range(3)], axis=0)
        m_ref[...] = jnp.full(m_ref.shape, NEG, F32)
        l_ref[...] = jnp.zeros(l_ref.shape, F32)
        acc_ref[...] = jnp.zeros(acc_ref.shape, F32)

        def step(chunk, masked):
            kv = chunk_rows(kv_ref, rank, chunk)
            scores = lax.dot_general(queries, kv[:, :256], NT, preferred_element_type=F32)
            if masked:
                scores = causal(scores, block * 128, chunk * 512, False)
            before = m_ref[...]
            after = jnp.maximum(before, jnp.max(scores, axis=1, keepdims=True))
            weights = jnp.exp(scores - wide(after))
            factor = jnp.exp(before - after)
            m_ref[...] = after
            partial = (weights[:, :128] + weights[:, 128:256]) + (
                weights[:, 256:384] + weights[:, 384:]
            )
            l_ref[...] = l_ref[...] * factor + partial
            acc_ref[...] = acc_ref[...] * factor + value_halves(
                jnp.dot(weights.astype(BF16), kv[:, 128:], preferred_element_type=F32)
            )

        last = block // 4

        def full(chunk, inner):
            step(chunk, False)
            return inner

        lax.fori_loop(0, last, full, 0)
        step(last, True)
        lane = lax.broadcasted_iota(jnp.int32, (128, 128), 1)
        total = jnp.sum(l_ref[...], axis=1, keepdims=True)
        log_sum = m_ref[...] + jnp.log(total)
        lse_ref[slot] = log_sum
        outs = acc_ref[...] / total
        attn_ref[slot, :, :128] = jnp.where(lane < 64, outs[:128], outs[128:256]).astype(BF16)
        attn_ref[slot, :, 128:] = jnp.where(lane < 64, 0.0, outs[256:]).astype(BF16)
        return carry

    lax.fori_loop(0, 4, tile, 0)


def vmem_spec():
    return pl.BlockSpec(memory_space=pltpu.VMEM)


def forward_attention(pos, q, kv):
    return pl.pallas_call(
        forward_kernel,
        out_shape=(
            jax.ShapeDtypeStruct((4, 128, 256), BF16),
            jax.ShapeDtypeStruct((4, 384, 128), F32),
        ),
        in_specs=[pl.BlockSpec(memory_space=pltpu.SMEM), vmem_spec(), vmem_spec()],
        out_specs=(vmem_spec(), vmem_spec()),
        scratch_shapes=[pltpu.VMEM((384, 128), F32)] * 3,
        compiler_params=pltpu.CompilerParams(vmem_limit_bytes=VMEM_LIMIT),
        cost_estimate=pl.CostEstimate(
            flops=3 * 512 * 4096 * 512, transcendentals=3 * 512 * 4096, bytes_accessed=8 * 2**20
        ),
        name="attention_forward",
    )(pos, q, kv)


def grad_rows_kernel(dr_ref, w_ref, attn_ref, lse_ref, do_ref, delta_ref):
    lane = lax.broadcasted_iota(jnp.int32, (512, 128), 1)
    grads = lax.dot_general(dr_ref[...], w_ref[...], NT, preferred_element_type=F32).astype(BF16)
    attn = attn_ref[...].reshape(512, 256).astype(F32)
    product = grads.astype(F32) * attn
    extra = jnp.zeros((512, 128), BF16)
    for h, run in enumerate((0, 1, 3)):
        delta = jnp.sum(slot_only(product, run), axis=1, keepdims=True)
        delta = jnp.broadcast_to(delta, (512, 128))
        for k in range(4):
            delta_ref[k, 128 * h : 128 * h + 128] = delta[128 * k : 128 * k + 128]
        log_sum = jnp.concatenate([lse_ref[k, 128 * h : 128 * h + 128] for k in range(4)], axis=0)
        for p, (piece, other) in enumerate(zip(pieces(-delta), pieces(-log_sum))):
            extra = jnp.where(lane == 3 * h + p, piece, extra)
            extra = jnp.where(lane == 16 + 3 * h + p, other, extra)
    do_ref[:, :, :128] = grads[:, :128].reshape(4, 128, 128)
    do_ref[:, :, 128:] = jnp.where(lane < 64, extra, grads[:, 128:]).reshape(4, 128, 128)


def grad_rows(dr_low, w_rows, attn, lse):
    return pl.pallas_call(
        grad_rows_kernel,
        out_shape=(
            jax.ShapeDtypeStruct((4, 128, 256), BF16),
            jax.ShapeDtypeStruct((4, 384, 128), F32),
        ),
        in_specs=[vmem_spec()] * 4,
        out_specs=(vmem_spec(), vmem_spec()),
        compiler_params=pltpu.CompilerParams(vmem_limit_bytes=VMEM_LIMIT),
        name="attention_grad_rows",
    )(dr_low, w_rows, attn, lse)


def query_grad_kernel(
    pos_ref, q_ref, do_ref, lse_ref, delta_ref, kv_ref, dq_ref, sum_ref, acc_ref
):
    seq = pos_ref[0]
    rank = pos_ref[1]

    def tile(k, carry):
        slot = rank ^ k
        block = k * 16 + seq
        q_rows = q_ref[slot]
        do_rows = do_ref[slot]
        queries = jnp.concatenate([slot_only(q_rows, h) for h in range(3)], axis=0)
        turned = jnp.concatenate([do_rows[:, 128:], do_rows[:, :128]], axis=1)
        grads = jnp.concatenate([slot_only(turned, run) for run in (2, 3, 1)], axis=0)
        acc_ref[...] = jnp.zeros(acc_ref.shape, F32)

        def step(chunk, masked):
            kv = chunk_rows(kv_ref, rank, chunk)
            scores = lax.dot_general(queries, kv[:, :256], NT, preferred_element_type=F32)
            scores = scores - wide(lse_ref[slot])
            if masked:
                scores = causal(scores, block * 128, chunk * 512, False)
            weights = jnp.exp(scores)
            grad_weights = lax.dot_general(grads, kv[:, 128:], NT, preferred_element_type=F32)
            grad_scores = (weights * (grad_weights - wide(delta_ref[slot]))).astype(BF16)
            acc_ref[...] += row_halves(
                jnp.dot(grad_scores, kv[:, :256], preferred_element_type=F32)
            )

        last = block // 4

        def full(chunk, inner):
            step(chunk, False)
            return inner

        lax.fori_loop(0, last, full, 0)
        step(last, True)
        lane = lax.broadcasted_iota(jnp.int32, (128, 128), 1)
        acc = acc_ref[...] * 0.125
        rows = jnp.concatenate(
            [
                jnp.where(lane < 64, acc[:128], acc[128:256]),
                jnp.where(lane < 64, acc[256:], 0.0),
            ],
            axis=1,
        )
        dq_ref[slot] = rows.astype(BF16)
        return carry + jnp.sum(rows, axis=0, keepdims=True)

    sum_ref[...] = lax.fori_loop(0, 4, tile, jnp.zeros((1, 256), F32))


def query_grad(pos, q, do, lse, delta, kv):
    return pl.pallas_call(
        query_grad_kernel,
        out_shape=(
            jax.ShapeDtypeStruct((4, 128, 256), BF16),
            jax.ShapeDtypeStruct((1, 256), F32),
        ),
        in_specs=[pl.BlockSpec(memory_space=pltpu.SMEM)] + [vmem_spec()] * 5,
        out_specs=(vmem_spec(), vmem_spec()),
        scratch_shapes=[pltpu.VMEM((384, 128), F32)],
        compiler_params=pltpu.CompilerParams(vmem_limit_bytes=VMEM_LIMIT),
        cost_estimate=pl.CostEstimate(
            flops=3 * 512 * 4096 * 768, transcendentals=3 * 512 * 4096, bytes_accessed=8 * 2**20
        ),
        name="attention_query_grad",
    )(pos, q, do, lse, delta, kv)


def key_grad_kernel(
    pos_ref, kv_ref, qg_ref, dog_ref, dkv_ref, sum_ref, dk_ref, dv_ref, join_ref
):
    seq = pos_ref[0]
    rank = pos_ref[1]

    def join(chunk, carry):
        q_rows = chunk_rows(qg_ref, rank, chunk)[:, 128:]
        do_rows = chunk_rows(dog_ref, rank, chunk)[:, 128:]
        join_ref[chunk] = jnp.concatenate([q_rows[:, :64], do_rows[:, :64]], axis=1)
        return carry

    lax.fori_loop(seq // 4, 16, join, 0)

    def tile(k, carry):
        slot = rank ^ k
        block = k * 16 + seq
        rows = kv_ref[slot]
        lane = lax.broadcasted_iota(jnp.int32, (128, 256), 1)
        key_rows = rows[:, :256]
        value_rows = jnp.concatenate([rows[:, 256:], rows[:, 128:256]], axis=1)
        keys = []
        values = []
        for h, run in enumerate((0, 1, 3)):
            key_ones = jnp.logical_and(lane >= 208 + 3 * h, lane < 211 + 3 * h)
            value_ones = jnp.logical_and(lane >= 128 + 3 * h, lane < 131 + 3 * h)
            keys.append(jnp.where(key_ones, 1.0, slot_only(key_rows, h)).astype(BF16))
            values.append(jnp.where(value_ones, 1.0, slot_only(value_rows, run)).astype(BF16))
        keys = jnp.concatenate(keys, axis=0)
        values = jnp.concatenate(values, axis=0)
        dk_ref[...] = jnp.zeros(dk_ref.shape, F32)
        dv_ref[...] = jnp.zeros(dv_ref.shape, F32)

        def step(chunk, masked):
            q_rows = chunk_rows(qg_ref, rank, chunk)[:, :128]
            q_rows = jnp.concatenate([q_rows, join_ref[chunk]], axis=1)
            do_rows = chunk_rows(dog_ref, rank, chunk)
            scores = lax.dot_general(keys, q_rows, NT, preferred_element_type=F32)
            if masked:
                scores = causal(scores, chunk * 512, block * 128, True)
            weights = jnp.exp(scores)
            grad_weights = lax.dot_general(values, do_rows, NT, preferred_element_type=F32)
            grad_scores = (weights * grad_weights).astype(BF16)
            dv_ref[...] += row_halves(
                jnp.dot(weights.astype(BF16), do_rows, preferred_element_type=F32)
            )
            dk_ref[...] += row_halves(jnp.dot(grad_scores, q_rows, preferred_element_type=F32))

        first = block // 4

        def full(chunk, inner):
            step(chunk, False)
            return inner

        step(first, True)
        lax.fori_loop(first + 1, 16, full, 0)
        half = lax.broadcasted_iota(jnp.int32, (128, 128), 1) < 64
        grads = jnp.concatenate(
            [
                jnp.where(half, dk_ref[:128], dk_ref[128:256]),
                jnp.where(half, dk_ref[256:], dv_ref[256:]),
                jnp.where(half, dv_ref[:128], dv_ref[128:256]),
            ],
            axis=1,
        )
        dkv_ref[slot] = grads.astype(BF16)
        return carry + jnp.sum(grads, axis=0, keepdims=True)

    sum_ref[...] = lax.fori_loop(0, 4, tile, jnp.zeros((1, 384), F32))


def key_grad(pos, kv_own, q_all, do_all):
    return pl.pallas_call(
        key_grad_kernel,
        out_shape=(
            jax.ShapeDtypeStruct((4, 128, 384), BF16),
            jax.ShapeDtypeStruct((1, 384), F32),
        ),
        in_specs=[pl.BlockSpec(memory_space=pltpu.SMEM)] + [vmem_spec()] * 3,
        out_specs=(vmem_spec(), vmem_spec()),
        scratch_shapes=[
            pltpu.VMEM((384, 128), F32),
            pltpu.VMEM((384, 128), F32),
            pltpu.VMEM((16, 512, 128), BF16),
        ],
        compiler_params=pltpu.CompilerParams(vmem_limit_bytes=VMEM_LIMIT),
        cost_estimate=pl.CostEstimate(
            flops=3 * 512 * 4096 * 1024, transcendentals=3 * 512 * 4096, bytes_accessed=10 * 2**20
        ),
        name="attention_key_grad",
    )(pos, kv_own, q_all, do_all)


def first_grads_kernel(
    norm_ref, hat_ref, q_ref, kv_ref, w_ref, q_sum_ref, kv_sum_ref, local_ref, own_ref, other_ref
):
    cols = jnp.concatenate([q_ref[...].reshape(512, 256), kv_ref[...].reshape(512, 384)], axis=1)
    for half in range(2):
        grads = jnp.dot(
            norm_ref[384 * half : 384 * half + 384], cols, preferred_element_type=F32
        )
        for block in range(16):
            local_ref[block % 2, block // 2, 24 * half : 24 * half + 24] = grads[
                24 * block : 24 * block + 24
            ]
    gain = jnp.zeros((1, 768), F32)
    shift = jnp.zeros((1, 768), F32)
    for k in range(4):
        rows = slice(128 * k, 128 * k + 128)
        part = lax.dot_general(cols[rows], w_ref[...], NT, preferred_element_type=F32)
        if k == 0:
            own_ref[...] = part
        else:
            other_ref[k - 1] = part.astype(BF16)
        gain = gain + jnp.sum(part * hat_ref[rows], axis=0, keepdims=True)
        shift = shift + jnp.sum(part, axis=0, keepdims=True)
    extra = (
        jnp.concatenate([q_sum_ref[...], kv_sum_ref[...]], axis=1),
        gain[:, :640],
        jnp.concatenate([gain[:, 640:], shift[:, :512]], axis=1),
        jnp.concatenate([shift[:, 512:], jnp.zeros((1, 384), F32)], axis=1),
    )
    top = lax.broadcasted_iota(jnp.int32, (8, 640), 0) == 0
    for block in range(16):
        rows = jnp.zeros((8, 640), F32)
        if block < 4:
            rows = jnp.where(top, extra[block], rows)
        local_ref[block % 2, block // 2, 48:] = rows


def first_grads(norm_t, hat, dq, dkv, w_cols, q_sum, kv_sum):
    return pl.pallas_call(
        first_grads_kernel,
        out_shape=(
            jax.ShapeDtypeStruct((2, 8, 56, 640), F32),
            jax.ShapeDtypeStruct((128, 768), F32),
            jax.ShapeDtypeStruct((3, 128, 768), BF16),
        ),
        in_specs=[vmem_spec()] * 7,
        out_specs=(vmem_spec(), vmem_spec(), vmem_spec()),
        compiler_params=pltpu.CompilerParams(vmem_limit_bytes=VMEM_LIMIT),
        name="first_grads",
    )(norm_t, hat, dq, dkv, w_cols, q_sum, kv_sum)


def unpack_kernel(pos_ref, in_ref, out_w_ref, fc_w_ref, qkv_ref, proj_ref, sum_ref):
    step = pl.program_id(0)
    rank = pos_ref[0]

    @pl.when(step < 4)
    def _():
        for t in range(2):
            for g in range(4):
                out_w_ref[g, t] = in_ref[t, rank ^ g, :48].astype(F32)

    @pl.when(step >= 4)
    def _():
        for t in range(2):
            for g in range(4):
                rows = in_ref[t, rank ^ g, :48].astype(F32)
                fc_w_ref[t, :, 384 * g : 384 * g + 384] = rows[:, :384]
                fc_w_ref[t, :, 1536 + 384 * g : 1920 + 384 * g] = rows[:, 384:]

    for t in range(2):
        rows = [in_ref[t, rank ^ g, 48:].astype(F32) for g in range(4)]
        qkv_ref[t, :, :768] = jnp.concatenate([r[:24, :192] for r in rows], axis=1)
        qkv_ref[t, :, 768:1536] = jnp.concatenate([r[:24, 256:448] for r in rows], axis=1)
        qkv_ref[t, :, 1536:] = jnp.concatenate(
            [part for r in rows for part in (r[:24, 512:640], r[:24, 448:512])], axis=1
        )
        first = [r[37:38] for r in rows]
        second = [r[36:37] for r in rows]
        sum_ref[t] = jnp.concatenate(
            [
                (first[0] + first[1]) + (first[2] + first[3]),
                (second[0] + second[1]) + (second[2] + second[3]),
                jnp.zeros((6, 768), F32),
            ]
            + first
            + second,
            axis=0,
        )
    for g in range(2):
        pieces_of = [
            in_ref[t, rank ^ (2 * pos_ref[1] + g), 48:].astype(F32)[24:36] for t in range(2)
        ]
        proj_ref[g, 0] = jnp.concatenate(pieces_of, axis=0)


def unpack(pos, totals):
    out_w, fc_w, qkv_w, proj_w, sums = pl.pallas_call(
        unpack_kernel,
        grid_spec=pltpu.PrefetchScalarGridSpec(
            num_scalar_prefetch=1,
            grid=(8,),
            in_specs=[pl.BlockSpec((2, 4, 88, 768), lambda s, pos: (s, 0, 0, 0))],
            out_specs=(
                pl.BlockSpec((4, 2, 48, 768), lambda s, pos: (0, jnp.minimum(s, 3), 0, 0)),
                pl.BlockSpec((2, 48, 3072), lambda s, pos: (jnp.maximum(s - 4, 0), 0, 0)),
                pl.BlockSpec((2, 24, 2304), lambda s, pos: (s, 0, 0)),
                pl.BlockSpec((2, 1, 24, 768), lambda s, pos: (0, s, 0, 0)),
                pl.BlockSpec((2, 16, 768), lambda s, pos: (s, 0, 0)),
            ),
        ),
        out_shape=(
            jax.ShapeDtypeStruct((4, 8, 48, 768), F32),
            jax.ShapeDtypeStruct((8, 48, 3072), F32),
            jax.ShapeDtypeStruct((16, 24, 2304), F32),
            jax.ShapeDtypeStruct((2, 8, 24, 768), F32),
            jax.ShapeDtypeStruct((16, 16, 768), F32),
        ),
        compiler_params=pltpu.CompilerParams(vmem_limit_bytes=VMEM_LIMIT),
        name="unpack_grads",
    )(pos, totals)
    return (
        out_w.reshape(1536, 768),
        fc_w.reshape(384, 3072),
        qkv_w.reshape(384, 2304),
        proj_w.reshape(384, 768),
        sums,
    )


def swap(values, axis):
    return lax.ppermute(values, axis, [(0, 1), (1, 0)])


def to_rank(values, offset):
    return lax.ppermute(values, TP, [(a, a ^ offset) for a in range(4)])


def gather_ranks(values):
    return [values] + [to_rank(values, r) for r in (1, 2, 3)]


def pick(values, index, axis=0):
    return lax.dynamic_index_in_dim(values, index, axis, keepdims=False)


def normalize(values):
    center = jnp.mean(values, axis=-1, keepdims=True)
    centered = values - center
    scale = lax.rsqrt(jnp.mean(centered * centered, axis=-1, keepdims=True) + EPS)
    return (centered * scale, scale)


def norm_back(grad, normed, scale, gain):
    grad_normed = grad * gain
    first = jnp.mean(grad_normed, axis=-1, keepdims=True)
    second = jnp.mean(grad_normed * normed, axis=-1, keepdims=True)
    return scale * (grad_normed - first - normed * second)


def dot(a, b):
    return jnp.dot(a, b, preferred_element_type=F32)


def dot_nt(a, b):
    return jnp.einsum("ab,cb->ac", a, b, preferred_element_type=F32)


def dot_tn(a, b):
    return jnp.einsum("ta,tb->ab", a, b, preferred_element_type=F32)


def both_shards(own, fs):
    peer = swap(own, "fsdp")
    first = jnp.where(fs == 0, own, peer)
    second = jnp.where(fs == 0, peer, own)
    return jnp.stack([first, second])


def fetch_by_core(own):
    core = lax.axis_index("core")
    half = own.shape[0] // 2
    part = swap(lax.dynamic_slice_in_dim(own, half * core, half, 0), "fsdp")
    return (part, swap(part, "core"))


def join_shards(own, fetched, fs):
    core = lax.axis_index("core")
    part, other = fetched
    peer = jnp.concatenate(
        [jnp.where(core == 0, part, other), jnp.where(core == 0, other, part)], axis=0
    )
    first = jnp.where(fs == 0, own, peer)
    second = jnp.where(fs == 0, peer, own)
    return jnp.stack([first, second])


def after(values, *earlier):
    return lax.optimization_barrier((values, *earlier))[0]


def to_block(values, offset):
    return lax.ppermute(values, BLOCKS, [(a, a ^ offset) for a in range(8)])


def reduce_by_permute(local, beside):
    core = lax.axis_index("core")
    block = lax.axis_index(BLOCKS)
    pair = pick(local, core) + swap(pick(local, 1 - core), "core")
    pair, beside = lax.optimization_barrier((pair, beside))
    moved = [to_block(pick(pair, block ^ r), r) for r in range(1, 8)]
    total = pick(pair, block)
    for values in moved:
        total = total + values
    return (total, beside)


def body(
    block_in,
    out_grad,
    ln1_gain,
    ln1_bias,
    w_qkv,
    q_bias,
    v_bias,
    w_proj,
    b_proj,
    ln2_gain,
    ln2_bias,
    w_fc,
    b_fc,
    w_out,
    b_out,
):
    rank = lax.axis_index(TP)
    seq = lax.axis_index(SEQ_AXES)
    fs = lax.axis_index("fsdp")
    pos = jnp.stack([seq, rank]).astype(jnp.int32)

    x_low = jnp.concatenate(gather_ranks(block_in[0]), axis=0)

    def head_columns(which):
        w_q = lax.dynamic_slice_in_dim(w_qkv, 192 * which, 192, 1)
        w_k = lax.dynamic_slice_in_dim(w_qkv, 768 + 192 * which, 192, 1)
        w_v = lax.dynamic_slice_in_dim(w_qkv, 1536 + 192 * which, 192, 1)
        return jnp.concatenate(
            [w_q, jnp.zeros((384, 64), BF16), w_k, w_v[:, 128:], w_v[:, :128]], axis=1
        )

    qkv_shard = head_columns(rank ^ 2)
    qkv_peer = lax.ppermute(qkv_shard, ("zl", "fsdp"), [(a, 3 - a) for a in range(4)])
    vectors = (ln1_gain, ln1_bias, q_bias, v_bias, b_proj, ln2_gain, ln2_bias, b_out, b_fc)
    vectors = lax.optimization_barrier((qkv_shard,) + vectors)[1:]
    small = jnp.stack([v.astype(F32) for v in vectors[:8]])
    small = jnp.concatenate([small, vectors[8].astype(F32).reshape(4, 384)], axis=0)
    small = both_shards(small, fs)
    qkv_own = head_columns(rank)
    w_cols = jnp.concatenate(
        [jnp.where(fs == 0, qkv_own, qkv_peer), jnp.where(fs == 0, qkv_peer, qkv_own)], axis=0
    )
    wide_vectors = small[:, :8].transpose(1, 0, 2).reshape(8, 768)
    gain_one, shift_one, query_bias, value_bias = wide_vectors[:4]
    proj_bias, gain_two, shift_two, out_bias = wide_vectors[4:]
    fc_bias = pick(small[:, 8:], rank, 1).reshape(768)
    q_own = lax.dynamic_slice_in_dim(query_bias, 192 * rank, 192, 0)
    v_own = lax.dynamic_slice_in_dim(value_bias, 192 * rank, 192, 0)
    qkv_bias = jnp.concatenate(
        [q_own, jnp.zeros((64 + 192,), F32), v_own[128:], v_own[:128]], axis=0
    )
    fc_shard = jnp.concatenate(
        [
            lax.dynamic_slice_in_dim(w_fc, 384 * rank, 384, 1),
            lax.dynamic_slice_in_dim(w_fc, 1536 + 384 * rank, 384, 1),
        ],
        axis=1,
    )
    out_shard = lax.dynamic_slice_in_dim(w_out, 384 * rank, 384, 0)
    fetched = (fetch_by_core(w_proj), fetch_by_core(fc_shard), fetch_by_core(out_shard))

    x = x_low.astype(F32)
    x_normed, x_scale = normalize(x)
    normed_one = (x_normed * gain_one + shift_one).astype(BF16)
    projected = dot(normed_one, w_cols) + qkv_bias
    q_scaled = (projected[:, :256].astype(BF16) * 0.125).astype(BF16).reshape(4, 128, 256)
    kv_own = projected[:, 256:].astype(BF16).reshape(4, 128, 384)
    kv_all = lax.all_gather(kv_own, SEQ_AXES, axis=0, tiled=False)
    q_all = lax.all_gather(q_scaled, SEQ_AXES, axis=0, tiled=False)
    normed_one_t = normed_one.T
    cot_ranks = tuple(gather_ranks(out_grad[0]))
    kv_all, fetched, cot_ranks, normed_one_t = lax.optimization_barrier(
        (kv_all, fetched, cot_ranks, normed_one_t)
    )
    attn, lse = forward_attention(pos, q_scaled, kv_all)

    attn_ranks, q_all = lax.optimization_barrier((tuple(gather_ranks(attn)), q_all))
    proj_rows = join_shards(w_proj, fetched[0], fs).reshape(4, 3, 64, 768)
    proj_rows = jnp.concatenate(
        [proj_rows[:, :2], jnp.zeros((4, 1, 64, 768), BF16), proj_rows[:, 2:]], axis=1
    ).reshape(4, 256, 768)
    proj_ranks = jnp.stack([pick(proj_rows, rank ^ r) for r in range(4)])
    fc_cols = join_shards(fc_shard, fetched[1], fs).reshape(768, 768)
    out_rows = join_shards(out_shard, fetched[2], fs).reshape(768, 768)
    cot_low = jnp.concatenate(cot_ranks, axis=0)
    residual = x + proj_bias
    attn_full = jnp.concatenate(
        [
            jnp.concatenate([attn_ranks[r][k ^ r] for k in range(4)], axis=0) for r in range(4)
        ],
        axis=1,
    )
    residual = residual + dot(attn_full, proj_ranks.reshape(1024, 768))

    r_normed, r_scale = normalize(residual)
    normed_two = (r_normed * gain_two + shift_two).astype(BF16)
    hidden = dot(normed_two, fc_cols) + fc_bias
    grad_act = dot_nt(cot_low, out_rows)
    inner = GELU_F * (hidden + GELU_C * hidden * hidden * hidden)
    tanh = jnp.tanh(inner)
    activated = (0.5 * hidden * (1.0 + tanh)).astype(BF16)
    slope = 0.5 * (1.0 + tanh) + 0.5 * hidden * (1.0 - tanh * tanh) * GELU_F * (
        1.0 + 3.0 * GELU_C * hidden * hidden
    )
    grad_hidden = grad_act * slope
    grad_hidden_low = grad_hidden.astype(BF16)
    partial_two = dot_nt(grad_hidden_low, fc_cols).reshape(4, 128, 768)
    moved_two = tuple(to_rank(partial_two[r], r) for r in (1, 2, 3))
    grad_out_w = dot_tn(activated, cot_low).reshape(2, 384, 768)
    grad_fc_w = dot_tn(normed_two, grad_hidden_low).reshape(2, 384, 768)
    moved_two, grad_out_w, grad_fc_w = lax.optimization_barrier(
        (moved_two, grad_out_w, grad_fc_w)
    )
    grad_normed_two = partial_two[0] + moved_two[0] + moved_two[1] + moved_two[2]

    cot_own = out_grad[0].astype(F32)
    grad_residual = (
        norm_back(grad_normed_two, r_normed[:128], r_scale[:128], gain_two) + cot_own
    )
    residual_ranks = tuple(gather_ranks(grad_residual.astype(BF16)))
    local = jnp.pad(
        jnp.concatenate([grad_out_w, grad_fc_w], axis=1)
        .reshape(2, 16, 48, 768)
        .transpose(1, 0, 2, 3)
        .reshape(16, 96, 768),
        ((0, 0), (0, 16), (0, 0)),
    )
    residual_ranks, local = lax.optimization_barrier((residual_ranks, local))
    grad_residual_low = jnp.concatenate(residual_ranks, axis=0)
    do_aug, delta = grad_rows(grad_residual_low, proj_ranks[0], attn, lse)
    do_all = lax.all_gather(after(do_aug, q_all), SEQ_AXES, axis=0, tiled=False)
    grad_q, grad_q_sum = query_grad(pos, q_scaled, do_aug, lse, delta, kv_all)

    (
        activated,
        attn_late,
        grad_q,
        grad_normed_two,
        grad_residual,
        grad_hidden,
        cot_own,
    ) = lax.optimization_barrier(
        (activated, attn, grad_q, grad_normed_two, grad_residual, grad_hidden, cot_own)
    )
    out_partial = dot(activated, out_rows).reshape(4, 128, 768)
    grad_proj_w = dot_tn(attn_late.reshape(512, 256), grad_residual_low)
    grad_proj_w = jnp.concatenate([grad_proj_w[:128], grad_proj_w[192:]], axis=0)
    extra = jnp.stack(
        [
            jnp.sum(grad_normed_two * r_normed[:128], axis=0),
            jnp.sum(grad_normed_two, axis=0),
            jnp.sum(grad_residual, axis=0),
            jnp.sum(cot_own, axis=0),
            jnp.sum(grad_hidden, axis=0),
        ]
        + [jnp.zeros((768,), F32)] * 11
    )
    shared = jnp.concatenate(
        [grad_proj_w.reshape(16, 12, 768), extra[:, None], jnp.zeros((16, 3, 768), F32)], axis=1
    )
    local = lax.dynamic_update_slice(local, shared, (0, 96, 0))
    out_low = out_partial[1:].astype(BF16)
    out_low = (None,) + tuple(out_low)
    local, do_all, out_low = lax.optimization_barrier((local, do_all, out_low))
    early = lax.psum_scatter(local, SEQ_AXES, scatter_dimension=0, tiled=False)
    out_moved = tuple(to_rank(out_low[r], r) for r in (1, 2, 3))

    grad_kv, grad_kv_sum = key_grad(pos, kv_own, q_all, do_all)
    grad_kv, out_moved = lax.optimization_barrier((grad_kv, out_moved))
    late_local, partial_one, partial_low = first_grads(
        normed_one_t, x_normed, grad_q, grad_kv, w_cols, grad_q_sum, grad_kv_sum
    )
    late, one_moved = reduce_by_permute(
        late_local, tuple(to_rank(partial_low[r - 1], r) for r in (1, 2, 3))
    )

    early, late, one_moved = lax.optimization_barrier((early, late, one_moved))
    late = jnp.concatenate([late, jnp.zeros((56, 128), F32)], axis=1)

    def rows_of(which):
        return jnp.concatenate(
            [
                lax.dynamic_slice_in_dim(early, 48 * which, 48, 0),
                lax.dynamic_slice_in_dim(late, 24 * which, 24, 0),
                early[96:109],
                late[48:51],
            ],
            axis=0,
        )

    totals = (rows_of(fs) + swap(rows_of(1 - fs), "fsdp")).astype(BF16)
    totals = jnp.stack(gather_ranks(totals))
    totals = lax.all_gather(totals, SEQ_AXES, axis=0, tiled=False)
    output = (
        out_partial[0]
        + out_moved[0].astype(F32)
        + out_moved[1].astype(F32)
        + out_moved[2].astype(F32)
        + out_bias
        + residual[:128]
    ).astype(BF16)
    grad_normed_one = (
        partial_one
        + one_moved[0].astype(F32)
        + one_moved[1].astype(F32)
        + one_moved[2].astype(F32)
    )
    input_grad = (
        norm_back(grad_normed_one, x_normed[:128], x_scale[:128], gain_one) + grad_residual
    )
    totals, input_grad, output = lax.optimization_barrier((totals, input_grad, output))
    g_w_out, g_w_fc, g_w_qkv, g_w_proj, sums = unpack(
        jnp.stack([rank, fs]).astype(jnp.int32), totals
    )

    def own_half(values):
        return lax.dynamic_slice_in_dim(values, 384 * fs, 384, values.ndim - 1)

    mlp_sums = own_half(sums[:4, 1])
    g_b_fc = pick(sums[4, 12:].reshape(4, 2, 384), fs, 1).reshape(1536)
    bias_row = sums[0, 8:12]
    g_q_bias = own_half(bias_row[:, :192].reshape(768))
    g_v_bias = own_half(
        jnp.concatenate([bias_row[:, 512:640], bias_row[:, 448:512]], axis=1).reshape(768)
    )
    ln_one = own_half(sums[1:4, 0, :640].reshape(1920)[:1536].reshape(2, 768))
    return (
        output[None],
        input_grad[None],
        ln_one[0],
        ln_one[1],
        g_w_qkv,
        g_q_bias,
        g_v_bias,
        g_w_proj,
        mlp_sums[2],
        mlp_sums[0],
        mlp_sums[1],
        g_w_fc,
        g_b_fc,
        g_w_out,
        mlp_sums[3],
    )


def solution(mesh):
    split = Mesh(
        mesh.devices.reshape(2, 2, 2, 2, 2, 2, 2),
        ("zl", "xh", "xl", "yh", "yl", "core", "fsdp"),
    )
    tokens = P("fsdp", CTX, None)
    vector = P("fsdp")
    matrix = P("fsdp", None)
    in_specs = (
        tokens,
        tokens,
        vector,
        vector,
        matrix,
        vector,
        vector,
        matrix,
        vector,
        vector,
        vector,
        matrix,
        vector,
        matrix,
        vector,
    )
    out_specs = (
        tokens,
        tokens,
        vector,
        vector,
        matrix,
        vector,
        vector,
        matrix,
        vector,
        vector,
        vector,
        matrix,
        vector,
        matrix,
        vector,
    )
    return jax.shard_map(body, mesh=split, in_specs=in_specs, out_specs=out_specs, check_vma=False)
```
